32 devices in a mesh: context: 8 (over y, x, core), tensor: 4 (over z).
Axes of the slice: x: 2, y: 2, z: 4, core: 2. Of those that a mesh axis runs over, the one named last changes fastest.
Arguments:
- block_input: bfloat16 [4, 4096, 2048], P(None, 'context'), may hold values from -6 to 6
- doc_lengths: int32 [4, 8], replicated, may hold values from 0 to 4096, as said below
- norm_gains: bfloat16 [2, 2048], P(None, 'context'), may hold values from 0.099609375 to 1.8984375
- qkv_weight: bfloat16 [3, 2048, 2048], P(None, 'context', 'tensor'), may hold values from -0.125 to 0.125
- out_weight: bfloat16 [2048, 2048], P('tensor', 'context'), may hold values from -1 to 1
- gateup_weight: bfloat16 [2, 2048, 4096], P(None, 'context', 'tensor'), may hold values from -0.125 to 0.125
- down_weight: bfloat16 [4096, 2048], P('tensor', 'context'), may hold values from -0.09375 to 0.09375
- cotangent: bfloat16 [4, 4096, 2048], P(None, 'context'), may hold values from -6 to 6
Outputs:
- block_output: bfloat16 [4, 4096, 2048], P(None, 'context')
- input_grad: float32 [4, 4096, 2048], P(None, 'context')
- gains_grad: float32 [2, 2048], P(None, 'context')
- qkv_grad: float32 [3, 2048, 2048], P(None, 'context', 'tensor')
- out_grad: float32 [2048, 2048], P('tensor', 'context')
- gateup_grad: float32 [2, 2048, 4096], P(None, 'context', 'tensor')
- down_grad: float32 [4096, 2048], P('tensor', 'context')
The draws below stay inside these ranges and needn't reach their ends.
Inputs may be any that keep to these rules, and one draw needn't show every extreme that they name: `doc_lengths`: each row sums to 4096. In each micro-batch, rows m * 2 to m * 2 + 1, one row drawn from the seed is a single document of 4096 tokens followed by zeros; every other row holds 8 documents of one token or more.
All inputs are finite; a program needn't handle non-finite values.
Results may differ from the reference program's by a relative error of at most 0.024.
Values may be sent and summed in bfloat16 or wider, within the bound.
No kernel may reach another device: no remote copies, remote signals or barrier semaphores. Data moves between devices by JAX's collectives and lax.ppermute only.
A program may use at most 576 MiB of HBM per device.

```python
import math
import jax
import jax.numpy as jnp
from jax import lax

D = 2048
HEADS = 32
HEAD_DIM = 64
FF = 4096
WINDOW = 2048
SEQ_LEN = 4096
SB = 2
MB = 2
DOCS = 8
SEQS = 4
N_TENSOR = 4


def draw_doc_lengths(key, part):
    first_key = jax.random.fold_in(key, 11)
    second_key = jax.random.fold_in(key, 12)
    weights = jax.random.randint(first_key, (SEQS, DOCS), 1, 9, dtype=jnp.int32)
    running = jnp.cumsum(weights, axis=1).astype(jnp.int32)
    totals = running[:, -1:]
    bounds = running * SEQ_LEN // totals
    previous = jnp.concatenate([jnp.zeros((SEQS, 1), jnp.int32), bounds[:, :-1]], axis=1)
    ragged = bounds - previous
    chosen = jax.random.randint(second_key, (MB,), 0, SB, dtype=jnp.int32)
    row_ids = jnp.arange(SEQS, dtype=jnp.int32)
    single = row_ids % SB == chosen[row_ids // SB]
    columns = jnp.arange(DOCS, dtype=jnp.int32)
    whole_doc = jnp.where(columns[None, :] == 0, SEQ_LEN, 0).astype(jnp.int32)
    return jnp.where(single[:, None], whole_doc, ragged).astype(jnp.int32)


def block_levels(stream_key, dims, pieces, smallest, largest):
    def one(dim, shards_of):
        draws = jax.random.uniform(jax.random.fold_in(jax.random.fold_in(stream_key, 6), dim), (shards_of,), jnp.float32, smallest / len(pieces), largest / len(pieces))
        return jnp.repeat(jnp.exp(draws), dims[dim] // shards_of).reshape((-1,) + (1,) * (len(dims) - dim - 1))

    factor_of = one(*pieces[0])
    for cut in pieces[1:]:
        factor_of = factor_of * one(*cut)
    return factor_of


def normal_values(rng, extent, scale, limit, shards=(), kind=jnp.bfloat16):
    values = scale * jax.random.normal(rng, extent, jnp.float32)
    if shards:
        values = values * block_levels(rng, extent, shards, -0.22, 0.18)
    return jnp.clip(values, -limit, limit).astype(kind)


def setup_inputs(seed: int = 0) -> dict:
    seeds = jax.random.split(jax.random.key(seed), 9)
    block_input = normal_values(seeds[0], (SEQS, SEQ_LEN, D), 1.0, 6.0, ((1, 8),))
    doc_lengths = draw_doc_lengths(jax.random.fold_in(seeds[8], 71), 0)
    norm_gains = jnp.clip(1.0 + 0.18 * jax.random.normal(seeds[2], (2, D), jnp.float32), 0.099609375, 1.8984375).astype(jnp.bfloat16)
    qkv_weight = normal_values(seeds[3], (3, D, D), D ** -0.5, 0.125, ((1, 8), (2, 4)))
    out_weight = normal_values(seeds[4], (D, D), (D // 64) ** -0.5, 1.0, ((0, 4), (1, 8)))
    gateup_weight = normal_values(seeds[5], (2, D, FF), D ** -0.5, 0.125, ((1, 8), (2, 4)))
    down_weight = normal_values(seeds[6], (FF, D), FF ** -0.5, 0.09375, ((0, 4), (1, 8)))
    cotangent = normal_values(seeds[7], (SEQS, SEQ_LEN, D), 1.0, 6.0, ((1, 8),))
    return {"block_input": block_input, "doc_lengths": doc_lengths, "norm_gains": norm_gains, "qkv_weight": qkv_weight, "out_weight": out_weight, "gateup_weight": gateup_weight, "down_weight": down_weight, "cotangent": cotangent}


epsilon = 1e-05
rope_base = 10000.0
masked_fill = -1e+30
highest = lax.Precision.HIGHEST

@jax.custom_vjp
def low(v):
    return lax.optimization_barrier(v.astype(jnp.bfloat16)).astype(jnp.float32)

@jax.custom_vjp
def low_back(v):
    return v

def low_keep(v):
    return (low(v), None)

def low_pass(kept, grad):
    return (grad,)

def back_keep(v):
    return (v, None)

def back_low(kept, grad):
    return (low(grad),)
low.defvjp(low_keep, low_pass)
low_back.defvjp(back_keep, back_low)

def rope_tables(positions, head_dim):
    half_dim = head_dim // 2
    counter = jnp.arange(half_dim, dtype=jnp.float32)
    frequency = jnp.exp(counter * (-2.0 * math.log(rope_base) / head_dim))
    angles = positions.astype(jnp.float32)[:, None] * frequency[None, :]
    return (jnp.cos(angles)[:, None, :], jnp.sin(angles)[:, None, :])

def rotate(values, cosine, sine):
    half_dim = values.shape[-1] // 2
    front_half = values[..., :half_dim]
    back_half = values[..., half_dim:]
    return jnp.concatenate([front_half * cosine - back_half * sine, back_half * cosine + front_half * sine], axis=-1)

def attention(queries, keys, values, segment):
    block_rows = math.gcd(512, SEQ_LEN)
    score_scale = HEAD_DIM ** (-0.5)
    padded_keys = jnp.concatenate([jnp.zeros((WINDOW, HEADS, HEAD_DIM), keys.dtype), keys], axis=0)
    padded_values = jnp.concatenate([jnp.zeros((WINDOW, HEADS, HEAD_DIM), values.dtype), values], axis=0)
    padded_seg = jnp.concatenate([jnp.full((WINDOW,), -1, jnp.int32), segment], axis=0)

    def one_block(block_index):
        row_begin = (block_index * block_rows).astype(jnp.int32)
        query_rows = lax.dynamic_slice_in_dim(queries, row_begin, block_rows, 0)
        key_rows = lax.dynamic_slice_in_dim(padded_keys, row_begin, WINDOW + block_rows, 0)
        value_rows = lax.dynamic_slice_in_dim(padded_values, row_begin, WINDOW + block_rows, 0)
        key_seg = lax.dynamic_slice_in_dim(padded_seg, row_begin, WINDOW + block_rows, 0)
        query_seg = lax.dynamic_slice_in_dim(segment, row_begin, block_rows, 0)
        query_pos = row_begin + jnp.arange(block_rows, dtype=jnp.int32)
        key_pos = row_begin - WINDOW + jnp.arange(WINDOW + block_rows, dtype=jnp.int32)
        distance = query_pos[:, None] - key_pos[None, :]
        visible = (query_seg[:, None] == key_seg[None, :]) & (distance >= 0) & (distance < WINDOW)
        scores = low_back(jnp.einsum('qhe,khe->hqk', query_rows, key_rows, precision=highest) * score_scale)
        scores = jnp.where(visible[None], scores, masked_fill)
        weights = jax.nn.softmax(scores, axis=-1)
        return jnp.einsum('hqk,khe->qhe', low(weights), value_rows, precision=highest)
    outputs = lax.map(jax.checkpoint(one_block), jnp.arange(SEQ_LEN // block_rows).astype(jnp.int32))
    return outputs.reshape(SEQ_LEN, HEADS * HEAD_DIM)

def forward_seq(rows, gains, qkv_weight, out_weight, gateup_weight, down_weight, segment):
    head_width = D // N_TENSOR
    hidden_width = FF // N_TENSOR
    inv_one = lax.rsqrt(lax.optimization_barrier(jnp.mean(rows * rows, axis=-1, keepdims=True)) + epsilon)
    normed_one = low(rows * inv_one * gains[0])
    copies_one = low_back(jnp.broadcast_to(normed_one, (N_TENSOR, SEQ_LEN, D)))
    projected = low_back(jnp.einsum('tnd,kdte->ktne', copies_one, qkv_weight.reshape(3, D, N_TENSOR, head_width), precision=highest))
    projected = jnp.transpose(projected, (0, 2, 1, 3)).reshape(3, SEQ_LEN, HEADS, HEAD_DIM)
    cosine, sine = rope_tables(jnp.arange(SEQ_LEN, dtype=jnp.int32), HEAD_DIM)
    queries = low(rotate(projected[0], cosine, sine))
    keys = low(rotate(projected[1], cosine, sine))
    values = low(projected[2])
    attended = attention(queries, keys, values, segment)
    attended = low(low_back(attended.reshape(SEQ_LEN, N_TENSOR, head_width)))
    parts = jnp.einsum('ntc,tcd->tnd', attended, out_weight.reshape(N_TENSOR, head_width, D), precision=highest)
    attention_branch = low_back(lax.optimization_barrier(jnp.sum(low(parts), axis=0)))
    hidden = rows + attention_branch
    inv_two = lax.rsqrt(lax.optimization_barrier(jnp.mean(hidden * hidden, axis=-1, keepdims=True)) + epsilon)
    normed_two = low(hidden * inv_two * gains[1])
    copies_two = low_back(jnp.broadcast_to(normed_two, (N_TENSOR, SEQ_LEN, D)))
    gate_up = low_back(jnp.einsum('tnd,kdtf->ktnf', copies_two, gateup_weight.reshape(2, D, N_TENSOR, hidden_width), precision=highest))
    activation = low(jax.nn.silu(gate_up[0]) * gate_up[1])
    down_parts = jnp.einsum('tnf,tfd->tnd', activation, down_weight.reshape(N_TENSOR, hidden_width, D), precision=highest)
    return hidden + lax.optimization_barrier(jnp.sum(low(down_parts), axis=0))

def reference(block_input, doc_lengths, norm_gains, qkv_weight, out_weight, gateup_weight, down_weight, cotangent):
    gains = norm_gains.astype(jnp.float32)
    qkv_full = qkv_weight.astype(jnp.float32)
    out_full = out_weight.astype(jnp.float32)
    gateup_full = gateup_weight.astype(jnp.float32)
    down_full = down_weight.astype(jnp.float32)
    positions = jnp.arange(SEQ_LEN, dtype=jnp.int32)

    def one_sequence(carried, item):
        rows, lengths, incoming = item
        doc_ends = jnp.cumsum(lengths).astype(jnp.int32)
        segment = lax.optimization_barrier(jnp.sum((positions[:, None] >= doc_ends[None, :]).astype(jnp.int32), axis=-1)).astype(jnp.int32)

        def closed(rows_in, gains_in, qkv_in, out_in, gateup_in, down_in):
            return forward_seq(rows_in, gains_in, qkv_in, out_in, gateup_in, down_in, segment)
        result, pullback = jax.vjp(closed, rows, gains, qkv_full, out_full, gateup_full, down_full)
        grads = pullback(incoming)
        carried = tuple((total + piece for total, piece in zip(carried, grads[1:])))
        return (carried, (result.astype(jnp.bfloat16), grads[0]))
    initial = (jnp.zeros((2, D), jnp.float32), jnp.zeros((3, D, D), jnp.float32), jnp.zeros((D, D), jnp.float32), jnp.zeros((2, D, FF), jnp.float32), jnp.zeros((FF, D), jnp.float32))
    totals, outputs = lax.scan(one_sequence, initial, (block_input.astype(jnp.float32), doc_lengths, cotangent.astype(jnp.float32)))
    return (outputs[0], outputs[1], totals[0], totals[1], totals[2], totals[3], totals[4])
```

```python
import functools
import math

import jax
import jax.numpy as jnp
from jax import lax
from jax.experimental import pallas as pl
from jax.experimental.pallas import tpu as pltpu
from jax.sharding import Mesh
from jax.sharding import PartitionSpec as P

HEAD_DIM = 64
WINDOW = 2048
BLOCK = 256

epsilon = 1e-05
rope_base = 10000.0
masked_fill = -1e30

f32 = jnp.float32
bf16 = jnp.bfloat16
VMEM_BYTES = 56 * 1024 * 1024


def dot(a, b, ca, cb):
    return lax.dot_general(a, b, (((ca,), (cb,)), ((), ())), preferred_element_type=f32)


def visible_block(low_row, q0, k0, block):
    key = k0 + lax.broadcasted_iota(jnp.int32, (block, block), 0)
    query = q0 + lax.broadcasted_iota(jnp.int32, (block, block), 1)
    return (key >= low_row) & (key <= query)


def key_loops(lo_ref, full_ref, step, carry):
    qb = pl.program_id(0)
    lo = lo_ref[qb]
    full = jnp.minimum(jnp.maximum(full_ref[qb], lo), qb)
    carry = lax.fori_loop(lo, full, functools.partial(step, True), carry)
    carry = lax.fori_loop(full, qb, functools.partial(step, False), carry)
    return step(True, qb, carry)


def attend_kernel(lo_ref, full_ref, low_ref, q_ref, k_ref, v_ref, o_ref, lse_ref, acc_ref):
    heads = k_ref.shape[0]
    block = q_ref.shape[1]
    q0 = pl.program_id(0) * block
    acc_ref[...] = jnp.zeros_like(acc_ref)

    def step(masked, kb, carry):
        k0 = pl.multiple_of(kb * block, block)
        if masked:
            visible = visible_block(low_ref[...], q0, k0, block)
        out = []
        for h in range(heads):
            top, total = carry[h]
            rows = pl.ds(h * HEAD_DIM, HEAD_DIM)
            scores = dot(k_ref[h, pl.ds(k0, block), :], q_ref[rows, :], 1, 0)
            if masked:
                scores = jnp.where(visible, scores, masked_fill)
            new_top = jnp.maximum(top, jnp.max(scores, axis=0, keepdims=True))
            weights = jnp.exp(scores - new_top)
            fade = jnp.exp(top - new_top)
            total = total * fade + jnp.sum(weights, axis=0, keepdims=True)
            acc_ref[rows, :] = acc_ref[rows, :] * fade + dot(
                v_ref[rows, pl.ds(k0, block)], weights.astype(bf16), 1, 0
            )
            out.append((new_top, total))
        return tuple(out)

    start = tuple(
        (jnp.full((1, block), masked_fill, f32), jnp.zeros((1, block), f32)) for _ in range(heads)
    )
    final = key_loops(lo_ref, full_ref, step, start)
    for h in range(heads):
        top, total = final[h]
        rows = pl.ds(h * HEAD_DIM, HEAD_DIM)
        o_ref[rows, :] = (acc_ref[rows, :] / total).astype(bf16)
        lse_ref[h : h + 1, :] = top + jnp.log(total)


def attend_back_kernel(
    lo_ref,
    full_ref,
    low_ref,
    q_ref,
    g_ref,
    o_ref,
    lse_ref,
    k_ref,
    v_ref,
    kt_ref,
    dq_ref,
    dk_ref,
    dv_ref,
):
    heads = k_ref.shape[0]
    block = q_ref.shape[1]
    q0 = pl.program_id(0) * block

    @pl.when(pl.program_id(0) == 0)
    def _():
        dk_ref[...] = jnp.zeros_like(dk_ref)
        dv_ref[...] = jnp.zeros_like(dv_ref)

    dq_ref[...] = jnp.zeros_like(dq_ref)
    inner = []
    for h in range(heads):
        rows = pl.ds(h * HEAD_DIM, HEAD_DIM)
        inner.append(
            jnp.sum(
                g_ref[rows, :].astype(f32) * o_ref[rows, :].astype(f32), axis=0, keepdims=True
            )
        )

    def step(masked, kb, carry):
        k0 = pl.multiple_of(kb * block, block)
        cols = pl.ds(k0, block)
        if masked:
            visible = visible_block(low_ref[...], q0, k0, block)
        for h in range(heads):
            rows = pl.ds(h * HEAD_DIM, HEAD_DIM)
            scores = dot(k_ref[h, cols, :], q_ref[rows, :], 1, 0)
            if masked:
                scores = jnp.where(visible, scores, masked_fill)
            probs = jnp.exp(scores - lse_ref[h : h + 1, :])
            grad_probs = dot(v_ref[h, cols, :], g_ref[rows, :], 1, 0)
            grad_scores = (probs * (grad_probs - inner[h])).astype(bf16)
            dv_ref[rows, cols] += dot(g_ref[rows, :], probs.astype(bf16), 1, 1)
            dk_ref[rows, cols] += dot(q_ref[rows, :], grad_scores, 1, 1)
            dq_ref[rows, :] += dot(kt_ref[rows, cols], grad_scores, 1, 0)
        return carry

    key_loops(lo_ref, full_ref, step, 0)


def attention_specs(heads, length, block):
    width = heads * HEAD_DIM
    whole_t = pl.BlockSpec((width, length), lambda i, *_: (0, 0))
    whole_h = pl.BlockSpec((heads, length, HEAD_DIM), lambda i, *_: (0, 0, 0))
    tile = pl.BlockSpec((width, block), lambda i, *_: (0, i))
    low = pl.BlockSpec((1, block), lambda i, *_: (0, i))
    stat = pl.BlockSpec((heads, block), lambda i, *_: (0, i))
    return whole_t, whole_h, tile, low, stat


def attend(bounds, q_t, k_h, v_t):
    heads, length, _ = k_h.shape
    width = heads * HEAD_DIM
    block = math.gcd(BLOCK, length)
    whole_t, whole_h, tile, low, stat = attention_specs(heads, length, block)
    pairs = length * WINDOW * heads
    return pl.pallas_call(
        attend_kernel,
        out_shape=(
            jax.ShapeDtypeStruct((width, length), bf16),
            jax.ShapeDtypeStruct((heads, length), f32),
        ),
        grid_spec=pltpu.PrefetchScalarGridSpec(
            num_scalar_prefetch=2,
            grid=(length // block,),
            in_specs=[low, tile, whole_h, whole_t],
            out_specs=[tile, stat],
            scratch_shapes=[pltpu.VMEM((width, block), f32)],
        ),
        compiler_params=pltpu.CompilerParams(vmem_limit_bytes=VMEM_BYTES),
        cost_estimate=pl.CostEstimate(
            flops=pairs * 4 * 256, transcendentals=pairs, bytes_accessed=length * width * 8
        ),
        name="attend",
    )(*bounds, q_t, k_h, v_t)


def attend_back(bounds, q_t, g_t, o_t, lse, k_h, v_h, k_t):
    heads, length, _ = k_h.shape
    width = heads * HEAD_DIM
    block = math.gcd(BLOCK, length)
    whole_t, whole_h, tile, low, stat = attention_specs(heads, length, block)
    pairs = length * WINDOW * heads
    return pl.pallas_call(
        attend_back_kernel,
        out_shape=tuple(jax.ShapeDtypeStruct((width, length), f32) for _ in range(3)),
        grid_spec=pltpu.PrefetchScalarGridSpec(
            num_scalar_prefetch=2,
            grid=(length // block,),
            in_specs=[low, tile, tile, tile, stat, whole_h, whole_h, whole_t],
            out_specs=[tile, whole_t, whole_t],
        ),
        compiler_params=pltpu.CompilerParams(vmem_limit_bytes=VMEM_BYTES),
        cost_estimate=pl.CostEstimate(
            flops=pairs * 10 * 256, transcendentals=pairs, bytes_accessed=length * width * 24
        ),
        name="attend_back",
    )(*bounds, q_t, g_t, o_t, lse, k_h, v_h, k_t)


def attention_bounds(lengths, length):
    docs = lengths.shape[0]
    upto = jnp.arange(docs)[:, None] >= jnp.arange(docs)[None, :]
    ends = jnp.sum(jnp.where(upto, lengths[None, :], 0), axis=1)
    position = jnp.arange(length, dtype=jnp.int32)
    starts = jnp.max(jnp.where(ends[:, None] <= position[None, :], ends[:, None], 0), axis=0)
    low = jnp.maximum(starts, position - (WINDOW - 1)).astype(jnp.int32)
    block = math.gcd(BLOCK, length)
    by_block = low.reshape(length // block, block)
    first = by_block[:, 0] // block
    full = (by_block[:, -1] + block - 1) // block
    return first, full, low.reshape(1, length)


def rope_tables(length):
    half_dim = HEAD_DIM // 2
    counter = jnp.arange(half_dim, dtype=f32)
    frequency = jnp.exp(counter * (-2.0 * math.log(rope_base) / HEAD_DIM))
    angles = frequency[:, None] * jnp.arange(length, dtype=f32)[None, :]
    return jnp.cos(angles)[None], jnp.sin(angles)[None]


def rotate(values, cosine, sine):
    heads = values.shape[0] // HEAD_DIM
    v = values.reshape(heads, 2, HEAD_DIM // 2, values.shape[1])
    a, b = v[:, 0], v[:, 1]
    out = jnp.stack([a * cosine - b * sine, b * cosine + a * sine], axis=1)
    return out.reshape(values.shape)


def norm_inverse(rows):
    return lax.rsqrt(jnp.mean(rows * rows, axis=-1, keepdims=True) + epsilon)


def norm_backward(grad_normed, normal, inverse, gain):
    grad_normal = grad_normed * gain
    inner = jnp.mean(grad_normal * normal, axis=-1, keepdims=True)
    return inverse * (grad_normal - normal * inner), jnp.sum(grad_normed * normal, axis=0)


def shards(
    parts,
    block_input,
    doc_lengths,
    norm_gains,
    qkv_weight,
    out_weight,
    gateup_weight,
    down_weight,
    cotangent,
):
    n_context, seqs, n_extra = parts
    plane = ("context", "extra")
    model = block_input.shape[2]
    local_len = block_input.shape[1]
    length = local_len * n_context
    own_len = local_len // n_extra
    rows = model // n_context
    block_heads = qkv_weight.shape[2] // HEAD_DIM
    heads = seqs * block_heads // n_context
    block_hidden = gateup_weight.shape[2] // n_context
    hidden_width = seqs * block_hidden
    width = heads * HEAD_DIM
    seq = lax.axis_index("seq")
    first_row = lax.axis_index("extra") * own_len

    def exchange(a):
        return lax.all_to_all(a, "context", split_axis=0, concat_axis=0, tiled=True)

    def gather_plane(a):
        return lax.all_gather(a, plane, axis=0, tiled=True)

    def scatter_plane(a):
        return lax.psum_scatter(a.astype(bf16), plane, scatter_dimension=0, tiled=True).astype(f32)

    def own(a):
        return lax.dynamic_slice(a, (seq, first_row, 0), (1, own_len, model))[0]

    def gather_heads(a):
        m = a.shape[1]
        if block_heads % n_context == 0:
            a = exchange(a.reshape(n_context, -1, rows))
            a = lax.all_gather(a, "seq", axis=0, tiled=False)
            a = a.reshape(seqs, n_context, block_heads // n_context, m, rows)
            return a.transpose(0, 2, 3, 1, 4).reshape(heads, m, model)
        a = lax.all_gather(a, "seq", axis=0, tiled=True)
        a = exchange(a.reshape(n_context, -1, rows))
        return a.reshape(n_context, heads, m, rows).transpose(1, 2, 0, 3).reshape(heads, m, model)

    def scatter_heads(a):
        m = a.shape[1]
        a = a.astype(bf16)
        if block_heads % n_context == 0:
            a = a.reshape(seqs, block_heads // n_context, m, n_context, rows)
            a = a.transpose(0, 3, 1, 2, 4).reshape(seqs, n_context, -1, rows)
            a = lax.psum_scatter(a, "seq", scatter_dimension=0, tiled=False)
            return exchange(a).reshape(block_heads, m, rows).astype(f32)
        a = a.reshape(heads, m, n_context, rows).transpose(2, 0, 1, 3)
        a = exchange(a.reshape(n_context, -1, rows)).reshape(seqs * block_heads, m, rows)
        return lax.psum_scatter(a, "seq", scatter_dimension=0, tiled=True).astype(f32)

    def gather_hidden(a):
        a = lax.all_gather(exchange(a), "seq", axis=0, tiled=False)
        return a.transpose(0, 2, 1, 3).reshape(seqs, a.shape[2], model)

    def scatter_hidden(a):
        m = a.shape[1]
        a = a.astype(bf16).reshape(seqs, m, n_context, rows).transpose(0, 2, 1, 3)
        return exchange(lax.psum_scatter(a, "seq", scatter_dimension=0, tiled=False)).astype(f32)

    gains = lax.all_gather(norm_gains, "context", axis=1, tiled=True).astype(f32)
    rows_in = own(block_input).astype(f32)
    incoming = own(cotangent)

    qkv_local = qkv_weight.reshape(3, rows, block_heads, HEAD_DIM).transpose(2, 0, 3, 1)
    qkv_full = gather_heads(qkv_local.reshape(block_heads, 3 * HEAD_DIM, rows))
    qkv_t = qkv_full.reshape(heads, 3, HEAD_DIM, model).transpose(1, 0, 2, 3)
    qkv_t = qkv_t.reshape(3 * width, model)
    inverse_one = norm_inverse(rows_in)
    normal_one = rows_in * inverse_one
    normed_one = gather_plane((normal_one * gains[0]).astype(bf16))
    out_full = gather_heads(out_weight.reshape(block_heads, HEAD_DIM, rows)).reshape(width, model)
    gateup_local = gateup_weight.reshape(2, rows, n_context, block_hidden).transpose(2, 0, 3, 1)
    gateup_full = gather_hidden(gateup_local.reshape(n_context, 2 * block_hidden, rows))
    gateup_t = gateup_full.reshape(seqs, 2, block_hidden, model).transpose(1, 0, 2, 3)
    gateup_t = gateup_t.reshape(2 * hidden_width, model)
    down_full = gather_hidden(down_weight.reshape(n_context, block_hidden, rows))
    down_full = down_full.reshape(hidden_width, model)
    incoming_all = gather_plane(incoming)

    bounds = attention_bounds(lax.dynamic_slice_in_dim(doc_lengths, seq, 1, 0)[0], length)
    cosine, sine = rope_tables(length)
    score_scale = HEAD_DIM ** (-0.5)

    projected = dot(qkv_t, normed_one, 1, 1)
    q_t = rotate(projected[:width], cosine, sine).astype(bf16) * bf16(score_scale)
    k_t = rotate(projected[width : 2 * width], cosine, sine).astype(bf16)
    v_t = projected[2 * width :].astype(bf16)
    k_h = k_t.reshape(heads, HEAD_DIM, length).transpose(0, 2, 1)
    v_h = v_t.reshape(heads, HEAD_DIM, length).transpose(0, 2, 1)
    o_t, lse = attend(bounds, q_t, k_h, v_t)

    attention_branch = scatter_plane(dot(o_t, out_full, 0, 0))
    hidden = rows_in + attention_branch
    inverse_two = norm_inverse(hidden)
    normal_two = hidden * inverse_two
    normed_two = gather_plane((normal_two * gains[1]).astype(bf16))

    grad_activation = dot(incoming_all, down_full, 1, 1)
    gate_up = dot(normed_two, gateup_t, 1, 1)
    gate, up = gate_up[:, :hidden_width], gate_up[:, hidden_width:]
    gate_sigmoid = jax.nn.sigmoid(gate)
    gate_silu = gate * gate_sigmoid
    activation = (gate_silu * up).astype(bf16)
    grad_gate = grad_activation * up * gate_sigmoid * (1.0 + gate * (1.0 - gate_sigmoid))
    grad_up = grad_activation * gate_silu
    grad_gateup = jnp.concatenate([grad_gate, grad_up], axis=1).astype(bf16)
    grad_normed_two = scatter_plane(dot(grad_gateup, gateup_t, 1, 0))
    feedforward_branch = scatter_plane(dot(activation, down_full, 1, 0))
    result = (hidden + feedforward_branch).astype(bf16)

    grad_rows_two, gain_two = norm_backward(grad_normed_two, normal_two, inverse_two, gains[1])
    grad_hidden = incoming.astype(f32) + grad_rows_two
    grad_hidden_all = gather_plane(grad_hidden.astype(bf16))

    down_grad = dot(activation, incoming_all, 0, 0)
    gateup_grad = dot(grad_gateup, normed_two, 0, 0)
    down_grad = scatter_hidden(down_grad.reshape(seqs, block_hidden, model))
    gateup_grad = gateup_grad.reshape(2, seqs, block_hidden, model).transpose(1, 0, 2, 3)
    gateup_grad = scatter_hidden(gateup_grad.reshape(seqs, 2 * block_hidden, model))

    g_t = dot(out_full, grad_hidden_all, 1, 1).astype(bf16)
    out_grad = scatter_heads(dot(o_t, grad_hidden_all, 1, 0).reshape(heads, HEAD_DIM, model))
    dq_t, dk_t, dv_t = attend_back(bounds, q_t, g_t, o_t, lse, k_h, v_h, k_t)
    grad_projected = jnp.concatenate(
        [rotate(dq_t * score_scale, cosine, -sine), rotate(dk_t, cosine, -sine), dv_t], axis=0
    ).astype(bf16)
    grad_normed_one = scatter_plane(dot(grad_projected, qkv_t, 0, 0))
    qkv_grad = dot(grad_projected, normed_one, 1, 0)
    qkv_grad = qkv_grad.reshape(3, heads, HEAD_DIM, model).transpose(1, 0, 2, 3)
    qkv_grad = scatter_heads(qkv_grad.reshape(heads, 3 * HEAD_DIM, model))

    grad_rows_one, gain_one = norm_backward(grad_normed_one, normal_one, inverse_one, gains[0])
    grad_input = (grad_hidden + grad_rows_one).astype(bf16)

    def everywhere(a):
        a = lax.all_gather(a, ("seq", "extra"), axis=0, tiled=True)
        return a.reshape(seqs, local_len, model)

    gains_grad = lax.psum_scatter(
        jnp.stack([gain_one, gain_two]), "context", scatter_dimension=1, tiled=True
    )
    gains_grad = lax.psum(gains_grad, ("seq", "extra"))
    qkv_grad = qkv_grad.reshape(block_heads, 3, HEAD_DIM, rows).transpose(1, 3, 0, 2)
    gateup_grad = gateup_grad.reshape(n_context, 2, block_hidden, rows).transpose(1, 3, 0, 2)
    return (
        everywhere(result),
        everywhere(grad_input).astype(f32),
        gains_grad,
        qkv_grad.reshape(qkv_weight.shape),
        out_grad.reshape(out_weight.shape),
        gateup_grad.reshape(gateup_weight.shape),
        down_grad.reshape(down_weight.shape),
    )


def solution(mesh):
    n_context, n_tensor = mesh.shape["context"], mesh.shape["tensor"]
    tensor = ("seq", "extra")

    def program(block_input, *others):
        seqs = block_input.shape[0]
        n_extra = n_tensor // seqs
        assert n_extra * seqs == n_tensor
        split = Mesh(
            mesh.devices.reshape(n_context, seqs, n_extra), ("context", "seq", "extra")
        )
        in_specs = (
            P(None, "context", None),
            P(),
            P(None, "context"),
            P(None, "context", tensor),
            P(tensor, "context"),
            P(None, "context", tensor),
            P(tensor, "context"),
            P(None, "context", None),
        )
        out_specs = (
            P(None, "context", None),
            P(None, "context", None),
            P(None, "context"),
            P(None, "context", tensor),
            P(tensor, "context"),
            P(None, "context", tensor),
            P(tensor, "context"),
        )
        return jax.shard_map(
            functools.partial(shards, (n_context, seqs, n_extra)),
            mesh=split,
            in_specs=in_specs,
            out_specs=out_specs,
            check_vma=False,
        )(block_input, *others)

    return program
```

```python
import functools
import math

import jax
import jax.numpy as jnp
from jax import lax
from jax.experimental import pallas as pl
from jax.experimental.pallas import tpu as pltpu
from jax.sharding import Mesh
from jax.sharding import PartitionSpec as P

HEAD_DIM = 64
WINDOW = 2048
BLOCK = 512
TAIL_CHUNKS = 2

epsilon = 1e-05
rope_base = 10000.0
masked_fill = -1e30

f32 = jnp.float32
bf16 = jnp.bfloat16
VMEM_BYTES = 56 * 1024 * 1024


def dot(a, b, ca, cb):
    return lax.dot_general(a, b, (((ca,), (cb,)), ((), ())), preferred_element_type=f32)


def visible_block(low_row, q0, k0, q_block, k_block):
    key = k0 + lax.broadcasted_iota(jnp.int32, (k_block, q_block), 0)
    query = q0 + lax.broadcasted_iota(jnp.int32, (k_block, q_block), 1)
    return (key >= low_row) & (key <= query)


def key_loops(lo_ref, full_ref, q_block, k_block, step, carry):
    qb = pl.program_id(0)
    lo = lo_ref[qb]
    diagonal = qb * q_block // k_block
    full = jnp.minimum(jnp.maximum(full_ref[qb], lo), diagonal)
    carry = lax.fori_loop(lo, full, functools.partial(step, True), carry)
    carry = lax.fori_loop(full, diagonal, functools.partial(step, False), carry)
    for extra in range(max(1, q_block // k_block)):
        carry = step(True, diagonal + extra, carry)
    return carry


def attend_kernel(k_block, lo_ref, full_ref, low_ref, q_ref, k_ref, v_ref, o_ref, lse_ref, acc_ref):
    heads = range(k_ref.shape[0])
    q_block = q_ref.shape[1]
    q0 = pl.program_id(0) * q_block
    rows = [pl.ds(h * HEAD_DIM, HEAD_DIM) for h in heads]
    acc_ref[...] = jnp.zeros_like(acc_ref)

    def step(masked, kb, carry):
        k0 = pl.multiple_of(kb * k_block, k_block)
        cols = pl.ds(k0, k_block)
        scores = [dot(k_ref[h, cols, :], q_ref[rows[h], :], 1, 0) for h in heads]
        if masked:
            visible = visible_block(low_ref[...], q0, k0, q_block, k_block)
            scores = [jnp.where(visible, v, masked_fill) for v in scores]
        top = [jnp.maximum(carry[h][0], jnp.max(scores[h], axis=0, keepdims=True)) for h in heads]
        weights = [jnp.exp(scores[h] - top[h]) for h in heads]
        added = [dot(v_ref[rows[h], cols], weights[h].astype(bf16), 1, 0) for h in heads]
        out = []
        for h in heads:
            fade = jnp.exp(carry[h][0] - top[h])
            total = carry[h][1] * fade + jnp.sum(weights[h], axis=0, keepdims=True)
            acc_ref[rows[h], :] = acc_ref[rows[h], :] * fade + added[h]
            out.append((top[h], total))
        return tuple(out)

    start = tuple(
        (jnp.full((1, q_block), masked_fill, f32), jnp.zeros((1, q_block), f32)) for _ in heads
    )
    final = key_loops(lo_ref, full_ref, q_block, k_block, step, start)
    for h in heads:
        top, total = final[h]
        o_ref[rows[h], :] = (acc_ref[rows[h], :] / total).astype(bf16)
        lse_ref[h : h + 1, :] = top + jnp.log(total)


def attend_back_kernel(
    k_block,
    lo_ref,
    full_ref,
    low_ref,
    q_ref,
    g_ref,
    o_ref,
    lse_ref,
    k_ref,
    v_ref,
    kt_ref,
    dq_ref,
    dk_ref,
    dv_ref,
):
    heads = range(k_ref.shape[0])
    q_block = q_ref.shape[1]
    q0 = pl.program_id(0) * q_block
    rows = [pl.ds(h * HEAD_DIM, HEAD_DIM) for h in heads]

    @pl.when(pl.program_id(0) == 0)
    def _():
        dk_ref[...] = jnp.zeros_like(dk_ref)
        dv_ref[...] = jnp.zeros_like(dv_ref)

    dq_ref[...] = jnp.zeros_like(dq_ref)
    inner = [
        jnp.sum(g_ref[r, :].astype(f32) * o_ref[r, :].astype(f32), axis=0, keepdims=True)
        for r in rows
    ]

    def step(masked, kb, carry):
        k0 = pl.multiple_of(kb * k_block, k_block)
        cols = pl.ds(k0, k_block)
        if masked:
            visible = visible_block(low_ref[...], q0, k0, q_block, k_block)
        for h in heads:
            r = rows[h]
            scores = dot(k_ref[h, cols, :], q_ref[r, :], 1, 0)
            grad_probs = dot(v_ref[h, cols, :], g_ref[r, :], 1, 0)
            if masked:
                scores = jnp.where(visible, scores, masked_fill)
            probs = jnp.exp(scores - lse_ref[h : h + 1, :])
            grad_scores = (probs * (grad_probs - inner[h])).astype(bf16)
            dv = dot(g_ref[r, :], probs.astype(bf16), 1, 1)
            dk = dot(q_ref[r, :], grad_scores, 1, 1)
            dq = dot(kt_ref[r, cols], grad_scores, 1, 0)
            dv_ref[r, cols] += dv
            dk_ref[r, cols] += dk
            dq_ref[r, :] += dq
        return carry

    key_loops(lo_ref, full_ref, q_block, k_block, step, 0)


def attention_specs(heads, length, q_block):
    width = heads * HEAD_DIM
    once = pl.Buffered(1)
    whole_t = pl.BlockSpec((width, length), lambda i, *_: (0, 0), pipeline_mode=once)
    whole_h = pl.BlockSpec((heads, length, HEAD_DIM), lambda i, *_: (0, 0, 0), pipeline_mode=once)
    tile = pl.BlockSpec((width, q_block), lambda i, *_: (0, i))
    low = pl.BlockSpec((1, q_block), lambda i, *_: (0, i))
    stat = pl.BlockSpec((heads, q_block), lambda i, *_: (0, i))
    return whole_t, whole_h, tile, low, stat


def attend(bounds, q_t, k_h, v_t):
    heads, length, _ = k_h.shape
    width = heads * HEAD_DIM
    block = math.gcd(BLOCK, length)
    whole_t, whole_h, tile, low, stat = attention_specs(heads, length, block)
    pairs = length * WINDOW * heads
    return pl.pallas_call(
        functools.partial(attend_kernel, block),
        out_shape=(
            jax.ShapeDtypeStruct((width, length), bf16),
            jax.ShapeDtypeStruct((heads, length), f32),
        ),
        grid_spec=pltpu.PrefetchScalarGridSpec(
            num_scalar_prefetch=2,
            grid=(length // block,),
            in_specs=[low, tile, whole_h, whole_t],
            out_specs=[tile, stat],
            scratch_shapes=[pltpu.VMEM((width, block), f32)],
        ),
        compiler_params=pltpu.CompilerParams(vmem_limit_bytes=VMEM_BYTES),
        cost_estimate=pl.CostEstimate(
            flops=pairs * 6 * 256, transcendentals=pairs, bytes_accessed=length * width * 8
        ),
        name="attend",
    )(*bounds, q_t, k_h, v_t)


def attend_back(bounds, q_t, g_t, o_t, lse, k_h, v_h, k_t):
    heads, length, _ = k_h.shape
    width = heads * HEAD_DIM
    block = math.gcd(BLOCK, length)
    whole_t, whole_h, tile, low, stat = attention_specs(heads, length, block)
    pairs = length * WINDOW * heads
    return pl.pallas_call(
        functools.partial(attend_back_kernel, block),
        out_shape=tuple(jax.ShapeDtypeStruct((width, length), f32) for _ in range(3)),
        grid_spec=pltpu.PrefetchScalarGridSpec(
            num_scalar_prefetch=2,
            grid=(length // block,),
            in_specs=[low, tile, tile, tile, stat, whole_h, whole_h, whole_t],
            out_specs=[tile, whole_t, whole_t],
        ),
        compiler_params=pltpu.CompilerParams(vmem_limit_bytes=VMEM_BYTES),
        cost_estimate=pl.CostEstimate(
            flops=pairs * 12 * 256, transcendentals=pairs, bytes_accessed=length * width * 24
        ),
        name="attend_back",
    )(*bounds, q_t, g_t, o_t, lse, k_h, v_h, k_t)


def attention_bounds(lengths, length):
    docs = lengths.shape[0]
    upto = jnp.arange(docs)[:, None] >= jnp.arange(docs)[None, :]
    ends = jnp.sum(jnp.where(upto, lengths[None, :], 0), axis=1)
    position = jnp.arange(length, dtype=jnp.int32)
    starts = jnp.max(jnp.where(ends[:, None] <= position[None, :], ends[:, None], 0), axis=0)
    low = jnp.maximum(starts, position - (WINDOW - 1)).astype(jnp.int32)
    block = math.gcd(BLOCK, length)
    by_block = low.reshape(length // block, block)
    first = by_block[:, 0] // block
    full = (by_block[:, -1] + block - 1) // block
    return first, full, low.reshape(1, length)


def rope_tables(length):
    half_dim = HEAD_DIM // 2
    counter = jnp.arange(half_dim, dtype=f32)
    frequency = jnp.exp(counter * (-2.0 * math.log(rope_base) / HEAD_DIM))
    angles = frequency[:, None] * jnp.arange(length, dtype=f32)[None, :]
    return jnp.cos(angles)[None], jnp.sin(angles)[None]


def rotate(values, cosine, sine):
    heads = values.shape[0] // HEAD_DIM
    v = values.reshape(heads, 2, HEAD_DIM // 2, values.shape[1])
    a, b = v[:, 0], v[:, 1]
    out = jnp.stack([a * cosine - b * sine, b * cosine + a * sine], axis=1)
    return out.reshape(values.shape)


def norm_inverse(rows):
    return lax.rsqrt(jnp.mean(rows * rows, axis=-1, keepdims=True) + epsilon)


def norm_backward(grad_normed, normal, inverse, gain):
    grad_normal = grad_normed * gain
    inner = jnp.mean(grad_normal * normal, axis=-1, keepdims=True)
    return inverse * (grad_normal - normal * inner), jnp.sum(grad_normed * normal, axis=0)


def swap(a, axis):
    return lax.ppermute(a, axis, [(0, 1), (1, 0)])


def halve(a, axis, dim):
    index = lax.axis_index(axis)
    mine = lax.dynamic_index_in_dim(a, index, dim, False)
    other = lax.dynamic_index_in_dim(a, 1 - index, dim, False)
    return mine.astype(f32) + swap(other, axis).astype(f32)


def after(a, *others):
    return lax.optimization_barrier((a, *others))[0]


def shards(
    parts,
    block_input,
    doc_lengths,
    norm_gains,
    qkv_weight,
    out_weight,
    gateup_weight,
    down_weight,
    cotangent,
):
    n_chips, n_pair, n_core, seqs, n_extra = parts
    n_context = n_chips * n_pair * n_core
    context = ("chips", "pair", "core")
    plane = (*context, "extra")
    everyone = (*plane, "seq")
    cube = n_chips == n_pair == n_core == 2 and n_extra == 1
    model = block_input.shape[2]
    local_len = block_input.shape[1]
    length = local_len * n_context
    own_len = local_len // n_extra
    rows = model // n_context
    block_heads = qkv_weight.shape[2] // HEAD_DIM
    heads = seqs * block_heads // n_context
    split_heads = block_heads % n_context == 0
    block_hidden = gateup_weight.shape[2] // n_context
    hidden_width = seqs * block_hidden
    width = heads * HEAD_DIM
    seq = lax.axis_index("seq")
    first_row = lax.axis_index("extra") * own_len

    def exchange(a):
        return lax.all_to_all(a, context, split_axis=0, concat_axis=0, tiled=True)

    def send(a, *pairs):
        return lax.ppermute(a, "seq", pairs)

    def up(a, first=0):
        return send(a, *((i, i + 1) for i in range(first, seqs - 1)))

    def down(a, last=None):
        return send(a, *((i, i - 1) for i in range(1, seqs if last is None else last)))

    def spread_near(a):
        return [up(a), down(a)]

    def spread_far(near):
        across = jnp.where(seq == 1, near[0], near[1])
        return [up(near[0], 1), down(near[1], seqs - 1), send(across, (1, 3), (2, 0))]

    def spread_blocks(a, near, far):
        return [
            a,
            jnp.where(seq == 0, far[2], near[0]),
            jnp.where(seq >= 2, far[0], far[1]),
            jnp.where(seq == seqs - 1, far[2], near[1]),
        ]

    def spread_line(a, near, far):
        line = jnp.stack([far[2], far[0], near[0], a, near[1], far[1], far[2]])
        return lax.dynamic_slice_in_dim(line, seqs - 1 - seq, seqs, 0)

    def collect_far(blocks):
        across = jnp.where(seq == 0, blocks[1], blocks[3])
        return [
            send(blocks[2], *((i, i + 1) for i in range(seqs - 2))),
            send(blocks[2], *((i, i - 1) for i in range(2, seqs))),
            send(across, (0, 2), (3, 1)),
        ]

    def collect_near(blocks, far):
        above = blocks[3].astype(f32) + far[0].astype(f32) + jnp.where(seq == 2, far[2], 0)
        below = blocks[1].astype(f32) + far[1].astype(f32) + jnp.where(seq == 1, far[2], 0)
        return [blocks[0], up(above.astype(bf16)), down(below.astype(bf16))]

    def total(blocks):
        return sum((b.astype(f32) for b in blocks[1:]), blocks[0].astype(f32))

    def gather_plane(a):
        return lax.all_gather(a, plane, axis=0, tiled=True)

    def scatter_plane(a):
        return lax.psum_scatter(a.astype(bf16), plane, scatter_dimension=0, tiled=True).astype(f32)

    def scatter_start(part):
        part = part.astype(bf16)
        if not cube:
            return [scatter_plane(part)]
        size = part.shape[0] // n_context
        a = halve(part.reshape(n_chips, n_pair, n_core, size, model), "core", 2).astype(bf16)
        one, two = a[:, :, : size // 2], a[:, :, size // 2 :]
        return [halve(one, "pair", 1).astype(bf16), halve(two, "chips", 0).astype(bf16)]

    def scatter_end(halves):
        if not cube:
            return halves[0]
        return jnp.concatenate([halve(halves[0], "chips", 0), halve(halves[1], "pair", 0)], axis=0)

    def scatter_rows(part):
        return scatter_end(scatter_start(part))

    def own(a):
        return lax.dynamic_slice(a, (seq, first_row, 0), (1, own_len, model))[0]

    def heads_out(a):
        if split_heads:
            return exchange(a.reshape(n_context, -1, rows))
        m = a.shape[1]
        a = lax.all_gather(a, "seq", axis=0, tiled=True)
        return exchange(a.reshape(n_context, heads * m, rows))

    def heads_spread(a):
        near = spread_near(a)
        return spread_blocks(a, near, spread_far(near))

    def heads_whole(blocks, m):
        a = jnp.stack(blocks).reshape(len(blocks), n_context, heads // len(blocks), m, rows)
        return a.transpose(0, 2, 3, 1, 4).reshape(heads, m, model)

    def heads_split(a):
        a = a.astype(bf16).reshape(seqs, heads // seqs, a.shape[1], n_context, rows)
        return list(a.transpose(0, 3, 1, 2, 4).reshape(seqs, n_context, -1, rows))

    def heads_back(a):
        m = a.shape[1]
        if split_heads:
            blocks = heads_split(a)
            blocks = collect_near(blocks, collect_far(blocks))
            return exchange(total(blocks).astype(bf16)).reshape(block_heads, m, rows).astype(f32)
        a = a.astype(bf16).reshape(heads, m, n_context, rows).transpose(2, 0, 1, 3)
        a = exchange(a.reshape(n_context, -1, rows)).reshape(seqs * block_heads, m, rows)
        return lax.psum_scatter(a, "seq", scatter_dimension=0, tiled=True).astype(f32)

    gains = lax.all_gather(norm_gains, context, axis=1, tiled=True).astype(f32)
    rows_in = own(block_input).astype(f32)
    incoming = own(cotangent)
    inverse_one = norm_inverse(rows_in)
    normal_one = rows_in * inverse_one
    normed_one = gather_plane((normal_one * gains[0]).astype(bf16))

    qkv_local = qkv_weight.reshape(3, rows, block_heads, HEAD_DIM).transpose(2, 0, 3, 1)
    qkv_block = heads_out(qkv_local.reshape(block_heads, 3 * HEAD_DIM, rows))
    qkv_block, out_local, gateup_local, down_local = lax.optimization_barrier(
        (qkv_block, out_weight, gateup_weight, down_weight)
    )
    qkv_blocks = heads_spread(qkv_block) if split_heads else [qkv_block]
    qkv_t = heads_whole(qkv_blocks, 3 * HEAD_DIM).reshape(heads, 3, HEAD_DIM, model)
    qkv_t = qkv_t.transpose(1, 0, 2, 3).reshape(3 * width, model)
    out_block = heads_out(out_local.reshape(block_heads, HEAD_DIM, rows))
    gateup_local = gateup_local.reshape(2, rows, n_context, block_hidden).transpose(2, 0, 3, 1)
    hidden_block = exchange(
        jnp.concatenate(
            [
                gateup_local.reshape(n_context, 2 * block_hidden, rows),
                down_local.reshape(n_context, block_hidden, rows),
            ],
            axis=1,
        )
    )
    cosine, sine = rope_tables(length)
    bounds = attention_bounds(lax.dynamic_slice_in_dim(doc_lengths, seq, 1, 0)[0], length)
    normed_one, incoming_now, qkv_t, out_block, hidden_block, cosine, sine, bounds = (
        lax.optimization_barrier(
            (normed_one, incoming, qkv_t, out_block, hidden_block, cosine, sine, bounds)
        )
    )

    incoming_all = gather_plane(incoming_now)
    hidden_near = spread_near(hidden_block)
    out_blocks = heads_spread(out_block) if split_heads else [out_block]
    score_scale = HEAD_DIM ** (-0.5)
    projected = dot(qkv_t, normed_one, 1, 1)
    q_t = rotate(projected[:width], cosine, sine).astype(bf16) * bf16(score_scale)
    k_t = rotate(projected[width : 2 * width], cosine, sine).astype(bf16)
    v_t = projected[2 * width :].astype(bf16)
    k_h = k_t.reshape(heads, HEAD_DIM, length).transpose(0, 2, 1)
    v_h = v_t.reshape(heads, HEAD_DIM, length).transpose(0, 2, 1)
    q_t, hidden_near, out_blocks = lax.optimization_barrier((q_t, hidden_near, out_blocks))
    hidden_far = spread_far(hidden_near)
    o_t, lse = attend(bounds, q_t, k_h, v_t)
    o_t, incoming_all, hidden_far = lax.optimization_barrier((o_t, incoming_all, hidden_far))

    out_full = heads_whole(out_blocks, HEAD_DIM).reshape(width, model)
    attention_branch = scatter_rows(dot(o_t, out_full, 0, 0))
    hidden = rows_in + attention_branch
    inverse_two = norm_inverse(hidden)
    normal_two = hidden * inverse_two
    normed_two = gather_plane((normal_two * gains[1]).astype(bf16))

    hidden_full = jnp.stack(spread_blocks(hidden_block, hidden_near, hidden_far))
    hidden_full = hidden_full.reshape(seqs, n_context, 3, block_hidden, rows)
    hidden_full = hidden_full.transpose(2, 0, 3, 1, 4).reshape(3 * hidden_width, model)
    gateup_t = hidden_full[: 2 * hidden_width]
    down_full = hidden_full[2 * hidden_width :]
    grad_activation = dot(incoming_all, down_full, 1, 1)
    normed_two, grad_activation = lax.optimization_barrier((normed_two, grad_activation))

    gate_up = dot(normed_two, gateup_t, 1, 1)
    gate, raised = gate_up[:, :hidden_width], gate_up[:, hidden_width:]
    gate_sigmoid = jax.nn.sigmoid(gate)
    gate_silu = gate * gate_sigmoid
    activation = (gate_silu * raised).astype(bf16)
    grad_gate = grad_activation * raised * gate_sigmoid * (1.0 + gate * (1.0 - gate_sigmoid))
    grad_up = grad_activation * gate_silu
    grad_gateup = jnp.concatenate([grad_gate, grad_up], axis=1).astype(bf16)
    feedforward_halves = scatter_start(dot(activation, down_full, 1, 0))
    second_halves = scatter_start(dot(grad_gateup, gateup_t, 1, 0))
    down_grad = dot(activation, incoming_all, 0, 0).astype(bf16)
    gateup_grad = dot(grad_gateup, normed_two, 0, 0).astype(bf16)
    hidden_grads = jnp.concatenate(
        [
            gateup_grad.reshape(2, seqs, block_hidden, n_context, rows),
            down_grad.reshape(1, seqs, block_hidden, n_context, rows),
        ],
        axis=0,
    )
    hidden_grads = list(hidden_grads.transpose(1, 3, 0, 2, 4).reshape(seqs, n_context, -1, rows))
    second_halves, hidden_grads = lax.optimization_barrier((second_halves, hidden_grads))
    hidden_grads_far = collect_far(hidden_grads)
    feedforward_branch = scatter_end(feedforward_halves)
    result = (hidden + feedforward_branch).astype(bf16)
    if n_extra > 1:
        result = lax.all_gather(result, "extra", axis=0, tiled=True)
    grad_normed_two = scatter_end(second_halves)
    grad_normed_two, result, hidden_grads_far = lax.optimization_barrier(
        (grad_normed_two, result, hidden_grads_far)
    )

    hidden_grads = collect_near(hidden_grads, hidden_grads_far)
    result_near = spread_near(result)
    grad_rows_two, gain_two = norm_backward(grad_normed_two, normal_two, inverse_two, gains[1])
    grad_hidden = incoming.astype(f32) + grad_rows_two
    grad_hidden_all = gather_plane(grad_hidden.astype(bf16))
    grad_hidden_all, hidden_grads, result_near = lax.optimization_barrier(
        (grad_hidden_all, hidden_grads, result_near)
    )

    result_far = spread_far(result_near)
    g_t = dot(out_full, grad_hidden_all, 1, 1).astype(bf16)
    dq_t, dk_t, dv_t = attend_back(bounds, q_t, g_t, o_t, lse, k_h, v_h, k_t)
    dq_t, dk_t, dv_t, result_far = lax.optimization_barrier((dq_t, dk_t, dv_t, result_far))
    grad_projected = jnp.concatenate(
        [rotate(dq_t * score_scale, cosine, -sine), rotate(dk_t, cosine, -sine), dv_t], axis=0
    ).astype(bf16)

    piece = own_len // TAIL_CHUNKS
    first_part = dot(grad_projected, qkv_t, 0, 0).astype(bf16)
    first_part = first_part.reshape(n_context * n_extra, own_len, model)
    input_pieces = []
    gain_one = jnp.zeros((model,), f32)
    for i in range(TAIL_CHUNKS):
        part = slice(i * piece, (i + 1) * piece)
        grad_normed_one = scatter_rows(first_part[:, part].reshape(-1, model))
        grad_rows_one, gain_part = norm_backward(
            grad_normed_one, normal_one[part], inverse_one[part], gains[0]
        )
        gain_one = gain_one + gain_part
        grad_input = (grad_hidden[part] + grad_rows_one).astype(bf16)
        gathered = lax.all_gather(grad_input, ("seq", "extra"), axis=0, tiled=False)
        input_pieces.append(gathered.reshape(seqs, n_extra, piece, model))

    out_grad = dot(o_t, grad_hidden_all, 1, 0).reshape(heads, HEAD_DIM, model)
    qkv_grad = dot(grad_projected, normed_one, 1, 0)
    qkv_grad = qkv_grad.reshape(3, heads, HEAD_DIM, model).transpose(1, 0, 2, 3)
    qkv_grad = qkv_grad.reshape(heads, 3 * HEAD_DIM, model)
    heads_grad = heads_back(jnp.concatenate([qkv_grad, out_grad], axis=1))
    qkv_grad = heads_grad[:, : 3 * HEAD_DIM].reshape(block_heads, 3, HEAD_DIM, rows)
    out_grad = heads_grad[:, 3 * HEAD_DIM :]
    hidden_grad = exchange(total(hidden_grads).astype(bf16)).astype(f32)
    hidden_grad = hidden_grad.reshape(n_context, 3, block_hidden, rows)

    results = spread_line(result, result_near, result_far)
    gains_grad = lax.psum(jnp.stack([gain_one, gain_two]), everyone)
    gains_grad = lax.dynamic_slice_in_dim(gains_grad, lax.axis_index(context) * rows, rows, 1)
    input_pieces[-1] = after(input_pieces[-1], gains_grad)
    input_grad = jnp.concatenate(input_pieces, axis=2).astype(f32)
    return (
        results,
        input_grad.reshape(seqs, local_len, model),
        gains_grad,
        qkv_grad.transpose(1, 3, 0, 2).reshape(qkv_weight.shape),
        out_grad.reshape(out_weight.shape),
        hidden_grad[:, :2].transpose(1, 3, 0, 2).reshape(gateup_weight.shape),
        hidden_grad[:, 2].reshape(down_weight.shape),
    )


def solution(mesh):
    n_context, n_tensor = mesh.shape["context"], mesh.shape["tensor"]
    n_core, n_pair = math.gcd(n_context, 2), math.gcd(n_context, 4) // math.gcd(n_context, 2)
    context, tensor = ("chips", "pair", "core"), ("seq", "extra")

    def program(block_input, *others):
        seqs = block_input.shape[0]
        n_extra = n_tensor // seqs
        assert n_extra * seqs == n_tensor and seqs == 4
        parts = (n_context // (n_pair * n_core), n_pair, n_core, seqs, n_extra)
        split = Mesh(mesh.devices.reshape(parts), (*context, *tensor))
        in_specs = (
            P(None, context, None),
            P(),
            P(None, context),
            P(None, context, tensor),
            P(tensor, context),
            P(None, context, tensor),
            P(tensor, context),
            P(None, context, None),
        )
        out_specs = (
            P(None, context, None),
            P(None, context, None),
            P(None, context),
            P(None, context, tensor),
            P(tensor, context),
            P(None, context, tensor),
            P(tensor, context),
        )
        return jax.shard_map(
            functools.partial(shards, parts),
            mesh=split,
            in_specs=in_specs,
            out_specs=out_specs,
            check_vma=False,
        )(block_input, *others)

    return program
```

```python
import functools
import math

import jax
import jax.numpy as jnp
from jax import lax
from jax.experimental import pallas as pl
from jax.experimental.pallas import tpu as pltpu
from jax.sharding import Mesh
from jax.sharding import PartitionSpec as P

HEAD_DIM = 64
WINDOW = 2048
BLOCK = 512

epsilon = 1e-05
rope_base = 10000.0
masked_fill = -1e30

f32 = jnp.float32
bf16 = jnp.bfloat16
VMEM_BYTES = 56 * 1024 * 1024


def dot(a, b, ca, cb):
    return lax.dot_general(a, b, (((ca,), (cb,)), ((), ())), preferred_element_type=f32)


def visible_block(low_row, q0, k0, q_block, k_block):
    key = k0 + lax.broadcasted_iota(jnp.int32, (k_block, q_block), 0)
    query = q0 + lax.broadcasted_iota(jnp.int32, (k_block, q_block), 1)
    return (key >= low_row) & (key <= query)


def key_loops(lo_ref, full_ref, q_block, k_block, step, carry):
    qb = pl.program_id(0)
    lo = lo_ref[qb]
    diagonal = qb * q_block // k_block
    full = jnp.minimum(jnp.maximum(full_ref[qb], lo), diagonal)
    carry = lax.fori_loop(lo, full, functools.partial(step, True), carry)
    carry = lax.fori_loop(full, diagonal, functools.partial(step, False), carry)
    for extra in range(max(1, q_block // k_block)):
        carry = step(True, diagonal + extra, carry)
    return carry


def attend_kernel(k_block, lo_ref, full_ref, low_ref, q_ref, k_ref, v_ref, o_ref, lse_ref, acc_ref):
    heads = range(k_ref.shape[0])
    q_block = q_ref.shape[1]
    q0 = pl.program_id(0) * q_block
    rows = [pl.ds(h * HEAD_DIM, HEAD_DIM) for h in heads]
    acc_ref[...] = jnp.zeros_like(acc_ref)

    def step(masked, kb, carry):
        k0 = pl.multiple_of(kb * k_block, k_block)
        cols = pl.ds(k0, k_block)
        scores = [dot(k_ref[h, cols, :], q_ref[rows[h], :], 1, 0) for h in heads]
        if masked:
            visible = visible_block(low_ref[...], q0, k0, q_block, k_block)
            scores = [jnp.where(visible, v, masked_fill) for v in scores]
        top = [jnp.maximum(carry[h][0], jnp.max(scores[h], axis=0, keepdims=True)) for h in heads]
        weights = [jnp.exp(scores[h] - top[h]) for h in heads]
        added = [dot(v_ref[rows[h], cols], weights[h].astype(bf16), 1, 0) for h in heads]
        out = []
        for h in heads:
            fade = jnp.exp(carry[h][0] - top[h])
            total = carry[h][1] * fade + jnp.sum(weights[h], axis=0, keepdims=True)
            acc_ref[rows[h], :] = acc_ref[rows[h], :] * fade + added[h]
            out.append((top[h], total))
        return tuple(out)

    start = tuple(
        (jnp.full((1, q_block), masked_fill, f32), jnp.zeros((1, q_block), f32)) for _ in heads
    )
    final = key_loops(lo_ref, full_ref, q_block, k_block, step, start)
    for h in heads:
        top, total = final[h]
        o_ref[rows[h], :] = (acc_ref[rows[h], :] / total).astype(bf16)
        lse_ref[h : h + 1, :] = top + jnp.log(total)


def attend_back_kernel(
    k_block,
    lo_ref,
    full_ref,
    low_ref,
    q_ref,
    g_ref,
    o_ref,
    lse_ref,
    k_ref,
    v_ref,
    kt_ref,
    dq_ref,
    dk_ref,
    dv_ref,
):
    heads = range(k_ref.shape[0])
    q_block = q_ref.shape[1]
    q0 = pl.program_id(0) * q_block
    rows = [pl.ds(h * HEAD_DIM, HEAD_DIM) for h in heads]

    @pl.when(pl.program_id(0) == 0)
    def _():
        dk_ref[...] = jnp.zeros_like(dk_ref)
        dv_ref[...] = jnp.zeros_like(dv_ref)

    dq_ref[...] = jnp.zeros_like(dq_ref)
    inner = [
        jnp.sum(g_ref[r, :].astype(f32) * o_ref[r, :].astype(f32), axis=0, keepdims=True)
        for r in rows
    ]

    def step(masked, kb, carry):
        k0 = pl.multiple_of(kb * k_block, k_block)
        cols = pl.ds(k0, k_block)
        if masked:
            visible = visible_block(low_ref[...], q0, k0, q_block, k_block)
        for h in heads:
            r = rows[h]
            scores = dot(k_ref[h, cols, :], q_ref[r, :], 1, 0)
            grad_probs = dot(v_ref[h, cols, :], g_ref[r, :], 1, 0)
            if masked:
                scores = jnp.where(visible, scores, masked_fill)
            probs = jnp.exp(scores - lse_ref[h : h + 1, :])
            grad_scores = (probs * (grad_probs - inner[h])).astype(bf16)
            dv = dot(g_ref[r, :], probs.astype(bf16), 1, 1)
            dk = dot(q_ref[r, :], grad_scores, 1, 1)
            dq = dot(kt_ref[r, cols], grad_scores, 1, 0)
            dv_ref[r, cols] += dv
            dk_ref[r, cols] += dk
            dq_ref[r, :] += dq
        return carry

    key_loops(lo_ref, full_ref, q_block, k_block, step, 0)


def attention_specs(heads, length, q_block):
    width = heads * HEAD_DIM
    once = pl.Buffered(1)
    whole_t = pl.BlockSpec((width, length), lambda i, *_: (0, 0), pipeline_mode=once)
    whole_h = pl.BlockSpec((heads, length, HEAD_DIM), lambda i, *_: (0, 0, 0), pipeline_mode=once)
    tile = pl.BlockSpec((width, q_block), lambda i, *_: (0, i))
    low = pl.BlockSpec((1, q_block), lambda i, *_: (0, i))
    stat = pl.BlockSpec((heads, q_block), lambda i, *_: (0, i))
    return whole_t, whole_h, tile, low, stat


def attend(bounds, q_t, k_h, v_t):
    heads, length, _ = k_h.shape
    width = heads * HEAD_DIM
    block = math.gcd(BLOCK, length)
    whole_t, whole_h, tile, low, stat = attention_specs(heads, length, block)
    pairs = length * WINDOW * heads
    return pl.pallas_call(
        functools.partial(attend_kernel, block),
        out_shape=(
            jax.ShapeDtypeStruct((width, length), bf16),
            jax.ShapeDtypeStruct((heads, length), f32),
        ),
        grid_spec=pltpu.PrefetchScalarGridSpec(
            num_scalar_prefetch=2,
            grid=(length // block,),
            in_specs=[low, tile, whole_h, whole_t],
            out_specs=[tile, stat],
            scratch_shapes=[pltpu.VMEM((width, block), f32)],
        ),
        compiler_params=pltpu.CompilerParams(vmem_limit_bytes=VMEM_BYTES),
        cost_estimate=pl.CostEstimate(
            flops=pairs * 6 * 256, transcendentals=pairs, bytes_accessed=length * width * 8
        ),
        name="attend",
    )(*bounds, q_t, k_h, v_t)


def attend_back(bounds, q_t, g_t, o_t, lse, k_h, v_h, k_t):
    heads, length, _ = k_h.shape
    width = heads * HEAD_DIM
    block = math.gcd(BLOCK, length)
    whole_t, whole_h, tile, low, stat = attention_specs(heads, length, block)
    pairs = length * WINDOW * heads
    return pl.pallas_call(
        functools.partial(attend_back_kernel, block),
        out_shape=tuple(jax.ShapeDtypeStruct((width, length), f32) for _ in range(3)),
        grid_spec=pltpu.PrefetchScalarGridSpec(
            num_scalar_prefetch=2,
            grid=(length // block,),
            in_specs=[low, tile, tile, tile, stat, whole_h, whole_h, whole_t],
            out_specs=[tile, whole_t, whole_t],
        ),
        compiler_params=pltpu.CompilerParams(vmem_limit_bytes=VMEM_BYTES),
        cost_estimate=pl.CostEstimate(
            flops=pairs * 12 * 256, transcendentals=pairs, bytes_accessed=length * width * 24
        ),
        name="attend_back",
    )(*bounds, q_t, g_t, o_t, lse, k_h, v_h, k_t)


def attention_bounds(lengths, length):
    docs = lengths.shape[0]
    upto = jnp.arange(docs)[:, None] >= jnp.arange(docs)[None, :]
    ends = jnp.sum(jnp.where(upto, lengths[None, :], 0), axis=1)
    position = jnp.arange(length, dtype=jnp.int32)
    starts = jnp.max(jnp.where(ends[:, None] <= position[None, :], ends[:, None], 0), axis=0)
    low = jnp.maximum(starts, position - (WINDOW - 1)).astype(jnp.int32)
    block = math.gcd(BLOCK, length)
    by_block = low.reshape(length // block, block)
    first = by_block[:, 0] // block
    full = (by_block[:, -1] + block - 1) // block
    return first, full, low.reshape(1, length)


def rope_tables(length):
    half_dim = HEAD_DIM // 2
    counter = jnp.arange(half_dim, dtype=f32)
    frequency = jnp.exp(counter * (-2.0 * math.log(rope_base) / HEAD_DIM))
    angles = frequency[:, None] * jnp.arange(length, dtype=f32)[None, :]
    return jnp.cos(angles)[None], jnp.sin(angles)[None]


def rotate(values, cosine, sine):
    heads = values.shape[0] // HEAD_DIM
    v = values.reshape(heads, 2, HEAD_DIM // 2, values.shape[1])
    a, b = v[:, 0], v[:, 1]
    out = jnp.stack([a * cosine - b * sine, b * cosine + a * sine], axis=1)
    return out.reshape(values.shape)


def norm_inverse(rows):
    return lax.rsqrt(jnp.mean(rows * rows, axis=-1, keepdims=True) + epsilon)


def norm_backward(grad_normed, normal, inverse, gain):
    grad_normal = grad_normed * gain
    inner = jnp.mean(grad_normal * normal, axis=-1, keepdims=True)
    return inverse * (grad_normal - normal * inner), jnp.sum(grad_normed * normal, axis=0)


def swap(a, axis):
    return lax.ppermute(a, axis, [(0, 1), (1, 0)])


def halve(a, axis, dim):
    index = lax.axis_index(axis)
    mine = lax.dynamic_index_in_dim(a, index, dim, False)
    other = lax.dynamic_index_in_dim(a, 1 - index, dim, False)
    return mine.astype(f32) + swap(other, axis).astype(f32)


def after(a, *others):
    return lax.optimization_barrier((a, *others))[0]


def shards(
    parts,
    block_input,
    doc_lengths,
    norm_gains,
    qkv_weight,
    out_weight,
    gateup_weight,
    down_weight,
    cotangent,
):
    n_chips, n_pair, n_core, seqs, n_extra = parts
    n_context = n_chips * n_pair * n_core
    context = ("chips", "pair", "core")
    plane = (*context, "extra")
    everyone = (*plane, "seq")
    cube = n_chips == n_pair == n_core == 2 and n_extra == 1
    model = block_input.shape[2]
    local_len = block_input.shape[1]
    length = local_len * n_context
    own_len = local_len // n_extra
    rows = model // n_context
    block_heads = qkv_weight.shape[2] // HEAD_DIM
    heads = seqs * block_heads // n_context
    split_heads = block_heads % n_context == 0
    block_hidden = gateup_weight.shape[2] // n_context
    hidden_width = seqs * block_hidden
    width = heads * HEAD_DIM
    seq = lax.axis_index("seq")
    first_row = lax.axis_index("extra") * own_len

    def exchange(a):
        return lax.all_to_all(a, context, split_axis=0, concat_axis=0, tiled=True)

    def send(a, *pairs):
        return lax.ppermute(a, "seq", pairs)

    def up(a, first=0):
        return send(a, *((i, i + 1) for i in range(first, seqs - 1)))

    def down(a, last=None):
        return send(a, *((i, i - 1) for i in range(1, seqs if last is None else last)))

    def spread_near(a):
        return [up(a), down(a)]

    def spread_far(near):
        across = jnp.where(seq == 1, near[0], near[1])
        return [up(near[0], 1), down(near[1], seqs - 1), send(across, (1, 3), (2, 0))]

    def spread_blocks(a, near, far):
        return [
            a,
            jnp.where(seq == 0, far[2], near[0]),
            jnp.where(seq >= 2, far[0], far[1]),
            jnp.where(seq == seqs - 1, far[2], near[1]),
        ]

    def spread_line(a, near, far):
        line = jnp.stack([far[2], far[0], near[0], a, near[1], far[1], far[2]])
        return lax.dynamic_slice_in_dim(line, seqs - 1 - seq, seqs, 0)

    def collect_far(blocks):
        across = jnp.where(seq == 0, blocks[1], blocks[3])
        return [
            send(blocks[2], *((i, i + 1) for i in range(seqs - 2))),
            send(blocks[2], *((i, i - 1) for i in range(2, seqs))),
            send(across, (0, 2), (3, 1)),
        ]

    def collect_near(blocks, far):
        above = blocks[3].astype(f32) + far[0].astype(f32) + jnp.where(seq == 2, far[2], 0)
        below = blocks[1].astype(f32) + far[1].astype(f32) + jnp.where(seq == 1, far[2], 0)
        return [blocks[0], up(above.astype(bf16)), down(below.astype(bf16))]

    def total(blocks):
        return sum((b.astype(f32) for b in blocks[1:]), blocks[0].astype(f32))

    def gather_plane(a):
        return lax.all_gather(a, plane, axis=0, tiled=True)

    def scatter_plane(a):
        return lax.psum_scatter(a.astype(bf16), plane, scatter_dimension=0, tiled=True).astype(f32)

    def scatter_start(part):
        part = part.astype(bf16)
        if not cube:
            return [scatter_plane(part)]
        size = part.shape[0] // n_context
        a = halve(part.reshape(n_chips, n_pair, n_core, size, model), "core", 2).astype(bf16)
        one, two = a[:, :, : size // 2], a[:, :, size // 2 :]
        return [halve(one, "pair", 1).astype(bf16), halve(two, "chips", 0).astype(bf16)]

    def scatter_start_by_core(product, a):
        if not cube:
            return scatter_start(product(a))
        core = lax.axis_index("core")
        a = a.reshape(n_chips * n_pair, n_core, own_len, a.shape[1])

        def part(index):
            rows_of = lax.dynamic_index_in_dim(a, index, 1, False)
            return product(rows_of.reshape(-1, a.shape[3]))

        theirs = swap(part(1 - core).astype(bf16), "core")
        mine = (part(core) + theirs.astype(f32)).astype(bf16)
        return mine.reshape(n_chips, n_pair, own_len, model)

    def scatter_middle(a):
        if not cube:
            return a
        half = own_len // 2
        one, two = a[:, :, :half], a[:, :, half:]
        return [halve(one, "pair", 1).astype(bf16), halve(two, "chips", 0).astype(bf16)]

    def scatter_end(halves):
        if not cube:
            return halves[0]
        return jnp.concatenate([halve(halves[0], "chips", 0), halve(halves[1], "pair", 0)], axis=0)

    def scatter_rows(part):
        return scatter_end(scatter_start(part))

    def own(a):
        return lax.dynamic_slice(a, (seq, first_row, 0), (1, own_len, model))[0]

    def heads_out(a):
        if split_heads:
            return exchange(a.reshape(n_context, -1, rows))
        m = a.shape[1]
        a = lax.all_gather(a, "seq", axis=0, tiled=True)
        return exchange(a.reshape(n_context, heads * m, rows))

    def heads_spread(a):
        near = spread_near(a)
        return spread_blocks(a, near, spread_far(near))

    def heads_whole(blocks, m):
        a = jnp.stack(blocks).reshape(len(blocks), n_context, heads // len(blocks), m, rows)
        return a.transpose(0, 2, 3, 1, 4).reshape(heads, m, model)

    def heads_split(a):
        a = a.astype(bf16).reshape(seqs, heads // seqs, a.shape[1], n_context, rows)
        return list(a.transpose(0, 3, 1, 2, 4).reshape(seqs, n_context, -1, rows))

    def heads_back(a):
        m = a.shape[1]
        a = a.astype(bf16).reshape(heads, m, n_context, rows).transpose(2, 0, 1, 3)
        a = exchange(a.reshape(n_context, -1, rows)).reshape(seqs * block_heads, m, rows)
        return lax.psum_scatter(a, "seq", scatter_dimension=0, tiled=True).astype(f32)

    gains = lax.all_gather(norm_gains, context, axis=1, tiled=True).astype(f32)
    rows_in = own(block_input).astype(f32)
    incoming = own(cotangent)
    inverse_one = norm_inverse(rows_in)
    normal_one = rows_in * inverse_one
    normed_one = gather_plane((normal_one * gains[0]).astype(bf16))

    qkv_local = qkv_weight.reshape(3, rows, block_heads, HEAD_DIM).transpose(2, 0, 3, 1)
    qkv_block = heads_out(qkv_local.reshape(block_heads, 3 * HEAD_DIM, rows))
    qkv_block, out_local, gateup_local, down_local = lax.optimization_barrier(
        (qkv_block, out_weight, gateup_weight, down_weight)
    )
    qkv_blocks = heads_spread(qkv_block) if split_heads else [qkv_block]
    qkv_t = heads_whole(qkv_blocks, 3 * HEAD_DIM).reshape(heads, 3, HEAD_DIM, model)
    qkv_t = qkv_t.transpose(1, 0, 2, 3).reshape(3 * width, model)
    out_block = heads_out(out_local.reshape(block_heads, HEAD_DIM, rows))
    gateup_local = gateup_local.reshape(2, rows, n_context, block_hidden).transpose(2, 0, 3, 1)
    hidden_local = jnp.concatenate(
        [
            gateup_local.reshape(n_context, 2 * block_hidden, rows),
            down_local.reshape(n_context, block_hidden, rows),
        ],
        axis=1,
    )
    cosine, sine = rope_tables(length)
    bounds = attention_bounds(lax.dynamic_slice_in_dim(doc_lengths, seq, 1, 0)[0], length)
    normed_one, incoming_now, qkv_t, out_block, hidden_local, cosine, sine, bounds = (
        lax.optimization_barrier(
            (normed_one, incoming, qkv_t, out_block, hidden_local, cosine, sine, bounds)
        )
    )

    incoming_all = gather_plane(incoming_now)
    hidden_block = exchange(hidden_local)
    out_near = spread_near(out_block) if split_heads else []
    score_scale = HEAD_DIM ** (-0.5)
    projected = dot(qkv_t, normed_one, 1, 1)
    q_t = rotate(projected[:width], cosine, sine).astype(bf16) * bf16(score_scale)
    k_t = rotate(projected[width : 2 * width], cosine, sine).astype(bf16)
    v_t = projected[2 * width :].astype(bf16)
    k_h = k_t.reshape(heads, HEAD_DIM, length).transpose(0, 2, 1)
    v_h = v_t.reshape(heads, HEAD_DIM, length).transpose(0, 2, 1)
    q_t, hidden_block, out_near = lax.optimization_barrier((q_t, hidden_block, out_near))
    out_far = spread_far(out_near) if split_heads else []
    hidden_near = spread_near(hidden_block)
    o_t, lse = attend(bounds, q_t, k_h, v_t)
    o_t, incoming_all, hidden_near, out_far = lax.optimization_barrier(
        (o_t, incoming_all, hidden_near, out_far)
    )
    hidden_far = spread_far(hidden_near)

    out_blocks = spread_blocks(out_block, out_near, out_far) if split_heads else [out_block]
    out_full = heads_whole(out_blocks, HEAD_DIM).reshape(width, model)
    attention_branch = scatter_plane(dot(o_t, out_full, 0, 0))
    attention_branch, hidden_far = lax.optimization_barrier((attention_branch, hidden_far))
    hidden = rows_in + attention_branch
    inverse_two = norm_inverse(hidden)
    normal_two = hidden * inverse_two
    normed_two = gather_plane((normal_two * gains[1]).astype(bf16))

    hidden_full = jnp.stack(spread_blocks(hidden_block, hidden_near, hidden_far))
    hidden_full = hidden_full.reshape(seqs, n_context, 3, block_hidden, rows)
    hidden_full = hidden_full.transpose(2, 0, 3, 1, 4).reshape(3 * hidden_width, model)
    gateup_t = hidden_full[: 2 * hidden_width]
    down_full = hidden_full[2 * hidden_width :]
    grad_activation = dot(incoming_all, down_full, 1, 1)
    normed_two, grad_activation = lax.optimization_barrier((normed_two, grad_activation))

    gate_up = dot(normed_two, gateup_t, 1, 1)
    gate, raised = gate_up[:, :hidden_width], gate_up[:, hidden_width:]
    gate_sigmoid = jax.nn.sigmoid(gate)
    gate_silu = gate * gate_sigmoid
    activation = (gate_silu * raised).astype(bf16)
    grad_gate = grad_activation * raised * gate_sigmoid * (1.0 + gate * (1.0 - gate_sigmoid))
    grad_up = grad_activation * gate_silu
    grad_gateup = jnp.concatenate([grad_gate, grad_up], axis=1).astype(bf16)
    feedforward_branch = scatter_plane(dot(activation, down_full, 1, 0))
    second_sums = scatter_start_by_core(lambda a: dot(a, gateup_t, 1, 0), grad_gateup)
    grad_normed_two = scatter_end(scatter_middle(second_sums))
    grad_normed_two, feedforward_branch, activation, grad_gateup = lax.optimization_barrier(
        (grad_normed_two, feedforward_branch, activation, grad_gateup)
    )

    result = (hidden + feedforward_branch).astype(bf16)
    if n_extra > 1:
        result = lax.all_gather(result, "extra", axis=0, tiled=True)
    result_near = spread_near(result)
    grad_rows_two, gain_two = norm_backward(grad_normed_two, normal_two, inverse_two, gains[1])
    grad_hidden = incoming.astype(f32) + grad_rows_two
    grad_hidden_all = gather_plane(grad_hidden.astype(bf16))
    down_grad = dot(activation, incoming_all, 0, 0).astype(bf16)
    gateup_grad = dot(grad_gateup, normed_two, 0, 0).astype(bf16)
    hidden_grads = jnp.concatenate(
        [
            gateup_grad.reshape(2, seqs, block_hidden, n_context, rows),
            down_grad.reshape(1, seqs, block_hidden, n_context, rows),
        ],
        axis=0,
    )
    hidden_grads = list(hidden_grads.transpose(1, 3, 0, 2, 4).reshape(seqs, n_context, -1, rows))
    hidden_grads_far = collect_far(hidden_grads)
    grad_hidden_all, hidden_grads_far, result_near = lax.optimization_barrier(
        (grad_hidden_all, hidden_grads_far, result_near)
    )

    result_far = spread_far(result_near)
    g_t = dot(out_full, grad_hidden_all, 1, 1).astype(bf16)
    dq_t, dk_t, dv_t = attend_back(bounds, q_t, g_t, o_t, lse, k_h, v_h, k_t)
    dq_t, dk_t, dv_t, result_far = lax.optimization_barrier((dq_t, dk_t, dv_t, result_far))
    grad_projected = jnp.concatenate(
        [rotate(dq_t * score_scale, cosine, -sine), rotate(dk_t, cosine, -sine), dv_t], axis=0
    ).astype(bf16)

    first_part = dot(grad_projected, qkv_t, 0, 0).astype(bf16)
    first_part, grad_projected = lax.optimization_barrier((first_part, grad_projected))
    grad_normed_one = scatter_plane(first_part)
    hidden_grads = collect_near(hidden_grads, hidden_grads_far)
    qkv_grad = dot(grad_projected, normed_one, 1, 0)
    qkv_grad = qkv_grad.reshape(3, heads, HEAD_DIM, model).transpose(1, 0, 2, 3)
    qkv_grad = qkv_grad.reshape(heads, 3 * HEAD_DIM, model)
    out_grad = dot(o_t, grad_hidden_all, 1, 0).reshape(heads, HEAD_DIM, model)
    heads_grad = jnp.concatenate([qkv_grad, out_grad], axis=1)
    if split_heads:
        heads_grads = heads_split(heads_grad)
        heads_grads = collect_near(heads_grads, collect_far(heads_grads))
    else:
        heads_grads = []
    grad_normed_one, hidden_grads, heads_grads = lax.optimization_barrier(
        (grad_normed_one, hidden_grads, heads_grads)
    )

    grad_rows_one, gain_one = norm_backward(grad_normed_one, normal_one, inverse_one, gains[0])
    grad_input = (grad_hidden + grad_rows_one).astype(bf16)
    input_grad = lax.all_gather(grad_input, ("seq", "extra"), axis=0, tiled=True).astype(f32)
    if split_heads:
        heads_grad = exchange(total(heads_grads).astype(bf16)).astype(f32)
        heads_grad = heads_grad.reshape(block_heads, 4 * HEAD_DIM, rows)
    else:
        heads_grad = heads_back(heads_grad)
    qkv_grad = heads_grad[:, : 3 * HEAD_DIM].reshape(block_heads, 3, HEAD_DIM, rows)
    out_grad = heads_grad[:, 3 * HEAD_DIM :]
    hidden_grad = exchange(total(hidden_grads).astype(bf16)).astype(f32)
    hidden_grad = hidden_grad.reshape(n_context, 3, block_hidden, rows)

    gains_grad = jnp.stack([gain_one, gain_two]).reshape(2, n_context, rows).transpose(1, 0, 2)
    gains_grad = jnp.sum(exchange(gains_grad), axis=0)
    if n_extra > 1:
        gains_grad = lax.psum(gains_grad, "extra")
    gains_near = spread_near(gains_grad)
    gains_grad = jnp.sum(spread_line(gains_grad, gains_near, spread_far(gains_near)), axis=0)
    results = spread_line(result, result_near, result_far)
    return (
        results,
        input_grad.reshape(seqs, local_len, model),
        gains_grad,
        qkv_grad.transpose(1, 3, 0, 2).reshape(qkv_weight.shape),
        out_grad.reshape(out_weight.shape),
        hidden_grad[:, :2].transpose(1, 3, 0, 2).reshape(gateup_weight.shape),
        hidden_grad[:, 2].reshape(down_weight.shape),
    )


def solution(mesh):
    n_context, n_tensor = mesh.shape["context"], mesh.shape["tensor"]
    n_core, n_pair = math.gcd(n_context, 2), math.gcd(n_context, 4) // math.gcd(n_context, 2)
    context, tensor = ("chips", "pair", "core"), ("seq", "extra")

    def program(block_input, *others):
        seqs = block_input.shape[0]
        n_extra = n_tensor // seqs
        assert n_extra * seqs == n_tensor and seqs == 4
        parts = (n_context // (n_pair * n_core), n_pair, n_core, seqs, n_extra)
        split = Mesh(mesh.devices.reshape(parts), (*context, *tensor))
        in_specs = (
            P(None, context, None),
            P(),
            P(None, context),
            P(None, context, tensor),
            P(tensor, context),
            P(None, context, tensor),
            P(tensor, context),
            P(None, context, None),
        )
        out_specs = (
            P(None, context, None),
            P(None, context, None),
            P(None, context),
            P(None, context, tensor),
            P(tensor, context),
            P(None, context, tensor),
            P(tensor, context),
        )
        return jax.shard_map(
            functools.partial(shards, parts),
            mesh=split,
            in_specs=in_specs,
            out_specs=out_specs,
            check_vma=False,
        )(block_input, *others)

    return program
```

```python
import functools
import math

import jax
import jax.numpy as jnp
from jax import lax
from jax.experimental import pallas as pl
from jax.experimental.pallas import tpu as pltpu
from jax.sharding import Mesh
from jax.sharding import PartitionSpec as P

HEAD_DIM = 64
WINDOW = 2048
BLOCK = 512

epsilon = 1e-05
rope_base = 10000.0
masked_fill = -1e30

f32 = jnp.float32
bf16 = jnp.bfloat16
VMEM_BYTES = 56 * 1024 * 1024


def dot(a, b, ca, cb):
    return lax.dot_general(a, b, (((ca,), (cb,)), ((), ())), preferred_element_type=f32)


def visible_block(low_row, q0, k0, q_block, k_block):
    key = k0 + lax.broadcasted_iota(jnp.int32, (k_block, q_block), 0)
    query = q0 + lax.broadcasted_iota(jnp.int32, (k_block, q_block), 1)
    return (key >= low_row) & (key <= query)


def key_loops(lo_ref, full_ref, q_block, k_block, step, carry):
    qb = pl.program_id(0)
    lo = lo_ref[qb]
    diagonal = qb * q_block // k_block
    full = jnp.minimum(jnp.maximum(full_ref[qb], lo), diagonal)
    carry = lax.fori_loop(lo, full, functools.partial(step, True), carry)
    carry = lax.fori_loop(full, diagonal, functools.partial(step, False), carry)
    for extra in range(max(1, q_block // k_block)):
        carry = step(True, diagonal + extra, carry)
    return carry


def attend_kernel(
    k_block,
    lo_ref,
    full_ref,
    low_ref,
    q_ref,
    k_ref,
    v_ref,
    out_ref,
    o_ref,
    lse_ref,
    part_ref,
    acc_ref,
):
    heads = range(k_ref.shape[0])
    q_block = q_ref.shape[1]
    q0 = pl.program_id(0) * q_block
    rows = [pl.ds(h * HEAD_DIM, HEAD_DIM) for h in heads]
    acc_ref[...] = jnp.zeros_like(acc_ref)

    def step(masked, kb, carry):
        k0 = pl.multiple_of(kb * k_block, k_block)
        cols = pl.ds(k0, k_block)
        scores = [dot(k_ref[h, cols, :], q_ref[rows[h], :], 1, 0) for h in heads]
        if masked:
            visible = visible_block(low_ref[...], q0, k0, q_block, k_block)
            scores = [jnp.where(visible, v, masked_fill) for v in scores]
        top = [jnp.maximum(carry[h][0], jnp.max(scores[h], axis=0, keepdims=True)) for h in heads]
        weights = [jnp.exp(scores[h] - top[h]) for h in heads]
        added = [dot(v_ref[rows[h], cols], weights[h].astype(bf16), 1, 0) for h in heads]
        out = []
        for h in heads:
            fade = jnp.exp(carry[h][0] - top[h])
            total = carry[h][1] * fade + jnp.sum(weights[h], axis=0, keepdims=True)
            acc_ref[rows[h], :] = acc_ref[rows[h], :] * fade + added[h]
            out.append((top[h], total))
        return tuple(out)

    start = tuple(
        (jnp.full((1, q_block), masked_fill, f32), jnp.zeros((1, q_block), f32)) for _ in heads
    )
    final = key_loops(lo_ref, full_ref, q_block, k_block, step, start)
    for h in heads:
        top, total = final[h]
        o_ref[rows[h], :] = (acc_ref[rows[h], :] / total).astype(bf16)
        lse_ref[h : h + 1, :] = top + jnp.log(total)
    attended = o_ref[...]
    for c in range(0, out_ref.shape[1], k_block):
        cols = pl.ds(c, k_block)
        part_ref[:, cols] = dot(attended, out_ref[:, cols], 0, 0).astype(bf16)


def attend_back_kernel(
    k_block,
    lo_ref,
    full_ref,
    low_ref,
    q_ref,
    hidden_ref,
    o_ref,
    lse_ref,
    k_ref,
    v_ref,
    kt_ref,
    out_ref,
    cos_ref,
    sin_ref,
    grad_ref,
    g_ref,
    dq_ref,
    dk_ref,
    dv_ref,
):
    heads = range(k_ref.shape[0])
    q_block = q_ref.shape[1]
    q0 = pl.multiple_of(pl.program_id(0) * q_block, q_block)
    width = q_ref.shape[0]
    half_dim = HEAD_DIM // 2
    rows = [pl.ds(h * HEAD_DIM, HEAD_DIM) for h in heads]

    def unrotated(ref, here, cols):
        cosine, sine = cos_ref[:, cols], sin_ref[:, cols]
        out = []
        for h in heads:
            at = h * HEAD_DIM
            a, b = ref[at : at + half_dim, here], ref[at + half_dim : at + HEAD_DIM, here]
            out += [a * cosine + b * sine, b * cosine - a * sine]
        return jnp.concatenate(out, axis=0).T

    @pl.when(pl.program_id(0) == 0)
    def _():
        dk_ref[...] = jnp.zeros_like(dk_ref)
        dv_ref[...] = jnp.zeros_like(dv_ref)

    g_ref[...] = dot(out_ref[...], hidden_ref[...], 1, 1).astype(bf16)
    dq_ref[...] = jnp.zeros_like(dq_ref)
    inner = [
        jnp.sum(g_ref[r, :].astype(f32) * o_ref[r, :].astype(f32), axis=0, keepdims=True)
        for r in rows
    ]

    def step(masked, kb, carry):
        k0 = pl.multiple_of(kb * k_block, k_block)
        cols = pl.ds(k0, k_block)
        if masked:
            visible = visible_block(low_ref[...], q0, k0, q_block, k_block)
        for h in heads:
            r = rows[h]
            scores = dot(k_ref[h, cols, :], q_ref[r, :], 1, 0)
            grad_probs = dot(v_ref[h, cols, :], g_ref[r, :], 1, 0)
            if masked:
                scores = jnp.where(visible, scores, masked_fill)
            probs = jnp.exp(scores - lse_ref[h : h + 1, :])
            grad_scores = (probs * (grad_probs - inner[h])).astype(bf16)
            dv = dot(g_ref[r, :], probs.astype(bf16), 1, 1)
            dk = dot(q_ref[r, :], grad_scores, 1, 1)
            dq = dot(kt_ref[r, cols], grad_scores, 1, 0)
            dv_ref[r, cols] += dv
            dk_ref[r, cols] += dk
            dq_ref[r, :] += dq
        return carry

    key_loops(lo_ref, full_ref, q_block, k_block, step, 0)
    here = pl.ds(q0, q_block)
    dq = unrotated(dq_ref, slice(None), here) * HEAD_DIM ** (-0.5)
    grad_ref[here, 0:width] = dq.astype(bf16)

    @pl.when(pl.program_id(0) == pl.num_programs(0) - 1)
    def _():
        for c in range(0, kt_ref.shape[1], k_block):
            cols = pl.ds(c, k_block)
            grad_ref[cols, width : 2 * width] = unrotated(dk_ref, cols, cols).astype(bf16)
            grad_ref[cols, 2 * width : 3 * width] = dv_ref[:, cols].T.astype(bf16)


def attention_specs(heads, length, q_block):
    width = heads * HEAD_DIM
    once = pl.Buffered(1)
    whole_t = pl.BlockSpec((width, length), lambda i, *_: (0, 0), pipeline_mode=once)
    whole_h = pl.BlockSpec((heads, length, HEAD_DIM), lambda i, *_: (0, 0, 0), pipeline_mode=once)
    tile = pl.BlockSpec((width, q_block), lambda i, *_: (0, i))
    low = pl.BlockSpec((1, q_block), lambda i, *_: (0, i))
    stat = pl.BlockSpec((heads, q_block), lambda i, *_: (0, i))
    return whole_t, whole_h, tile, low, stat


def attend(bounds, q_t, k_h, v_t, out_full):
    heads, length, _ = k_h.shape
    width, model = out_full.shape
    block = math.gcd(BLOCK, length)
    whole_t, whole_h, tile, low, stat = attention_specs(heads, length, block)
    pairs = length * WINDOW * heads
    return pl.pallas_call(
        functools.partial(attend_kernel, block),
        out_shape=(
            jax.ShapeDtypeStruct((width, length), bf16),
            jax.ShapeDtypeStruct((heads, length), f32),
            jax.ShapeDtypeStruct((length, model), bf16),
        ),
        grid_spec=pltpu.PrefetchScalarGridSpec(
            num_scalar_prefetch=2,
            grid=(length // block,),
            in_specs=[
                low,
                tile,
                whole_h,
                whole_t,
                pl.BlockSpec((width, model), lambda i, *_: (0, 0), pipeline_mode=pl.Buffered(1)),
            ],
            out_specs=[tile, stat, pl.BlockSpec((block, model), lambda i, *_: (i, 0))],
            scratch_shapes=[pltpu.VMEM((width, block), f32)],
        ),
        compiler_params=pltpu.CompilerParams(vmem_limit_bytes=VMEM_BYTES),
        cost_estimate=pl.CostEstimate(
            flops=pairs * 6 * 256, transcendentals=pairs, bytes_accessed=length * model * 2
        ),
        name="attend",
    )(*bounds, q_t, k_h, v_t, out_full)


def attend_back(bounds, q_t, grad_hidden, o_t, lse, k_h, v_h, k_t, out_full, cosine, sine):
    heads, length, _ = k_h.shape
    width, model = out_full.shape
    block = math.gcd(BLOCK, length)
    whole_t, whole_h, tile, low, stat = attention_specs(heads, length, block)
    once = pl.Buffered(1)
    table = pl.BlockSpec((HEAD_DIM // 2, length), lambda i, *_: (0, 0), pipeline_mode=once)
    pairs = length * WINDOW * heads
    return pl.pallas_call(
        functools.partial(attend_back_kernel, block),
        out_shape=jax.ShapeDtypeStruct((length, 3 * width), bf16),
        grid_spec=pltpu.PrefetchScalarGridSpec(
            num_scalar_prefetch=2,
            grid=(length // block,),
            in_specs=[
                low,
                tile,
                pl.BlockSpec((block, model), lambda i, *_: (i, 0)),
                tile,
                stat,
                whole_h,
                whole_h,
                whole_t,
                pl.BlockSpec((width, model), lambda i, *_: (0, 0), pipeline_mode=once),
                table,
                table,
            ],
            out_specs=pl.BlockSpec((length, 3 * width), lambda i, *_: (0, 0)),
            scratch_shapes=[
                pltpu.VMEM((width, block), bf16),
                pltpu.VMEM((width, block), f32),
                pltpu.VMEM((width, length), f32),
                pltpu.VMEM((width, length), f32),
            ],
        ),
        compiler_params=pltpu.CompilerParams(vmem_limit_bytes=VMEM_BYTES),
        cost_estimate=pl.CostEstimate(
            flops=pairs * 12 * 256, transcendentals=pairs, bytes_accessed=length * width * 24
        ),
        name="attend_back",
    )(*bounds, q_t, grad_hidden, o_t, lse, k_h, v_h, k_t, out_full, cosine, sine)


def attention_bounds(lengths, length):
    docs = lengths.shape[0]
    upto = jnp.arange(docs)[:, None] >= jnp.arange(docs)[None, :]
    ends = jnp.sum(jnp.where(upto, lengths[None, :], 0), axis=1)
    position = jnp.arange(length, dtype=jnp.int32)
    starts = jnp.max(jnp.where(ends[:, None] <= position[None, :], ends[:, None], 0), axis=0)
    low = jnp.maximum(starts, position - (WINDOW - 1)).astype(jnp.int32)
    block = math.gcd(BLOCK, length)
    by_block = low.reshape(length // block, block)
    first = by_block[:, 0] // block
    full = (by_block[:, -1] + block - 1) // block
    return first, full, low.reshape(1, length)


def rope_tables(length):
    half_dim = HEAD_DIM // 2
    counter = jnp.arange(half_dim, dtype=f32)
    frequency = jnp.exp(counter * (-2.0 * math.log(rope_base) / HEAD_DIM))
    angles = frequency[:, None] * jnp.arange(length, dtype=f32)[None, :]
    return jnp.cos(angles), jnp.sin(angles)


def rotate(values, cosine, sine):
    heads = values.shape[0] // HEAD_DIM
    v = values.reshape(heads, 2, HEAD_DIM // 2, values.shape[1])
    a, b = v[:, 0], v[:, 1]
    out = jnp.stack([a * cosine - b * sine, b * cosine + a * sine], axis=1)
    return out.reshape(values.shape)


def norm_inverse(rows):
    return lax.rsqrt(jnp.mean(rows * rows, axis=-1, keepdims=True) + epsilon)


def norm_backward(grad_normed, normal, inverse, gain):
    grad_normal = grad_normed * gain
    inner = jnp.mean(grad_normal * normal, axis=-1, keepdims=True)
    return inverse * (grad_normal - normal * inner), jnp.sum(grad_normed * normal, axis=0)


def swap(a, axis):
    return lax.ppermute(a, axis, [(0, 1), (1, 0)])


def halve(a, axis, dim):
    index = lax.axis_index(axis)
    mine = lax.dynamic_index_in_dim(a, index, dim, False)
    other = lax.dynamic_index_in_dim(a, 1 - index, dim, False)
    return mine.astype(f32) + swap(other, axis).astype(f32)


def after(a, *others):
    return lax.optimization_barrier((a, *others))[0]


def shards(
    parts,
    block_input,
    doc_lengths,
    norm_gains,
    qkv_weight,
    out_weight,
    gateup_weight,
    down_weight,
    cotangent,
):
    n_chips, n_pair, n_core, seqs, n_extra = parts
    n_context = n_chips * n_pair * n_core
    context = ("chips", "pair", "core")
    plane = (*context, "extra")
    everyone = (*plane, "seq")
    cube = n_chips == n_pair == n_core == 2 and n_extra == 1
    model = block_input.shape[2]
    local_len = block_input.shape[1]
    length = local_len * n_context
    own_len = local_len // n_extra
    rows = model // n_context
    block_heads = qkv_weight.shape[2] // HEAD_DIM
    heads = seqs * block_heads // n_context
    split_heads = block_heads % n_context == 0
    block_hidden = gateup_weight.shape[2] // n_context
    hidden_width = seqs * block_hidden
    width = heads * HEAD_DIM
    seq = lax.axis_index("seq")
    first_row = lax.axis_index("extra") * own_len

    def exchange(a):
        return lax.all_to_all(a, context, split_axis=0, concat_axis=0, tiled=True)

    def send(a, *pairs):
        return lax.ppermute(a, "seq", pairs)

    def up(a, first=0):
        return send(a, *((i, i + 1) for i in range(first, seqs - 1)))

    def down(a, last=None):
        return send(a, *((i, i - 1) for i in range(1, seqs if last is None else last)))

    def spread_near(a):
        return [up(a), down(a)]

    def spread_far(near):
        across = jnp.where(seq == 1, near[0], near[1])
        return [up(near[0], 1), down(near[1], seqs - 1), send(across, (1, 3), (2, 0))]

    def spread_blocks(a, near, far):
        return [
            a,
            jnp.where(seq == 0, far[2], near[0]),
            jnp.where(seq >= 2, far[0], far[1]),
            jnp.where(seq == seqs - 1, far[2], near[1]),
        ]

    def spread_line(a, near, far):
        line = jnp.stack([far[2], far[0], near[0], a, near[1], far[1], far[2]])
        return lax.dynamic_slice_in_dim(line, seqs - 1 - seq, seqs, 0)

    def collect_far(blocks):
        across = jnp.where(seq == 0, blocks[1], blocks[3])
        return [
            send(blocks[2], *((i, i + 1) for i in range(seqs - 2))),
            send(blocks[2], *((i, i - 1) for i in range(2, seqs))),
            send(across, (0, 2), (3, 1)),
        ]

    def collect_near(blocks, far):
        above = blocks[3].astype(f32) + far[0].astype(f32) + jnp.where(seq == 2, far[2], 0)
        below = blocks[1].astype(f32) + far[1].astype(f32) + jnp.where(seq == 1, far[2], 0)
        return [blocks[0], up(above.astype(bf16)), down(below.astype(bf16))]

    def total(blocks):
        return sum((b.astype(f32) for b in blocks[1:]), blocks[0].astype(f32))

    def gather_plane(a):
        return lax.all_gather(a, plane, axis=0, tiled=True)

    def scatter_plane(a):
        return lax.psum_scatter(a.astype(bf16), plane, scatter_dimension=0, tiled=True).astype(f32)

    def scatter_cores(product, a, piece=slice(None)):
        a = a.reshape(-1, n_core, own_len, a.shape[1])[:, :, piece]
        if not cube:
            return product(a.reshape(-1, a.shape[3]))
        core = lax.axis_index("core")

        def part(index):
            rows_of = lax.dynamic_index_in_dim(a, index, 1, False)
            return product(rows_of.reshape(-1, a.shape[3]))

        theirs = swap(part(1 - core).astype(bf16), "core")
        mine = (part(core) + theirs.astype(f32)).astype(bf16)
        return mine.reshape(n_chips, n_pair, a.shape[2], model)

    def scatter_middle(a):
        if not cube:
            return [scatter_plane(a)]
        half = a.shape[2] // 2
        one, two = a[:, :, :half], a[:, :, half:]
        return [halve(one, "pair", 1).astype(bf16), halve(two, "chips", 0).astype(bf16)]

    def scatter_end(halves):
        if not cube:
            return halves[0]
        return jnp.concatenate([halve(halves[0], "chips", 0), halve(halves[1], "pair", 0)], axis=0)

    def own(a):
        return lax.dynamic_slice(a, (seq, first_row, 0), (1, own_len, model))[0]

    def heads_out(a):
        if split_heads:
            return exchange(a.reshape(n_context, -1, rows))
        m = a.shape[1]
        a = lax.all_gather(a, "seq", axis=0, tiled=True)
        return exchange(a.reshape(n_context, heads * m, rows))

    def heads_spread(a):
        near = spread_near(a)
        return spread_blocks(a, near, spread_far(near))

    def heads_whole(blocks, m):
        a = jnp.stack(blocks).reshape(len(blocks), n_context, heads // len(blocks), m, rows)
        return a.transpose(0, 2, 3, 1, 4).reshape(heads, m, model)

    def heads_split(a):
        a = a.astype(bf16).reshape(seqs, heads // seqs, a.shape[1], n_context, rows)
        return list(a.transpose(0, 3, 1, 2, 4).reshape(seqs, n_context, -1, rows))

    def heads_back(a):
        m = a.shape[1]
        a = a.astype(bf16).reshape(heads, m, n_context, rows).transpose(2, 0, 1, 3)
        a = exchange(a.reshape(n_context, -1, rows)).reshape(seqs * block_heads, m, rows)
        return lax.psum_scatter(a, "seq", scatter_dimension=0, tiled=True).astype(f32)

    gains = lax.all_gather(norm_gains, context, axis=1, tiled=True).astype(f32)
    rows_in = own(block_input).astype(f32)
    incoming = own(cotangent)
    inverse_one = norm_inverse(rows_in)
    normal_one = rows_in * inverse_one
    normed_one = gather_plane((normal_one * gains[0]).astype(bf16))

    qkv_local = qkv_weight.reshape(3, rows, block_heads, HEAD_DIM).transpose(2, 0, 3, 1)
    qkv_block = heads_out(qkv_local.reshape(block_heads, 3 * HEAD_DIM, rows))
    qkv_block, out_local, gateup_local, down_local = lax.optimization_barrier(
        (qkv_block, out_weight, gateup_weight, down_weight)
    )
    out_block = heads_out(out_local.reshape(block_heads, HEAD_DIM, rows))
    qkv_blocks = heads_spread(qkv_block) if split_heads else [qkv_block]
    out_near = spread_near(out_block) if split_heads else []
    qkv_t = heads_whole(qkv_blocks, 3 * HEAD_DIM).reshape(heads, 3, HEAD_DIM, model)
    qkv_t = qkv_t.transpose(1, 0, 2, 3).reshape(3 * width, model)
    gateup_local = gateup_local.reshape(2, rows, n_context, block_hidden).transpose(2, 0, 3, 1)
    hidden_local = jnp.concatenate(
        [
            gateup_local.reshape(n_context, 2 * block_hidden, rows),
            down_local.reshape(n_context, block_hidden, rows),
        ],
        axis=1,
    )
    cosine, sine = rope_tables(length)
    bounds = attention_bounds(lax.dynamic_slice_in_dim(doc_lengths, seq, 1, 0)[0], length)
    normed_one, incoming_now, qkv_t, out_near, hidden_local, cosine, sine, bounds = (
        lax.optimization_barrier(
            (normed_one, incoming, qkv_t, out_near, hidden_local, cosine, sine, bounds)
        )
    )

    incoming_all = gather_plane(incoming_now)
    out_far = spread_far(out_near) if split_heads else []
    score_scale = HEAD_DIM ** (-0.5)
    projected = dot(qkv_t, normed_one, 1, 1)
    q_t = rotate(projected[:width], cosine, sine).astype(bf16) * bf16(score_scale)
    k_t = rotate(projected[width : 2 * width], cosine, sine).astype(bf16)
    v_t = projected[2 * width :].astype(bf16)
    k_h = k_t.reshape(heads, HEAD_DIM, length).transpose(0, 2, 1)
    v_h = v_t.reshape(heads, HEAD_DIM, length).transpose(0, 2, 1)
    q_t, out_far = lax.optimization_barrier((q_t, out_far))
    out_blocks = spread_blocks(out_block, out_near, out_far) if split_heads else [out_block]
    out_full = heads_whole(out_blocks, HEAD_DIM).reshape(width, model)
    hidden_block = exchange(hidden_local)
    o_t, lse, attention_part = attend(bounds, q_t, k_h, v_t, out_full)
    attention_part, incoming_all, hidden_block = lax.optimization_barrier(
        (attention_part, incoming_all, hidden_block)
    )
    hidden_near = spread_near(hidden_block)
    hidden_far = spread_far(hidden_near)
    attention_branch = scatter_plane(attention_part)
    attention_branch, hidden_far = lax.optimization_barrier((attention_branch, hidden_far))
    hidden = rows_in + attention_branch
    inverse_two = norm_inverse(hidden)
    normal_two = hidden * inverse_two
    normed_two = gather_plane((normal_two * gains[1]).astype(bf16))

    hidden_full = jnp.stack(spread_blocks(hidden_block, hidden_near, hidden_far))
    hidden_full = hidden_full.reshape(seqs, n_context, 3, block_hidden, rows)
    hidden_full = hidden_full.transpose(2, 0, 3, 1, 4).reshape(3 * hidden_width, model)
    gateup_t = hidden_full[: 2 * hidden_width]
    down_full = hidden_full[2 * hidden_width :]
    grad_activation = dot(incoming_all, down_full, 1, 1)
    normed_two, grad_activation = lax.optimization_barrier((normed_two, grad_activation))

    gate_up = dot(normed_two, gateup_t, 1, 1)
    gate, raised = gate_up[:, :hidden_width], gate_up[:, hidden_width:]
    gate_sigmoid = jax.nn.sigmoid(gate)
    gate_silu = gate * gate_sigmoid
    activation = (gate_silu * raised).astype(bf16)
    grad_gate = grad_activation * raised * gate_sigmoid * (1.0 + gate * (1.0 - gate_sigmoid))
    grad_up = grad_activation * gate_silu
    grad_gateup = jnp.concatenate([grad_gate, grad_up], axis=1).astype(bf16)
    feedforward_branch = scatter_plane(dot(activation, down_full, 1, 0))
    second_sums = scatter_cores(lambda a: dot(a, gateup_t, 1, 0), grad_gateup)
    down_grad = dot(activation, incoming_all, 0, 0).astype(bf16)
    gateup_grad = dot(grad_gateup, normed_two, 0, 0).astype(bf16)
    hidden_grads = jnp.concatenate(
        [
            gateup_grad.reshape(2, seqs, block_hidden, n_context, rows),
            down_grad.reshape(1, seqs, block_hidden, n_context, rows),
        ],
        axis=0,
    )
    hidden_grads = list(hidden_grads.transpose(1, 3, 0, 2, 4).reshape(seqs, n_context, -1, rows))
    second_sums, hidden_grads = lax.optimization_barrier((second_sums, hidden_grads))
    hidden_grads_far = collect_far(hidden_grads)
    second_halves, hidden_grads_far = lax.optimization_barrier(
        (scatter_middle(second_sums), hidden_grads_far)
    )
    grad_normed_two = scatter_end(second_halves)
    grad_normed_two, feedforward_branch = lax.optimization_barrier(
        (grad_normed_two, feedforward_branch)
    )

    result = (hidden + feedforward_branch).astype(bf16)
    if n_extra > 1:
        result = lax.all_gather(result, "extra", axis=0, tiled=True)
    result_near = spread_near(result)
    grad_rows_two, gain_two = norm_backward(grad_normed_two, normal_two, inverse_two, gains[1])
    grad_hidden = incoming.astype(f32) + grad_rows_two
    grad_hidden_all = gather_plane(grad_hidden.astype(bf16))
    hidden_grads = collect_near(hidden_grads, hidden_grads_far)
    grad_hidden_all, hidden_grads, result_near = lax.optimization_barrier(
        (grad_hidden_all, hidden_grads, result_near)
    )

    result_far = spread_far(result_near)
    grad_projected = attend_back(
        bounds, q_t, grad_hidden_all, o_t, lse, k_h, v_h, k_t, out_full, cosine, sine
    )
    grad_projected, result_far = lax.optimization_barrier((grad_projected, result_far))

    first_part = dot(grad_projected, qkv_t, 1, 0).astype(bf16)
    first_part, grad_projected = lax.optimization_barrier((first_part, grad_projected))
    grad_normed_one = scatter_plane(first_part)
    qkv_grad = dot(grad_projected, normed_one, 0, 0)
    qkv_grad = qkv_grad.reshape(3, heads, HEAD_DIM, model).transpose(1, 0, 2, 3)
    qkv_grad = qkv_grad.reshape(heads, 3 * HEAD_DIM, model)
    out_grad = dot(o_t, grad_hidden_all, 1, 0).reshape(heads, HEAD_DIM, model)
    heads_grad = jnp.concatenate([qkv_grad, out_grad], axis=1)
    heads_grads = heads_split(heads_grad) if split_heads else []
    if split_heads:
        heads_grads = collect_near(heads_grads, collect_far(heads_grads))
    grad_normed_one, heads_grads = lax.optimization_barrier((grad_normed_one, heads_grads))

    grad_rows_one, gain_one = norm_backward(grad_normed_one, normal_one, inverse_one, gains[0])
    grad_input = (grad_hidden + grad_rows_one).astype(bf16)
    input_grad = lax.all_gather(grad_input, ("seq", "extra"), axis=0, tiled=True).astype(f32)
    if split_heads:
        heads_grad = exchange(total(heads_grads).astype(bf16)).astype(f32)
        heads_grad = heads_grad.reshape(block_heads, 4 * HEAD_DIM, rows)
    else:
        heads_grad = heads_back(heads_grad)
    qkv_grad = heads_grad[:, : 3 * HEAD_DIM].reshape(block_heads, 3, HEAD_DIM, rows)
    out_grad = heads_grad[:, 3 * HEAD_DIM :]
    hidden_grad = exchange(total(hidden_grads).astype(bf16)).astype(f32)
    hidden_grad = hidden_grad.reshape(n_context, 3, block_hidden, rows)

    gains_grad = jnp.stack([gain_one, gain_two]).reshape(2, n_context, rows).transpose(1, 0, 2)
    gains_grad = jnp.sum(exchange(gains_grad), axis=0)
    if n_extra > 1:
        gains_grad = lax.psum(gains_grad, "extra")
    gains_near = spread_near(gains_grad)
    gains_grad = jnp.sum(spread_line(gains_grad, gains_near, spread_far(gains_near)), axis=0)
    results = spread_line(result, result_near, result_far)
    return (
        results,
        input_grad.reshape(seqs, local_len, model),
        gains_grad,
        qkv_grad.transpose(1, 3, 0, 2).reshape(qkv_weight.shape),
        out_grad.reshape(out_weight.shape),
        hidden_grad[:, :2].transpose(1, 3, 0, 2).reshape(gateup_weight.shape),
        hidden_grad[:, 2].reshape(down_weight.shape),
    )


def solution(mesh):
    n_context, n_tensor = mesh.shape["context"], mesh.shape["tensor"]
    n_core, n_pair = math.gcd(n_context, 2), math.gcd(n_context, 4) // math.gcd(n_context, 2)
    context, tensor = ("chips", "pair", "core"), ("seq", "extra")

    def program(block_input, *others):
        seqs = block_input.shape[0]
        n_extra = n_tensor // seqs
        assert n_extra * seqs == n_tensor and seqs == 4
        parts = (n_context // (n_pair * n_core), n_pair, n_core, seqs, n_extra)
        split = Mesh(mesh.devices.reshape(parts), (*context, *tensor))
        in_specs = (
            P(None, context, None),
            P(),
            P(None, context),
            P(None, context, tensor),
            P(tensor, context),
            P(None, context, tensor),
            P(tensor, context),
            P(None, context, None),
        )
        out_specs = (
            P(None, context, None),
            P(None, context, None),
            P(None, context),
            P(None, context, tensor),
            P(tensor, context),
            P(None, context, tensor),
            P(tensor, context),
        )
        return jax.shard_map(
            functools.partial(shards, parts),
            mesh=split,
            in_specs=in_specs,
            out_specs=out_specs,
            check_vma=False,
        )(block_input, *others)

    return program
```

```python
import functools
import math

import jax
import jax.numpy as jnp
from jax import lax
from jax.experimental import pallas as pl
from jax.experimental.pallas import tpu as pltpu
from jax.sharding import Mesh
from jax.sharding import PartitionSpec as P

HEAD_DIM = 64
WINDOW = 2048
BLOCK = 512

epsilon = 1e-05
rope_base = 10000.0
masked_fill = -1e30
log2_e = math.log2(math.e)
query_scale = HEAD_DIM ** (-0.5) * log2_e

f32 = jnp.float32
bf16 = jnp.bfloat16
VMEM_BYTES = 56 * 1024 * 1024


def dot(a, b, ca, cb):
    return lax.dot_general(a, b, (((ca,), (cb,)), ((), ())), preferred_element_type=f32)


def visible_block(low_row, q0, k0, q_rows, k_rows):
    key = k0 + lax.broadcasted_iota(jnp.int32, (k_rows, q_rows), 0)
    query = q0 + lax.broadcasted_iota(jnp.int32, (k_rows, q_rows), 1)
    return (key >= low_row) & (key <= query)


def key_loops(lo_ref, full_ref, block, step, carry):
    qb = pl.program_id(0)
    lo = lo_ref[qb]
    full = jnp.minimum(jnp.maximum(full_ref[qb], lo), qb)

    def over(masked, kb, carry):
        return step(masked, pl.multiple_of(kb * block, block), block, 0, carry)

    carry = lax.fori_loop(lo, full, functools.partial(over, True), carry)
    return lax.fori_loop(full, qb, functools.partial(over, False), carry)


def project_kernel(x_ref, weight_ref, cos_ref, sin_ref, q_ref, k_ref, v_ref, kh_ref, vh_ref):
    width = q_ref.shape[0]
    half_dim = HEAD_DIM // 2
    cosine, sine = cos_ref[...], sin_ref[...]
    x = x_ref[...]

    def rotated(v):
        out = []
        for at in range(0, width, HEAD_DIM):
            a, b = v[at : at + half_dim], v[at + half_dim : at + HEAD_DIM]
            out += [a * cosine - b * sine, b * cosine + a * sine]
        return jnp.concatenate(out, axis=0)

    q_ref[...] = (rotated(dot(weight_ref[:width], x, 1, 1)) * query_scale).astype(bf16)
    keys = rotated(dot(weight_ref[width : 2 * width], x, 1, 1))
    values = dot(weight_ref[2 * width :], x, 1, 1)
    k_ref[...] = keys.astype(bf16)
    v_ref[...] = values.astype(bf16)
    keys, values = keys.T.astype(bf16), values.T.astype(bf16)
    for h in range(kh_ref.shape[0]):
        cols = slice(h * HEAD_DIM, (h + 1) * HEAD_DIM)
        kh_ref[h] = keys[:, cols]
        vh_ref[h] = values[:, cols]


def project(x, weight, cosine, sine):
    length, model = x.shape
    width = weight.shape[0] // 3
    heads = width // HEAD_DIM
    block = math.gcd(BLOCK, length)
    tile = pl.BlockSpec((width, block), lambda i: (0, i))
    by_head = pl.BlockSpec((heads, block, HEAD_DIM), lambda i: (0, i, 0))
    table = pl.BlockSpec((HEAD_DIM // 2, block), lambda i: (0, i))
    return pl.pallas_call(
        project_kernel,
        grid=(length // block,),
        out_shape=(
            *(jax.ShapeDtypeStruct((width, length), bf16) for _ in range(3)),
            *(jax.ShapeDtypeStruct((heads, length, HEAD_DIM), bf16) for _ in range(2)),
        ),
        in_specs=[
            pl.BlockSpec((block, model), lambda i: (i, 0)),
            pl.BlockSpec((3 * width, model), lambda i: (0, 0), pipeline_mode=pl.Buffered(1)),
            table,
            table,
        ],
        out_specs=[tile, tile, tile, by_head, by_head],
        compiler_params=pltpu.CompilerParams(vmem_limit_bytes=VMEM_BYTES),
        cost_estimate=pl.CostEstimate(
            flops=6 * length * width * model,
            transcendentals=0,
            bytes_accessed=2 * length * (model + 6 * width),
        ),
        name="project",
    )(x, weight, cosine, sine)


def attend_kernel(
    lo_ref,
    full_ref,
    low_ref,
    q_ref,
    k_ref,
    v_ref,
    out_ref,
    o_ref,
    lse_ref,
    part_ref,
    acc_ref,
):
    heads = range(k_ref.shape[0])
    block = q_ref.shape[1]
    q0 = pl.multiple_of(pl.program_id(0) * block, block)
    rows = [pl.ds(h * HEAD_DIM, HEAD_DIM) for h in heads]
    acc_ref[...] = jnp.zeros_like(acc_ref)

    def step(masked, k0, k_rows, q_from, carry):
        keys, mine = pl.ds(k0, k_rows), slice(q_from, block)
        scores = [dot(k_ref[h, keys, :], q_ref[rows[h], mine], 1, 0) for h in heads]
        if masked:
            visible = visible_block(low_ref[:, mine], q0 + q_from, k0, block - q_from, k_rows)
            scores = [jnp.where(visible, v, masked_fill) for v in scores]
        top = [jnp.maximum(carry[h][0], jnp.max(scores[h], axis=0, keepdims=True)) for h in heads]
        weights = [jnp.exp2(scores[h] - top[h]) for h in heads]
        added = [dot(v_ref[rows[h], keys], weights[h].astype(bf16), 1, 0) for h in heads]
        out = []
        for h in heads:
            fade = jnp.exp2(carry[h][0] - top[h])
            total = carry[h][1] * fade + jnp.sum(weights[h], axis=0, keepdims=True)
            acc_ref[rows[h], mine] = acc_ref[rows[h], mine] * fade + added[h]
            out.append((top[h], total))
        return tuple(out)

    start = tuple(
        (jnp.full((1, block), masked_fill, f32), jnp.zeros((1, block), f32)) for _ in heads
    )
    carry = key_loops(lo_ref, full_ref, block, step, start)
    half = block // 2
    carry = step(True, q0, half, 0, carry)
    later = tuple((top[:, half:], total[:, half:]) for top, total in carry)
    later = step(True, pl.multiple_of(q0 + half, half), half, half, later)
    for h in heads:
        top = jnp.concatenate([carry[h][0][:, :half], later[h][0]], axis=1)
        total = jnp.concatenate([carry[h][1][:, :half], later[h][1]], axis=1)
        o_ref[rows[h], :] = (acc_ref[rows[h], :] / total).astype(bf16)
        lse_ref[h : h + 1, :] = top + jnp.log(total) * log2_e
    attended = o_ref[...]
    for c in range(0, out_ref.shape[1], block):
        cols = pl.ds(c, block)
        part_ref[:, cols] = dot(attended, out_ref[:, cols], 0, 0).astype(bf16)


def attend_back_kernel(
    lo_ref,
    full_ref,
    low_ref,
    q_ref,
    hidden_ref,
    o_ref,
    lse_ref,
    k_ref,
    v_ref,
    kt_ref,
    out_ref,
    cos_ref,
    sin_ref,
    grad_ref,
    g_ref,
    dq_ref,
    dk_ref,
    dv_ref,
):
    heads = range(k_ref.shape[0])
    block = q_ref.shape[1]
    q0 = pl.multiple_of(pl.program_id(0) * block, block)
    width = q_ref.shape[0]
    half_dim = HEAD_DIM // 2
    rows = [pl.ds(h * HEAD_DIM, HEAD_DIM) for h in heads]

    def unrotated(ref, here, cols):
        cosine, sine = cos_ref[:, cols], sin_ref[:, cols]
        out = []
        for h in heads:
            at = h * HEAD_DIM
            a, b = ref[at : at + half_dim, here], ref[at + half_dim : at + HEAD_DIM, here]
            out += [a * cosine + b * sine, b * cosine - a * sine]
        return jnp.concatenate(out, axis=0).T

    @pl.when(pl.program_id(0) == 0)
    def _():
        dk_ref[...] = jnp.zeros_like(dk_ref)
        dv_ref[...] = jnp.zeros_like(dv_ref)

    g_ref[...] = dot(out_ref[...], hidden_ref[...], 1, 1).astype(bf16)
    dq_ref[...] = jnp.zeros_like(dq_ref)
    inner = [
        jnp.sum(g_ref[r, :].astype(f32) * o_ref[r, :].astype(f32), axis=0, keepdims=True)
        for r in rows
    ]

    def step(masked, k0, k_rows, q_from, carry):
        keys, mine = pl.ds(k0, k_rows), slice(q_from, block)
        if masked:
            visible = visible_block(low_ref[:, mine], q0 + q_from, k0, block - q_from, k_rows)
        for h in heads:
            r = rows[h]
            scores = dot(k_ref[h, keys, :], q_ref[r, mine], 1, 0)
            grad_probs = dot(v_ref[h, keys, :], g_ref[r, mine], 1, 0)
            if masked:
                scores = jnp.where(visible, scores, masked_fill)
            probs = jnp.exp2(scores - lse_ref[h : h + 1, mine])
            grad_scores = (probs * (grad_probs - inner[h][:, mine])).astype(bf16)
            dv = dot(g_ref[r, mine], probs.astype(bf16), 1, 1)
            dk = dot(q_ref[r, mine], grad_scores, 1, 1)
            dq = dot(kt_ref[r, keys], grad_scores, 1, 0)
            dv_ref[r, keys] += dv
            dk_ref[r, keys] += dk
            dq_ref[r, mine] += dq
        return carry

    key_loops(lo_ref, full_ref, block, step, 0)
    half = block // 2
    step(True, q0, half, 0, 0)
    step(True, pl.multiple_of(q0 + half, half), half, half, 0)
    here = pl.ds(q0, block)
    dq = unrotated(dq_ref, slice(None), here) * HEAD_DIM ** (-0.5)
    grad_ref[here, 0:width] = dq.astype(bf16)

    @pl.when(pl.program_id(0) == pl.num_programs(0) - 1)
    def _():
        for c in range(0, kt_ref.shape[1], block):
            cols = pl.ds(c, block)
            dk = unrotated(dk_ref, cols, cols) * (1 / log2_e)
            grad_ref[cols, width : 2 * width] = dk.astype(bf16)
            grad_ref[cols, 2 * width : 3 * width] = dv_ref[:, cols].T.astype(bf16)


def attention_specs(heads, length, q_block):
    width = heads * HEAD_DIM
    once = pl.Buffered(1)
    whole_t = pl.BlockSpec((width, length), lambda i, *_: (0, 0), pipeline_mode=once)
    whole_h = pl.BlockSpec((heads, length, HEAD_DIM), lambda i, *_: (0, 0, 0), pipeline_mode=once)
    tile = pl.BlockSpec((width, q_block), lambda i, *_: (0, i))
    low = pl.BlockSpec((1, q_block), lambda i, *_: (0, i))
    stat = pl.BlockSpec((heads, q_block), lambda i, *_: (0, i))
    return whole_t, whole_h, tile, low, stat


def attend(bounds, q_t, k_h, v_t, out_full):
    heads, length, _ = k_h.shape
    width, model = out_full.shape
    block = math.gcd(BLOCK, length)
    whole_t, whole_h, tile, low, stat = attention_specs(heads, length, block)
    pairs = length * WINDOW * heads
    return pl.pallas_call(
        attend_kernel,
        out_shape=(
            jax.ShapeDtypeStruct((width, length), bf16),
            jax.ShapeDtypeStruct((heads, length), f32),
            jax.ShapeDtypeStruct((length, model), bf16),
        ),
        grid_spec=pltpu.PrefetchScalarGridSpec(
            num_scalar_prefetch=2,
            grid=(length // block,),
            in_specs=[
                low,
                tile,
                whole_h,
                whole_t,
                pl.BlockSpec((width, model), lambda i, *_: (0, 0), pipeline_mode=pl.Buffered(1)),
            ],
            out_specs=[tile, stat, pl.BlockSpec((block, model), lambda i, *_: (i, 0))],
            scratch_shapes=[pltpu.VMEM((width, block), f32)],
        ),
        compiler_params=pltpu.CompilerParams(vmem_limit_bytes=VMEM_BYTES),
        cost_estimate=pl.CostEstimate(
            flops=pairs * 6 * 256, transcendentals=pairs, bytes_accessed=length * model * 2
        ),
        name="attend",
    )(*bounds, q_t, k_h, v_t, out_full)


def attend_back(bounds, q_t, grad_hidden, o_t, lse, k_h, v_h, k_t, out_full, cosine, sine):
    heads, length, _ = k_h.shape
    width, model = out_full.shape
    block = math.gcd(BLOCK, length)
    whole_t, whole_h, tile, low, stat = attention_specs(heads, length, block)
    once = pl.Buffered(1)
    table = pl.BlockSpec((HEAD_DIM // 2, length), lambda i, *_: (0, 0), pipeline_mode=once)
    pairs = length * WINDOW * heads
    return pl.pallas_call(
        attend_back_kernel,
        out_shape=jax.ShapeDtypeStruct((length, 3 * width), bf16),
        grid_spec=pltpu.PrefetchScalarGridSpec(
            num_scalar_prefetch=2,
            grid=(length // block,),
            in_specs=[
                low,
                tile,
                pl.BlockSpec((block, model), lambda i, *_: (i, 0)),
                tile,
                stat,
                whole_h,
                whole_h,
                whole_t,
                pl.BlockSpec((width, model), lambda i, *_: (0, 0), pipeline_mode=once),
                table,
                table,
            ],
            out_specs=pl.BlockSpec((length, 3 * width), lambda i, *_: (0, 0)),
            scratch_shapes=[
                pltpu.VMEM((width, block), bf16),
                pltpu.VMEM((width, block), f32),
                pltpu.VMEM((width, length), f32),
                pltpu.VMEM((width, length), f32),
            ],
        ),
        compiler_params=pltpu.CompilerParams(vmem_limit_bytes=VMEM_BYTES),
        cost_estimate=pl.CostEstimate(
            flops=pairs * 12 * 256, transcendentals=pairs, bytes_accessed=length * width * 24
        ),
        name="attend_back",
    )(*bounds, q_t, grad_hidden, o_t, lse, k_h, v_h, k_t, out_full, cosine, sine)


def feedforward_kernel(x_ref, ga_ref, gateup_ref, down_ref, act_ref, grad_ref, branch_ref):
    block, hidden = act_ref.shape
    step = math.gcd(hidden, 256)
    x = x_ref[...]
    for at in range(0, hidden, step):
        cols = slice(at, at + step)
        gate = dot(x, gateup_ref[at : at + step, :], 1, 1)
        raised = dot(x, gateup_ref[hidden + at : hidden + at + step, :], 1, 1)
        grad = ga_ref[:, cols]
        sigmoid = jax.nn.sigmoid(gate)
        silu = gate * sigmoid
        act_ref[:, cols] = (silu * raised).astype(bf16)
        grad_gate = grad * raised * sigmoid * (1.0 + gate * (1.0 - sigmoid))
        grad_ref[:, cols] = grad_gate.astype(bf16)
        grad_ref[:, hidden + at : hidden + at + step] = (grad * silu).astype(bf16)
    act = act_ref[...]
    for at in range(0, branch_ref.shape[1], block):
        cols = slice(at, at + block)
        branch_ref[:, cols] = dot(act, down_ref[:, cols], 1, 0).astype(bf16)


def feedforward(x, ga, gateup, down):
    length, model = x.shape
    hidden = down.shape[0]
    block = math.gcd(BLOCK, length)
    once = pl.Buffered(1)

    def rows_of(width):
        return pl.BlockSpec((block, width), lambda i: (i, 0))

    return pl.pallas_call(
        feedforward_kernel,
        grid=(length // block,),
        out_shape=tuple(
            jax.ShapeDtypeStruct((length, width), bf16) for width in (hidden, 2 * hidden, model)
        ),
        in_specs=[
            rows_of(model),
            rows_of(hidden),
            pl.BlockSpec((2 * hidden, model), lambda i: (0, 0), pipeline_mode=once),
            pl.BlockSpec((hidden, model), lambda i: (0, 0), pipeline_mode=once),
        ],
        out_specs=[rows_of(hidden), rows_of(2 * hidden), rows_of(model)],
        compiler_params=pltpu.CompilerParams(vmem_limit_bytes=VMEM_BYTES),
        cost_estimate=pl.CostEstimate(
            flops=6 * length * hidden * model,
            transcendentals=length * hidden,
            bytes_accessed=length * (4 * model + 10 * hidden),
        ),
        name="feedforward",
    )(x, ga, gateup, down)


def halves_kernel(order_ref, a_ref, b_ref, first_ref, second_ref):
    early = pl.program_id(0) < pl.num_programs(0) // 2

    @pl.when(early)
    def _():
        rows_kernel(a_ref, b_ref, first_ref)

    @pl.when(jnp.logical_not(early))
    def _():
        rows_kernel(a_ref, b_ref, second_ref)


def halves_product(order, a, b):
    length, inner = a.shape
    model = b.shape[1]
    count = order.shape[0]
    half, block = count // 2, length // count
    return pl.pallas_call(
        halves_kernel,
        out_shape=tuple(jax.ShapeDtypeStruct((length // 2, model), bf16) for _ in range(2)),
        grid_spec=pltpu.PrefetchScalarGridSpec(
            num_scalar_prefetch=1,
            grid=(count,),
            in_specs=[
                pl.BlockSpec((block, inner), lambda i, order: (order[i], 0)),
                pl.BlockSpec((inner, model), lambda i, _: (0, 0), pipeline_mode=pl.Buffered(1)),
            ],
            out_specs=[
                pl.BlockSpec((block, model), lambda i, _: (jnp.minimum(i, half - 1), 0)),
                pl.BlockSpec((block, model), lambda i, _: (jnp.maximum(i - half, 0), 0)),
            ],
        ),
        compiler_params=pltpu.CompilerParams(vmem_limit_bytes=VMEM_BYTES),
        cost_estimate=pl.CostEstimate(
            flops=2 * length * inner * model,
            transcendentals=0,
            bytes_accessed=2 * length * (inner + model),
        ),
        name="halves_product",
    )(order, a, b)


def rows_kernel(a_ref, b_ref, o_ref):
    a = a_ref[...]
    block = a_ref.shape[0]
    for at in range(0, o_ref.shape[1], block):
        cols = slice(at, at + block)
        o_ref[:, cols] = dot(a, b_ref[:, cols], 1, 0).astype(bf16)


def rows_product(a, b):
    length, inner = a.shape
    model = b.shape[1]
    block = math.gcd(BLOCK, length)
    return pl.pallas_call(
        rows_kernel,
        grid=(length // block,),
        out_shape=jax.ShapeDtypeStruct((length, model), bf16),
        in_specs=[
            pl.BlockSpec((block, inner), lambda i: (i, 0)),
            pl.BlockSpec((inner, model), lambda i: (0, 0), pipeline_mode=pl.Buffered(1)),
        ],
        out_specs=pl.BlockSpec((block, model), lambda i: (i, 0)),
        compiler_params=pltpu.CompilerParams(vmem_limit_bytes=VMEM_BYTES),
        cost_estimate=pl.CostEstimate(
            flops=2 * length * inner * model,
            transcendentals=0,
            bytes_accessed=2 * length * (inner + model),
        ),
        name="rows_product",
    )(a, b)


def attention_bounds(lengths, length):
    docs = lengths.shape[0]
    upto = jnp.arange(docs)[:, None] >= jnp.arange(docs)[None, :]
    ends = jnp.sum(jnp.where(upto, lengths[None, :], 0), axis=1)
    position = jnp.arange(length, dtype=jnp.int32)
    starts = jnp.max(jnp.where(ends[:, None] <= position[None, :], ends[:, None], 0), axis=0)
    low = jnp.maximum(starts, position - (WINDOW - 1)).astype(jnp.int32)
    block = math.gcd(BLOCK, length)
    by_block = low.reshape(length // block, block)
    first = by_block[:, 0] // block
    full = (by_block[:, -1] + block - 1) // block
    return first, full, low.reshape(1, length)


def rope_tables(length):
    half_dim = HEAD_DIM // 2
    counter = jnp.arange(half_dim, dtype=f32)
    frequency = jnp.exp(counter * (-2.0 * math.log(rope_base) / HEAD_DIM))
    angles = frequency[:, None] * jnp.arange(length, dtype=f32)[None, :]
    return jnp.cos(angles), jnp.sin(angles)


def norm_inverse(rows):
    return lax.rsqrt(jnp.mean(rows * rows, axis=-1, keepdims=True) + epsilon)


def norm_backward(grad_normed, normal, inverse, gain):
    grad_normal = grad_normed * gain
    inner = jnp.mean(grad_normal * normal, axis=-1, keepdims=True)
    return inverse * (grad_normal - normal * inner), jnp.sum(grad_normed * normal, axis=0)


def swap(a, axis):
    return lax.ppermute(a, axis, [(0, 1), (1, 0)])


def halve(a, axis, dim):
    index = lax.axis_index(axis)
    mine = lax.dynamic_index_in_dim(a, index, dim, False)
    other = lax.dynamic_index_in_dim(a, 1 - index, dim, False)
    return mine.astype(f32) + swap(other, axis).astype(f32)


def after(a, *others):
    return lax.optimization_barrier((a, *others))[0]


def shards(
    parts,
    block_input,
    doc_lengths,
    norm_gains,
    qkv_weight,
    out_weight,
    gateup_weight,
    down_weight,
    cotangent,
):
    n_chips, n_pair, n_core, seqs, n_extra = parts
    n_context = n_chips * n_pair * n_core
    context = ("chips", "pair", "core")
    plane = (*context, "extra")
    everyone = (*plane, "seq")
    cube = n_chips == n_pair == n_core == 2 and n_extra == 1
    model = block_input.shape[2]
    local_len = block_input.shape[1]
    length = local_len * n_context
    own_len = local_len // n_extra
    rows = model // n_context
    block_heads = qkv_weight.shape[2] // HEAD_DIM
    heads = seqs * block_heads // n_context
    split_heads = block_heads % n_context == 0
    block_hidden = gateup_weight.shape[2] // n_context
    hidden_width = seqs * block_hidden
    width = heads * HEAD_DIM
    seq = lax.axis_index("seq")
    first_row = lax.axis_index("extra") * own_len

    def exchange(a):
        return lax.all_to_all(a, context, split_axis=0, concat_axis=0, tiled=True)

    def send(a, *pairs):
        return lax.ppermute(a, "seq", pairs)

    def up(a, first=0):
        return send(a, *((i, i + 1) for i in range(first, seqs - 1)))

    def down(a, last=None):
        return send(a, *((i, i - 1) for i in range(1, seqs if last is None else last)))

    def spread_near(a):
        return [up(a), down(a)]

    def spread_far(near):
        across = jnp.where(seq == 1, near[0], near[1])
        return [up(near[0], 1), down(near[1], seqs - 1), send(across, (1, 3), (2, 0))]

    def spread_blocks(a, near, far):
        return [
            a,
            jnp.where(seq == 0, far[2], near[0]),
            jnp.where(seq >= 2, far[0], far[1]),
            jnp.where(seq == seqs - 1, far[2], near[1]),
        ]

    def spread_line(a, near, far):
        line = jnp.stack([far[2], far[0], near[0], a, near[1], far[1], far[2]])
        return lax.dynamic_slice_in_dim(line, seqs - 1 - seq, seqs, 0)

    def collect_far(blocks):
        across = jnp.where(seq == 0, blocks[1], blocks[3])
        return [
            send(blocks[2], *((i, i + 1) for i in range(seqs - 2))),
            send(blocks[2], *((i, i - 1) for i in range(2, seqs))),
            send(across, (0, 2), (3, 1)),
        ]

    def collect_near(blocks, far):
        above = blocks[3].astype(f32) + far[0].astype(f32) + jnp.where(seq == 2, far[2], 0)
        below = blocks[1].astype(f32) + far[1].astype(f32) + jnp.where(seq == 1, far[2], 0)
        return [blocks[0], up(above.astype(bf16)), down(below.astype(bf16))]

    def total(blocks):
        return sum((b.astype(f32) for b in blocks[1:]), blocks[0].astype(f32))

    def gather_plane(a):
        return lax.all_gather(a, plane, axis=0, tiled=True)

    def scatter_plane(a):
        return lax.psum_scatter(a.astype(bf16), plane, scatter_dimension=0, tiled=True).astype(f32)

    def scatter_middle(a):
        if not cube:
            return [scatter_plane(a)]
        half = a.shape[2] // 2
        one, two = a[:, :, :half], a[:, :, half:]
        return [halve(one, "pair", 1).astype(bf16), halve(two, "chips", 0).astype(bf16)]

    def scatter_end(halves):
        if not cube:
            return halves[0]
        return jnp.concatenate([halve(halves[0], "chips", 0), halve(halves[1], "pair", 0)], axis=0)

    def own(a):
        return lax.dynamic_slice(a, (seq, first_row, 0), (1, own_len, model))[0]

    def heads_out(a):
        if split_heads:
            return exchange(a.reshape(n_context, -1, rows))
        m = a.shape[1]
        a = lax.all_gather(a, "seq", axis=0, tiled=True)
        return exchange(a.reshape(n_context, heads * m, rows))

    def heads_spread(a):
        near = spread_near(a)
        return spread_blocks(a, near, spread_far(near))

    def heads_whole(blocks, m):
        a = jnp.stack(blocks).reshape(len(blocks), n_context, heads // len(blocks), m, rows)
        return a.transpose(0, 2, 3, 1, 4).reshape(heads, m, model)

    def heads_split(a):
        a = a.astype(bf16).reshape(seqs, heads // seqs, a.shape[1], n_context, rows)
        return list(a.transpose(0, 3, 1, 2, 4).reshape(seqs, n_context, -1, rows))

    def heads_back(a):
        m = a.shape[1]
        a = a.astype(bf16).reshape(heads, m, n_context, rows).transpose(2, 0, 1, 3)
        a = exchange(a.reshape(n_context, -1, rows)).reshape(seqs * block_heads, m, rows)
        return lax.psum_scatter(a, "seq", scatter_dimension=0, tiled=True).astype(f32)

    rows_in = own(block_input).astype(f32)
    incoming = own(cotangent)
    inverse_one = norm_inverse(rows_in)
    normal_one = rows_in * inverse_one
    normal_own = normal_one.astype(bf16)
    normal_all = gather_plane(normal_own)
    gains = lax.all_gather(after(norm_gains, normal_own), context, axis=1, tiled=True).astype(f32)

    qkv_local, out_local, gains = lax.optimization_barrier((qkv_weight, out_weight, gains))
    heads_local = jnp.concatenate(
        [
            qkv_local.reshape(3, rows, block_heads, HEAD_DIM).transpose(2, 0, 3, 1),
            out_local.reshape(block_heads, 1, HEAD_DIM, rows),
        ],
        axis=1,
    )
    heads_block = heads_out(heads_local.reshape(block_heads, 4 * HEAD_DIM, rows))
    heads_block = heads_block.reshape(n_context, -1, 4, HEAD_DIM, rows)
    qkv_block = heads_block[:, :, :3].reshape(n_context, -1, rows)
    out_block = heads_block[:, :, 3].reshape(n_context, -1, rows)
    qkv_blocks = heads_spread(qkv_block) if split_heads else [qkv_block]
    qkv_blocks, out_block, gateup_local, down_local = lax.optimization_barrier(
        (qkv_blocks, out_block, gateup_weight, down_weight)
    )
    out_near = spread_near(out_block) if split_heads else []
    qkv_t = heads_whole(qkv_blocks, 3 * HEAD_DIM).reshape(heads, 3, HEAD_DIM, model)
    qkv_t = qkv_t.transpose(1, 0, 2, 3).reshape(3 * width, model)
    qkv_gained = (qkv_t.astype(f32) * gains[0]).astype(bf16)
    gateup_local = gateup_local.reshape(2, rows, n_context, block_hidden).transpose(2, 0, 3, 1)
    hidden_local = jnp.concatenate(
        [
            gateup_local.reshape(n_context, 2 * block_hidden, rows),
            down_local.reshape(n_context, block_hidden, rows),
        ],
        axis=1,
    )
    cosine, sine = rope_tables(length)
    bounds = attention_bounds(lax.dynamic_slice_in_dim(doc_lengths, seq, 1, 0)[0], length)
    incoming_all = gather_plane(after(incoming, normal_all, *qkv_blocks))
    normal_all, qkv_t, qkv_gained, out_near, hidden_local, cosine, sine, bounds = (
        lax.optimization_barrier(
            (
                normal_all,
                qkv_t,
                qkv_gained,
                out_near,
                hidden_local,
                cosine,
                sine,
                bounds,
            )
        )
    )

    out_far = spread_far(out_near) if split_heads else []
    q_t, k_t, v_t, k_h, v_h = project(normal_all, qkv_gained, cosine, sine)
    q_t, out_far = lax.optimization_barrier((q_t, out_far))
    out_blocks = spread_blocks(out_block, out_near, out_far) if split_heads else [out_block]
    out_full = heads_whole(out_blocks, HEAD_DIM).reshape(width, model)
    hidden_block = exchange(hidden_local)
    o_t, lse, attention_part = attend(bounds, q_t, k_h, v_t, out_full)
    attention_part, incoming_all, hidden_block = lax.optimization_barrier(
        (attention_part, incoming_all, hidden_block)
    )
    hidden_near = spread_near(hidden_block)
    hidden_far = spread_far(hidden_near)
    attention_branch = scatter_plane(attention_part)
    attention_branch, hidden_far = lax.optimization_barrier((attention_branch, hidden_far))
    hidden = rows_in + attention_branch
    inverse_two = norm_inverse(hidden)
    normal_two = hidden * inverse_two
    normed_two = gather_plane((normal_two * gains[1]).astype(bf16))

    hidden_full = jnp.stack(spread_blocks(hidden_block, hidden_near, hidden_far))
    hidden_full = hidden_full.reshape(seqs, n_context, 3, block_hidden, rows)
    hidden_full = hidden_full.transpose(2, 0, 3, 1, 4).reshape(3 * hidden_width, model)
    gateup_t = hidden_full[: 2 * hidden_width]
    down_full = hidden_full[2 * hidden_width :]
    grad_activation = dot(incoming_all, down_full, 1, 1)
    normed_two, grad_activation = lax.optimization_barrier((normed_two, grad_activation))

    if cube:
        core = lax.axis_index("core")
        pairs = n_core * jnp.arange(n_chips * n_pair, dtype=jnp.int32)
        order = jnp.concatenate([pairs + 1 - core, pairs + core])
    else:
        order = jnp.arange(8, dtype=jnp.int32)
    activation, grad_gateup, feedforward_part = feedforward(
        normed_two, grad_activation, gateup_t, down_full
    )
    theirs, mine = halves_product(order, after(grad_gateup, feedforward_part), gateup_t)
    feedforward_branch = scatter_plane(feedforward_part)
    if cube:
        second_sums = (mine.astype(f32) + swap(theirs, "core").astype(f32)).astype(bf16)
        second_sums = second_sums.reshape(n_chips, n_pair, own_len, model)
    else:
        second_sums = jnp.concatenate([theirs, mine], axis=0)
    down_grad = dot(activation, incoming_all, 0, 0).astype(bf16)
    gateup_grad = dot(grad_gateup, normed_two, 0, 0).astype(bf16)
    hidden_grads = jnp.concatenate(
        [
            gateup_grad.reshape(2, seqs, block_hidden, n_context, rows),
            down_grad.reshape(1, seqs, block_hidden, n_context, rows),
        ],
        axis=0,
    )
    hidden_grads = list(hidden_grads.transpose(1, 3, 0, 2, 4).reshape(seqs, n_context, -1, rows))
    second_sums, hidden_grads = lax.optimization_barrier((second_sums, hidden_grads))
    hidden_grads_far = collect_far(hidden_grads)
    second_halves, hidden_grads_far = lax.optimization_barrier(
        (scatter_middle(second_sums), hidden_grads_far)
    )
    grad_normed_two = scatter_end(second_halves)
    grad_normed_two, feedforward_branch = lax.optimization_barrier(
        (grad_normed_two, feedforward_branch)
    )

    result = (hidden + feedforward_branch).astype(bf16)
    if n_extra > 1:
        result = lax.all_gather(result, "extra", axis=0, tiled=True)
    result_near = spread_near(result)
    grad_rows_two, gain_two = norm_backward(grad_normed_two, normal_two, inverse_two, gains[1])
    grad_hidden = incoming.astype(f32) + grad_rows_two
    grad_hidden_all = gather_plane(grad_hidden.astype(bf16))
    hidden_grads = collect_near(hidden_grads, hidden_grads_far)
    grad_hidden_all, hidden_grads, result_near = lax.optimization_barrier(
        (grad_hidden_all, hidden_grads, result_near)
    )

    result_far = spread_far(result_near)
    grad_projected = attend_back(
        bounds, q_t, grad_hidden_all, o_t, lse, k_h, v_h, k_t, out_full, cosine, sine
    )
    grad_projected, result_far = lax.optimization_barrier((grad_projected, result_far))

    first_part = rows_product(grad_projected, qkv_t)
    first_part, grad_projected = lax.optimization_barrier((first_part, grad_projected))
    grad_normed_one = scatter_plane(first_part)
    qkv_grad = dot(grad_projected, normal_all, 0, 0) * gains[0]
    qkv_grad = qkv_grad.reshape(3, heads, HEAD_DIM, model).transpose(1, 0, 2, 3)
    qkv_grad = qkv_grad.reshape(heads, 3 * HEAD_DIM, model)
    out_grad = dot(o_t, grad_hidden_all, 1, 0).reshape(heads, HEAD_DIM, model)
    heads_grad = jnp.concatenate([qkv_grad, out_grad], axis=1)
    heads_grads = heads_split(heads_grad) if split_heads else []
    if split_heads:
        heads_grads = collect_near(heads_grads, collect_far(heads_grads))
    grad_normed_one, heads_grads = lax.optimization_barrier((grad_normed_one, heads_grads))

    grad_rows_one, gain_one = norm_backward(grad_normed_one, normal_one, inverse_one, gains[0])
    grad_input = (grad_hidden + grad_rows_one).astype(bf16)
    input_grad = lax.all_gather(grad_input, ("seq", "extra"), axis=0, tiled=True).astype(f32)
    if split_heads:
        heads_grad = exchange(total(heads_grads).astype(bf16)).astype(f32)
        heads_grad = heads_grad.reshape(block_heads, 4 * HEAD_DIM, rows)
    else:
        heads_grad = heads_back(heads_grad)
    qkv_grad = heads_grad[:, : 3 * HEAD_DIM].reshape(block_heads, 3, HEAD_DIM, rows)
    out_grad = heads_grad[:, 3 * HEAD_DIM :]
    hidden_grad = exchange(total(hidden_grads).astype(bf16)).astype(f32)
    hidden_grad = hidden_grad.reshape(n_context, 3, block_hidden, rows)

    gains_grad = jnp.stack([gain_one, gain_two]).reshape(2, n_context, rows).transpose(1, 0, 2)
    gains_grad = jnp.sum(exchange(gains_grad), axis=0)
    if n_extra > 1:
        gains_grad = lax.psum(gains_grad, "extra")
    gains_near = spread_near(gains_grad)
    gains_grad = jnp.sum(spread_line(gains_grad, gains_near, spread_far(gains_near)), axis=0)
    results = spread_line(result, result_near, result_far)
    return (
        results,
        input_grad.reshape(seqs, local_len, model),
        gains_grad,
        qkv_grad.transpose(1, 3, 0, 2).reshape(qkv_weight.shape),
        out_grad.reshape(out_weight.shape),
        hidden_grad[:, :2].transpose(1, 3, 0, 2).reshape(gateup_weight.shape),
        hidden_grad[:, 2].reshape(down_weight.shape),
    )


def solution(mesh):
    n_context, n_tensor = mesh.shape["context"], mesh.shape["tensor"]
    n_core, n_pair = math.gcd(n_context, 2), math.gcd(n_context, 4) // math.gcd(n_context, 2)
    context, tensor = ("chips", "pair", "core"), ("seq", "extra")

    def program(block_input, *others):
        seqs = block_input.shape[0]
        n_extra = n_tensor // seqs
        assert n_extra * seqs == n_tensor and seqs == 4
        parts = (n_context // (n_pair * n_core), n_pair, n_core, seqs, n_extra)
        split = Mesh(mesh.devices.reshape(parts), (*context, *tensor))
        in_specs = (
            P(None, context, None),
            P(),
            P(None, context),
            P(None, context, tensor),
            P(tensor, context),
            P(None, context, tensor),
            P(tensor, context),
            P(None, context, None),
        )
        out_specs = (
            P(None, context, None),
            P(None, context, None),
            P(None, context),
            P(None, context, tensor),
            P(tensor, context),
            P(None, context, tensor),
            P(tensor, context),
        )
        return jax.shard_map(
            functools.partial(shards, parts),
            mesh=split,
            in_specs=in_specs,
            out_specs=out_specs,
            check_vma=False,
        )(block_input, *others)

    return program
```

```python
import functools
import math

import jax
import jax.numpy as jnp
from jax import lax
from jax.experimental import pallas as pl
from jax.experimental.pallas import tpu as pltpu
from jax.sharding import Mesh
from jax.sharding import PartitionSpec as P

HEAD_DIM = 64
WINDOW = 2048
BLOCK = 512

epsilon = 1e-05
rope_base = 10000.0
masked_fill = -1e30
log2_e = math.log2(math.e)
query_scale = HEAD_DIM ** (-0.5) * log2_e

f32 = jnp.float32
bf16 = jnp.bfloat16
VMEM_BYTES = 56 * 1024 * 1024


def dot(a, b, ca, cb):
    return lax.dot_general(a, b, (((ca,), (cb,)), ((), ())), preferred_element_type=f32)


def visible_block(low_row, q0, k0, q_rows, k_rows):
    key = k0 + lax.broadcasted_iota(jnp.int32, (k_rows, q_rows), 0)
    query = q0 + lax.broadcasted_iota(jnp.int32, (k_rows, q_rows), 1)
    return (key >= low_row) & (key <= query)


def key_loops(lo_ref, full_ref, block, step, carry):
    qb = pl.program_id(0)
    lo = lo_ref[qb]
    full = jnp.minimum(jnp.maximum(full_ref[qb], lo), qb)

    def over(masked, kb, carry):
        return step(masked, pl.multiple_of(kb * block, block), block, 0, carry)

    carry = lax.fori_loop(lo, full, functools.partial(over, True), carry)
    return lax.fori_loop(full, qb, functools.partial(over, False), carry)


def project_kernel(x_ref, weight_ref, cos_ref, sin_ref, q_ref, k_ref, v_ref, kh_ref, vh_ref):
    width = q_ref.shape[0]
    half_dim = HEAD_DIM // 2
    cosine, sine = cos_ref[...], sin_ref[...]
    x = x_ref[...]

    def rotated(v):
        out = []
        for at in range(0, width, HEAD_DIM):
            a, b = v[at : at + half_dim], v[at + half_dim : at + HEAD_DIM]
            out += [a * cosine - b * sine, b * cosine + a * sine]
        return jnp.concatenate(out, axis=0)

    q_ref[...] = (rotated(dot(weight_ref[:width], x, 1, 1)) * query_scale).astype(bf16)
    keys = rotated(dot(weight_ref[width : 2 * width], x, 1, 1))
    values = dot(weight_ref[2 * width :], x, 1, 1)
    k_ref[...] = keys.astype(bf16)
    v_ref[...] = values.astype(bf16)
    keys, values = keys.T.astype(bf16), values.T.astype(bf16)
    for h in range(kh_ref.shape[0]):
        cols = slice(h * HEAD_DIM, (h + 1) * HEAD_DIM)
        kh_ref[h] = keys[:, cols]
        vh_ref[h] = values[:, cols]


def project(x, weight, cosine, sine):
    length, model = x.shape
    width = weight.shape[0] // 3
    heads = width // HEAD_DIM
    block = math.gcd(BLOCK, length)
    tile = pl.BlockSpec((width, block), lambda i: (0, i))
    by_head = pl.BlockSpec((heads, block, HEAD_DIM), lambda i: (0, i, 0))
    table = pl.BlockSpec((HEAD_DIM // 2, block), lambda i: (0, i))
    return pl.pallas_call(
        project_kernel,
        grid=(length // block,),
        out_shape=(
            *(jax.ShapeDtypeStruct((width, length), bf16) for _ in range(3)),
            *(jax.ShapeDtypeStruct((heads, length, HEAD_DIM), bf16) for _ in range(2)),
        ),
        in_specs=[
            pl.BlockSpec((block, model), lambda i: (i, 0)),
            pl.BlockSpec((3 * width, model), lambda i: (0, 0), pipeline_mode=pl.Buffered(1)),
            table,
            table,
        ],
        out_specs=[tile, tile, tile, by_head, by_head],
        compiler_params=pltpu.CompilerParams(vmem_limit_bytes=VMEM_BYTES),
        cost_estimate=pl.CostEstimate(
            flops=6 * length * width * model,
            transcendentals=0,
            bytes_accessed=2 * length * (model + 6 * width),
        ),
        name="project",
    )(x, weight, cosine, sine)


def attend_kernel(
    lo_ref,
    full_ref,
    low_ref,
    q_ref,
    k_ref,
    v_ref,
    out_ref,
    o_ref,
    lse_ref,
    part_ref,
    acc_ref,
):
    heads = range(k_ref.shape[0])
    block = q_ref.shape[1]
    q0 = pl.multiple_of(pl.program_id(0) * block, block)
    rows = [pl.ds(h * HEAD_DIM, HEAD_DIM) for h in heads]
    acc_ref[...] = jnp.zeros_like(acc_ref)

    def step(masked, k0, k_rows, q_from, carry):
        keys, mine = pl.ds(k0, k_rows), slice(q_from, block)
        scores = [dot(k_ref[h, keys, :], q_ref[rows[h], mine], 1, 0) for h in heads]
        if masked:
            visible = visible_block(low_ref[:, mine], q0 + q_from, k0, block - q_from, k_rows)
            scores = [jnp.where(visible, v, masked_fill) for v in scores]
        top = [jnp.maximum(carry[h][0], jnp.max(scores[h], axis=0, keepdims=True)) for h in heads]
        weights = [jnp.exp2(scores[h] - top[h]) for h in heads]
        added = [dot(v_ref[rows[h], keys], weights[h].astype(bf16), 1, 0) for h in heads]
        out = []
        for h in heads:
            fade = jnp.exp2(carry[h][0] - top[h])
            total = carry[h][1] * fade + jnp.sum(weights[h], axis=0, keepdims=True)
            acc_ref[rows[h], mine] = acc_ref[rows[h], mine] * fade + added[h]
            out.append((top[h], total))
        return tuple(out)

    start = tuple(
        (jnp.full((1, block), masked_fill, f32), jnp.zeros((1, block), f32)) for _ in heads
    )
    carry = key_loops(lo_ref, full_ref, block, step, start)
    half = block // 2
    carry = step(True, q0, half, 0, carry)
    later = tuple((top[:, half:], total[:, half:]) for top, total in carry)
    later = step(True, pl.multiple_of(q0 + half, half), half, half, later)
    for h in heads:
        top = jnp.concatenate([carry[h][0][:, :half], later[h][0]], axis=1)
        total = jnp.concatenate([carry[h][1][:, :half], later[h][1]], axis=1)
        o_ref[rows[h], :] = (acc_ref[rows[h], :] / total).astype(bf16)
        lse_ref[h : h + 1, :] = top + jnp.log(total) * log2_e
    attended = o_ref[...]
    for c in range(0, out_ref.shape[1], block):
        cols = pl.ds(c, block)
        part_ref[:, cols] = dot(attended, out_ref[:, cols], 0, 0).astype(bf16)


def attend_back_kernel(
    lo_ref,
    full_ref,
    low_ref,
    q_ref,
    hidden_ref,
    o_ref,
    lse_ref,
    k_ref,
    v_ref,
    kt_ref,
    out_ref,
    cos_ref,
    sin_ref,
    grad_ref,
    g_ref,
    dq_ref,
    dk_ref,
    dv_ref,
):
    heads = range(k_ref.shape[0])
    block = q_ref.shape[1]
    q0 = pl.multiple_of(pl.program_id(0) * block, block)
    width = q_ref.shape[0]
    half_dim = HEAD_DIM // 2
    rows = [pl.ds(h * HEAD_DIM, HEAD_DIM) for h in heads]

    def unrotated(ref, here, cols):
        cosine, sine = cos_ref[:, cols], sin_ref[:, cols]
        out = []
        for h in heads:
            at = h * HEAD_DIM
            a, b = ref[at : at + half_dim, here], ref[at + half_dim : at + HEAD_DIM, here]
            out += [a * cosine + b * sine, b * cosine - a * sine]
        return jnp.concatenate(out, axis=0).T

    @pl.when(pl.program_id(0) == 0)
    def _():
        dk_ref[...] = jnp.zeros_like(dk_ref)
        dv_ref[...] = jnp.zeros_like(dv_ref)

    g_ref[...] = dot(out_ref[...], hidden_ref[...], 1, 1).astype(bf16)
    dq_ref[...] = jnp.zeros_like(dq_ref)
    inner = [
        jnp.sum(g_ref[r, :].astype(f32) * o_ref[r, :].astype(f32), axis=0, keepdims=True)
        for r in rows
    ]

    def step(masked, k0, k_rows, q_from, carry):
        keys, mine = pl.ds(k0, k_rows), slice(q_from, block)
        if masked:
            visible = visible_block(low_ref[:, mine], q0 + q_from, k0, block - q_from, k_rows)
        for h in heads:
            r = rows[h]
            scores = dot(k_ref[h, keys, :], q_ref[r, mine], 1, 0)
            grad_probs = dot(v_ref[h, keys, :], g_ref[r, mine], 1, 0)
            if masked:
                scores = jnp.where(visible, scores, masked_fill)
            probs = jnp.exp2(scores - lse_ref[h : h + 1, mine])
            grad_scores = (probs * (grad_probs - inner[h][:, mine])).astype(bf16)
            dv = dot(g_ref[r, mine], probs.astype(bf16), 1, 1)
            dk = dot(q_ref[r, mine], grad_scores, 1, 1)
            dq = dot(kt_ref[r, keys], grad_scores, 1, 0)
            dv_ref[r, keys] += dv
            dk_ref[r, keys] += dk
            dq_ref[r, mine] += dq
        return carry

    key_loops(lo_ref, full_ref, block, step, 0)
    half = block // 2
    step(True, q0, half, 0, 0)
    step(True, pl.multiple_of(q0 + half, half), half, half, 0)
    here = pl.ds(q0, block)
    dq = unrotated(dq_ref, slice(None), here) * HEAD_DIM ** (-0.5)
    grad_ref[here, 0:width] = dq.astype(bf16)

    @pl.when(pl.program_id(0) == pl.num_programs(0) - 1)
    def _():
        for c in range(0, kt_ref.shape[1], block):
            cols = pl.ds(c, block)
            dk = unrotated(dk_ref, cols, cols) * (1 / log2_e)
            grad_ref[cols, width : 2 * width] = dk.astype(bf16)
            grad_ref[cols, 2 * width : 3 * width] = dv_ref[:, cols].T.astype(bf16)


def attention_specs(heads, length, q_block):
    width = heads * HEAD_DIM
    once = pl.Buffered(1)
    whole_t = pl.BlockSpec((width, length), lambda i, *_: (0, 0), pipeline_mode=once)
    whole_h = pl.BlockSpec((heads, length, HEAD_DIM), lambda i, *_: (0, 0, 0), pipeline_mode=once)
    tile = pl.BlockSpec((width, q_block), lambda i, *_: (0, i))
    low = pl.BlockSpec((1, q_block), lambda i, *_: (0, i))
    stat = pl.BlockSpec((heads, q_block), lambda i, *_: (0, i))
    return whole_t, whole_h, tile, low, stat


def attend(bounds, q_t, k_h, v_t, out_full):
    heads, length, _ = k_h.shape
    width, model = out_full.shape
    block = math.gcd(BLOCK, length)
    whole_t, whole_h, tile, low, stat = attention_specs(heads, length, block)
    pairs = length * WINDOW * heads
    return pl.pallas_call(
        attend_kernel,
        out_shape=(
            jax.ShapeDtypeStruct((width, length), bf16),
            jax.ShapeDtypeStruct((heads, length), f32),
            jax.ShapeDtypeStruct((length, model), bf16),
        ),
        grid_spec=pltpu.PrefetchScalarGridSpec(
            num_scalar_prefetch=2,
            grid=(length // block,),
            in_specs=[
                low,
                tile,
                whole_h,
                whole_t,
                pl.BlockSpec((width, model), lambda i, *_: (0, 0), pipeline_mode=pl.Buffered(1)),
            ],
            out_specs=[tile, stat, pl.BlockSpec((block, model), lambda i, *_: (i, 0))],
            scratch_shapes=[pltpu.VMEM((width, block), f32)],
        ),
        compiler_params=pltpu.CompilerParams(vmem_limit_bytes=VMEM_BYTES),
        cost_estimate=pl.CostEstimate(
            flops=pairs * 6 * 256, transcendentals=pairs, bytes_accessed=length * model * 2
        ),
        name="attend",
    )(*bounds, q_t, k_h, v_t, out_full)


def attend_back(bounds, q_t, grad_hidden, o_t, lse, k_h, v_h, k_t, out_full, cosine, sine):
    heads, length, _ = k_h.shape
    width, model = out_full.shape
    block = math.gcd(BLOCK, length)
    whole_t, whole_h, tile, low, stat = attention_specs(heads, length, block)
    once = pl.Buffered(1)
    table = pl.BlockSpec((HEAD_DIM // 2, length), lambda i, *_: (0, 0), pipeline_mode=once)
    pairs = length * WINDOW * heads
    return pl.pallas_call(
        attend_back_kernel,
        out_shape=jax.ShapeDtypeStruct((length, 3 * width), bf16),
        grid_spec=pltpu.PrefetchScalarGridSpec(
            num_scalar_prefetch=2,
            grid=(length // block,),
            in_specs=[
                low,
                tile,
                pl.BlockSpec((block, model), lambda i, *_: (i, 0)),
                tile,
                stat,
                whole_h,
                whole_h,
                whole_t,
                pl.BlockSpec((width, model), lambda i, *_: (0, 0), pipeline_mode=once),
                table,
                table,
            ],
            out_specs=pl.BlockSpec((length, 3 * width), lambda i, *_: (0, 0)),
            scratch_shapes=[
                pltpu.VMEM((width, block), bf16),
                pltpu.VMEM((width, block), f32),
                pltpu.VMEM((width, length), f32),
                pltpu.VMEM((width, length), f32),
            ],
        ),
        compiler_params=pltpu.CompilerParams(vmem_limit_bytes=VMEM_BYTES),
        cost_estimate=pl.CostEstimate(
            flops=pairs * 12 * 256, transcendentals=pairs, bytes_accessed=length * width * 24
        ),
        name="attend_back",
    )(*bounds, q_t, grad_hidden, o_t, lse, k_h, v_h, k_t, out_full, cosine, sine)


def feedforward_kernel(x_ref, ga_ref, gateup_ref, down_ref, act_ref, grad_ref, branch_ref):
    block, hidden = act_ref.shape
    step = math.gcd(hidden, 256)
    x = x_ref[...]
    for at in range(0, hidden, step):
        cols = slice(at, at + step)
        gate = dot(x, gateup_ref[at : at + step, :], 1, 1)
        raised = dot(x, gateup_ref[hidden + at : hidden + at + step, :], 1, 1)
        grad = ga_ref[:, cols]
        sigmoid = jax.nn.sigmoid(gate)
        silu = gate * sigmoid
        act_ref[:, cols] = (silu * raised).astype(bf16)
        grad_gate = grad * raised * sigmoid * (1.0 + gate * (1.0 - sigmoid))
        grad_ref[:, cols] = grad_gate.astype(bf16)
        grad_ref[:, hidden + at : hidden + at + step] = (grad * silu).astype(bf16)
    act = act_ref[...]
    for at in range(0, branch_ref.shape[1], block):
        cols = slice(at, at + block)
        branch_ref[:, cols] = dot(act, down_ref[:, cols], 1, 0).astype(bf16)


def feedforward(x, ga, gateup, down):
    length, model = x.shape
    hidden = down.shape[0]
    block = math.gcd(BLOCK, length)
    once = pl.Buffered(1)

    def rows_of(width):
        return pl.BlockSpec((block, width), lambda i: (i, 0))

    return pl.pallas_call(
        feedforward_kernel,
        grid=(length // block,),
        out_shape=tuple(
            jax.ShapeDtypeStruct((length, width), bf16) for width in (hidden, 2 * hidden, model)
        ),
        in_specs=[
            rows_of(model),
            rows_of(hidden),
            pl.BlockSpec((2 * hidden, model), lambda i: (0, 0), pipeline_mode=once),
            pl.BlockSpec((hidden, model), lambda i: (0, 0), pipeline_mode=once),
        ],
        out_specs=[rows_of(hidden), rows_of(2 * hidden), rows_of(model)],
        compiler_params=pltpu.CompilerParams(vmem_limit_bytes=VMEM_BYTES),
        cost_estimate=pl.CostEstimate(
            flops=6 * length * hidden * model,
            transcendentals=length * hidden,
            bytes_accessed=length * (4 * model + 10 * hidden),
        ),
        name="feedforward",
    )(x, ga, gateup, down)


def halves_kernel(order_ref, a_ref, b_ref, first_ref, second_ref):
    early = pl.program_id(0) < pl.num_programs(0) // 2

    @pl.when(early)
    def _():
        rows_kernel(a_ref, b_ref, first_ref)

    @pl.when(jnp.logical_not(early))
    def _():
        rows_kernel(a_ref, b_ref, second_ref)


def halves_product(order, a, b):
    length, inner = a.shape
    model = b.shape[1]
    count = order.shape[0]
    half, block = count // 2, length // count
    return pl.pallas_call(
        halves_kernel,
        out_shape=tuple(jax.ShapeDtypeStruct((length // 2, model), bf16) for _ in range(2)),
        grid_spec=pltpu.PrefetchScalarGridSpec(
            num_scalar_prefetch=1,
            grid=(count,),
            in_specs=[
                pl.BlockSpec((block, inner), lambda i, order: (order[i], 0)),
                pl.BlockSpec((inner, model), lambda i, _: (0, 0), pipeline_mode=pl.Buffered(1)),
            ],
            out_specs=[
                pl.BlockSpec((block, model), lambda i, _: (jnp.minimum(i, half - 1), 0)),
                pl.BlockSpec((block, model), lambda i, _: (jnp.maximum(i - half, 0), 0)),
            ],
        ),
        compiler_params=pltpu.CompilerParams(vmem_limit_bytes=VMEM_BYTES),
        cost_estimate=pl.CostEstimate(
            flops=2 * length * inner * model,
            transcendentals=0,
            bytes_accessed=2 * length * (inner + model),
        ),
        name="halves_product",
    )(order, a, b)


def rows_kernel(a_ref, b_ref, o_ref):
    a = a_ref[...]
    block = a_ref.shape[0]
    for at in range(0, o_ref.shape[1], block):
        cols = slice(at, at + block)
        o_ref[:, cols] = dot(a, b_ref[:, cols], 1, 0).astype(bf16)


def rows_product(a, b):
    length, inner = a.shape
    model = b.shape[1]
    block = math.gcd(BLOCK, length)
    return pl.pallas_call(
        rows_kernel,
        grid=(length // block,),
        out_shape=jax.ShapeDtypeStruct((length, model), bf16),
        in_specs=[
            pl.BlockSpec((block, inner), lambda i: (i, 0)),
            pl.BlockSpec((inner, model), lambda i: (0, 0), pipeline_mode=pl.Buffered(1)),
        ],
        out_specs=pl.BlockSpec((block, model), lambda i: (i, 0)),
        compiler_params=pltpu.CompilerParams(vmem_limit_bytes=VMEM_BYTES),
        cost_estimate=pl.CostEstimate(
            flops=2 * length * inner * model,
            transcendentals=0,
            bytes_accessed=2 * length * (inner + model),
        ),
        name="rows_product",
    )(a, b)


def attention_bounds(lengths, length):
    docs = lengths.shape[0]
    upto = jnp.arange(docs)[:, None] >= jnp.arange(docs)[None, :]
    ends = jnp.sum(jnp.where(upto, lengths[None, :], 0), axis=1)
    position = jnp.arange(length, dtype=jnp.int32)
    starts = jnp.max(jnp.where(ends[:, None] <= position[None, :], ends[:, None], 0), axis=0)
    low = jnp.maximum(starts, position - (WINDOW - 1)).astype(jnp.int32)
    block = math.gcd(BLOCK, length)
    by_block = low.reshape(length // block, block)
    first = by_block[:, 0] // block
    full = (by_block[:, -1] + block - 1) // block
    return first, full, low.reshape(1, length)


def rope_tables(length):
    half_dim = HEAD_DIM // 2
    counter = jnp.arange(half_dim, dtype=f32)
    frequency = jnp.exp(counter * (-2.0 * math.log(rope_base) / HEAD_DIM))
    angles = frequency[:, None] * jnp.arange(length, dtype=f32)[None, :]
    return jnp.cos(angles), jnp.sin(angles)


def norm_inverse(rows):
    return lax.rsqrt(jnp.mean(rows * rows, axis=-1, keepdims=True) + epsilon)


def norm_backward(grad_normed, normal, inverse, gain):
    grad_normal = grad_normed * gain
    inner = jnp.mean(grad_normal * normal, axis=-1, keepdims=True)
    return inverse * (grad_normal - normal * inner), jnp.sum(grad_normed * normal, axis=0)


def swap(a, axis):
    return lax.ppermute(a, axis, [(0, 1), (1, 0)])


def halve(terms, axis, dim):
    def part(index):
        return sum(lax.dynamic_index_in_dim(a, index, dim, False).astype(f32) for a in terms)

    index = lax.axis_index(axis)
    return part(index) + swap(part(1 - index).astype(bf16), axis).astype(f32)


def after(a, *others):
    return lax.optimization_barrier((a, *others))[0]


def shards(
    parts,
    block_input,
    doc_lengths,
    norm_gains,
    qkv_weight,
    out_weight,
    gateup_weight,
    down_weight,
    cotangent,
):
    n_chips, n_pair, n_core, seqs, n_extra = parts
    n_context = n_chips * n_pair * n_core
    context = ("chips", "pair", "core")
    plane = (*context, "extra")
    everyone = (*plane, "seq")
    cube = n_chips == n_pair == n_core == 2 and n_extra == 1
    model = block_input.shape[2]
    local_len = block_input.shape[1]
    length = local_len * n_context
    own_len = local_len // n_extra
    rows = model // n_context
    block_heads = qkv_weight.shape[2] // HEAD_DIM
    heads = seqs * block_heads // n_context
    split_heads = block_heads % n_context == 0
    block_hidden = gateup_weight.shape[2] // n_context
    hidden_width = seqs * block_hidden
    width = heads * HEAD_DIM
    seq = lax.axis_index("seq")
    first_row = lax.axis_index("extra") * own_len

    def exchange(a):
        return lax.all_to_all(a, context, split_axis=0, concat_axis=0, tiled=True)

    def send(a, *pairs):
        return lax.ppermute(a, "seq", pairs)

    def up(a, first=0):
        return send(a, *((i, i + 1) for i in range(first, seqs - 1)))

    def down(a, last=None):
        return send(a, *((i, i - 1) for i in range(1, seqs if last is None else last)))

    def spread_near(a):
        return [up(a), down(a)]

    def spread_far(near):
        across = jnp.where(seq == 1, near[0], near[1])
        return [up(near[0], 1), down(near[1], seqs - 1), send(across, (1, 3), (2, 0))]

    def spread_blocks(a, near, far):
        return [
            a,
            jnp.where(seq == 0, far[2], near[0]),
            jnp.where(seq >= 2, far[0], far[1]),
            jnp.where(seq == seqs - 1, far[2], near[1]),
        ]

    def spread_line(a, near, far):
        line = jnp.stack([far[2], far[0], near[0], a, near[1], far[1], far[2]])
        return lax.dynamic_slice_in_dim(line, seqs - 1 - seq, seqs, 0)

    def collect_far(blocks):
        across = jnp.where(seq == 0, blocks[1], blocks[3])
        return [
            send(blocks[2], *((i, i + 1) for i in range(seqs - 2))),
            send(blocks[2], *((i, i - 1) for i in range(2, seqs))),
            send(across, (0, 2), (3, 1)),
        ]

    def collect_near(blocks, far):
        above = blocks[3].astype(f32) + far[0].astype(f32) + jnp.where(seq == 2, far[2], 0)
        below = blocks[1].astype(f32) + far[1].astype(f32) + jnp.where(seq == 1, far[2], 0)
        return [blocks[0], up(above.astype(bf16)), down(below.astype(bf16))]

    def total(blocks):
        return sum((b.astype(f32) for b in blocks[1:]), blocks[0].astype(f32))

    def gather_plane(a):
        return lax.all_gather(a, plane, axis=0, tiled=True)

    def scatter_plane(a):
        return lax.psum_scatter(a.astype(bf16), plane, scatter_dimension=0, tiled=True).astype(f32)

    def scatter_middle(terms):
        half = own_len // 2
        one, two = [a[:, :, :half] for a in terms], [a[:, :, half:] for a in terms]
        return [halve(one, "pair", 1).astype(bf16), halve(two, "chips", 0).astype(bf16)]

    def scatter_end(halves):
        return jnp.concatenate(
            [halve(halves[:1], "chips", 0), halve(halves[1:], "pair", 0)], axis=0
        )

    def own(a):
        return lax.dynamic_slice(a, (seq, first_row, 0), (1, own_len, model))[0]

    def heads_out(a):
        if split_heads:
            return exchange(a.reshape(n_context, -1, rows))
        m = a.shape[1]
        a = lax.all_gather(a, "seq", axis=0, tiled=True)
        return exchange(a.reshape(n_context, heads * m, rows))

    def heads_whole(blocks, m):
        a = jnp.stack(blocks).reshape(len(blocks), n_context, heads // len(blocks), m, rows)
        return a.transpose(0, 2, 3, 1, 4).reshape(heads, m, model)

    def heads_split(a):
        a = a.astype(bf16).reshape(seqs, heads // seqs, a.shape[1], n_context, rows)
        return list(a.transpose(0, 3, 1, 2, 4).reshape(seqs, n_context, -1, rows))

    def heads_back(a):
        m = a.shape[1]
        a = a.astype(bf16).reshape(heads, m, n_context, rows).transpose(2, 0, 1, 3)
        a = exchange(a.reshape(n_context, -1, rows)).reshape(seqs * block_heads, m, rows)
        return lax.psum_scatter(a, "seq", scatter_dimension=0, tiled=True).astype(f32)

    rows_in = own(block_input).astype(f32)
    incoming = own(cotangent)
    inverse_one = norm_inverse(rows_in)
    normal_one = rows_in * inverse_one
    normal_own = normal_one.astype(bf16)
    normal_all = gather_plane(normal_own)

    qkv_local, out_local, _ = lax.optimization_barrier((qkv_weight, out_weight, normal_own))
    heads_local = jnp.concatenate(
        [
            qkv_local.reshape(3, rows, block_heads, HEAD_DIM).transpose(2, 0, 3, 1),
            out_local.reshape(block_heads, 1, HEAD_DIM, rows),
        ],
        axis=1,
    )
    heads_block = heads_out(heads_local.reshape(block_heads, 4 * HEAD_DIM, rows))
    heads_block = heads_block.reshape(n_context, -1, 4, HEAD_DIM, rows)
    qkv_block = heads_block[:, :, :3].reshape(n_context, -1, rows)
    out_block = heads_block[:, :, 3].reshape(n_context, -1, rows)
    gains_local, gateup_local, down_local, qkv_block, out_block = lax.optimization_barrier(
        (norm_gains, gateup_weight, down_weight, qkv_block, out_block)
    )
    qkv_near = spread_near(qkv_block) if split_heads else []
    gateup_local = gateup_local.reshape(2, rows, n_context, block_hidden).transpose(2, 0, 3, 1)
    hidden_local = jnp.concatenate(
        [
            gateup_local.reshape(n_context, 2 * block_hidden, rows),
            down_local.reshape(n_context, block_hidden, rows),
        ],
        axis=1,
    )
    qkv_near, hidden_local, qkv_block, out_block = lax.optimization_barrier(
        (qkv_near, hidden_local, qkv_block, out_block)
    )
    if split_heads:
        qkv_blocks = spread_blocks(qkv_block, qkv_near, spread_far(qkv_near))
    else:
        qkv_blocks = [qkv_block]
    gains = lax.all_gather(gains_local, context, axis=1, tiled=True).astype(f32)
    out_near = spread_near(out_block) if split_heads else []
    qkv_blocks, out_near, gains = lax.optimization_barrier((qkv_blocks, out_near, gains))
    qkv_t = jnp.stack(qkv_blocks)
    qkv_t = qkv_t.reshape(len(qkv_blocks), n_context, -1, 3, HEAD_DIM, rows)
    qkv_t = qkv_t.transpose(3, 0, 2, 4, 1, 5).reshape(3 * width, model)
    qkv_gained = (qkv_t.astype(f32) * gains[0]).astype(bf16)
    cosine, sine = rope_tables(length)
    bounds = attention_bounds(lax.dynamic_slice_in_dim(doc_lengths, seq, 1, 0)[0], length)
    incoming_all = gather_plane(after(incoming, normal_all, *qkv_blocks))
    normal_all, qkv_t, qkv_gained, out_near, hidden_local, cosine, sine, bounds = (
        lax.optimization_barrier(
            (
                normal_all,
                qkv_t,
                qkv_gained,
                out_near,
                hidden_local,
                cosine,
                sine,
                bounds,
            )
        )
    )

    out_far = spread_far(out_near) if split_heads else []
    q_t, k_t, v_t, k_h, v_h = project(normal_all, qkv_gained, cosine, sine)
    q_t, out_far = lax.optimization_barrier((q_t, out_far))
    out_blocks = spread_blocks(out_block, out_near, out_far) if split_heads else [out_block]
    out_full = heads_whole(out_blocks, HEAD_DIM).reshape(width, model)
    hidden_block = exchange(hidden_local)
    o_t, lse, attention_part = attend(bounds, q_t, k_h, v_t, out_full)
    attention_part, incoming_all, hidden_block = lax.optimization_barrier(
        (attention_part, incoming_all, hidden_block)
    )
    hidden_near = spread_near(hidden_block)
    hidden_far = spread_far(hidden_near)
    attention_branch = scatter_plane(attention_part)
    attention_branch, hidden_far = lax.optimization_barrier((attention_branch, hidden_far))
    hidden = rows_in + attention_branch
    inverse_two = norm_inverse(hidden)
    normal_two = hidden * inverse_two
    normed_two = gather_plane((normal_two * gains[1]).astype(bf16))

    hidden_full = jnp.stack(spread_blocks(hidden_block, hidden_near, hidden_far))
    hidden_full = hidden_full.reshape(seqs, n_context, 3, block_hidden, rows)
    hidden_full = hidden_full.transpose(2, 0, 3, 1, 4).reshape(3 * hidden_width, model)
    gateup_t = hidden_full[: 2 * hidden_width]
    down_full = hidden_full[2 * hidden_width :]
    grad_activation = dot(incoming_all, down_full, 1, 1)
    normed_two, grad_activation = lax.optimization_barrier((normed_two, grad_activation))

    if cube:
        core = lax.axis_index("core")
        pairs = n_core * jnp.arange(n_chips * n_pair, dtype=jnp.int32)
        order = jnp.concatenate([pairs + 1 - core, pairs + core])
    else:
        order = jnp.arange(8, dtype=jnp.int32)
    activation, grad_gateup, feedforward_part = feedforward(
        normed_two, grad_activation, gateup_t, down_full
    )
    theirs, mine = halves_product(order, after(grad_gateup, feedforward_part), gateup_t)
    feedforward_branch = scatter_plane(feedforward_part)
    if cube:
        second_sums = (mine.astype(f32) + swap(theirs, "core").astype(f32)).astype(bf16)
        second_sums = [second_sums.reshape(n_chips, n_pair, own_len, model)]
    else:
        second_sums = [jnp.concatenate([theirs, mine], axis=0)]
    down_grad = dot(activation, incoming_all, 0, 0).astype(bf16)
    gateup_grad = dot(grad_gateup, normed_two, 0, 0).astype(bf16)
    hidden_grads = jnp.concatenate(
        [
            gateup_grad.reshape(2, seqs, block_hidden, n_context, rows),
            down_grad.reshape(1, seqs, block_hidden, n_context, rows),
        ],
        axis=0,
    )
    hidden_grads = list(hidden_grads.transpose(1, 3, 0, 2, 4).reshape(seqs, n_context, -1, rows))
    second_sums, hidden_grads = lax.optimization_barrier((second_sums, hidden_grads))
    hidden_grads_far = collect_far(hidden_grads)
    second_halves, hidden_grads_far = lax.optimization_barrier(
        (scatter_middle(second_sums) if cube else scatter_plane(*second_sums), hidden_grads_far)
    )
    grad_normed_two = scatter_end(second_halves) if cube else second_halves
    grad_normed_two, feedforward_branch = lax.optimization_barrier(
        (grad_normed_two, feedforward_branch)
    )

    result = (hidden + feedforward_branch).astype(bf16)
    if n_extra > 1:
        result = lax.all_gather(result, "extra", axis=0, tiled=True)
    result_near = spread_near(result)
    grad_rows_two, gain_two = norm_backward(grad_normed_two, normal_two, inverse_two, gains[1])
    grad_hidden = incoming.astype(f32) + grad_rows_two
    grad_hidden_all = gather_plane(grad_hidden.astype(bf16))
    hidden_grads = collect_near(hidden_grads, hidden_grads_far)
    grad_hidden_all, hidden_grads, result_near = lax.optimization_barrier(
        (grad_hidden_all, hidden_grads, result_near)
    )

    result_far = spread_far(result_near)
    grad_projected = attend_back(
        bounds, q_t, grad_hidden_all, o_t, lse, k_h, v_h, k_t, out_full, cosine, sine
    )
    grad_projected, result_far = lax.optimization_barrier((grad_projected, result_far))

    first_part = rows_product(grad_projected, qkv_t)
    first_part, grad_projected = lax.optimization_barrier((first_part, grad_projected))
    grad_normed_one = scatter_plane(first_part)
    qkv_grad = dot(grad_projected, normal_all, 0, 0) * gains[0]
    qkv_grad = qkv_grad.reshape(3, heads, HEAD_DIM, model).transpose(1, 0, 2, 3)
    qkv_grad = qkv_grad.reshape(heads, 3 * HEAD_DIM, model)
    out_grad = dot(o_t, grad_hidden_all, 1, 0).reshape(heads, HEAD_DIM, model)
    heads_grad = jnp.concatenate([qkv_grad, out_grad], axis=1)
    heads_grads = heads_split(heads_grad) if split_heads else []
    if split_heads:
        heads_grads = collect_near(heads_grads, collect_far(heads_grads))
    grad_normed_one, heads_grads = lax.optimization_barrier((grad_normed_one, heads_grads))

    grad_rows_one, gain_one = norm_backward(grad_normed_one, normal_one, inverse_one, gains[0])
    grad_input = (grad_hidden + grad_rows_one).astype(bf16)
    input_grad = lax.all_gather(grad_input, ("seq", "extra"), axis=0, tiled=True).astype(f32)
    if split_heads:
        heads_grad = exchange(total(heads_grads).astype(bf16)).astype(f32)
        heads_grad = heads_grad.reshape(block_heads, 4 * HEAD_DIM, rows)
    else:
        heads_grad = heads_back(heads_grad)
    qkv_grad = heads_grad[:, : 3 * HEAD_DIM].reshape(block_heads, 3, HEAD_DIM, rows)
    out_grad = heads_grad[:, 3 * HEAD_DIM :]
    hidden_grad = exchange(total(hidden_grads).astype(bf16)).astype(f32)
    hidden_grad = hidden_grad.reshape(n_context, 3, block_hidden, rows)

    gains_grad = jnp.stack([gain_one, gain_two]).reshape(2, n_context, rows).transpose(1, 0, 2)
    gains_grad = jnp.sum(exchange(gains_grad), axis=0)
    if n_extra > 1:
        gains_grad = lax.psum(gains_grad, "extra")
    gains_near = spread_near(gains_grad)
    gains_grad = jnp.sum(spread_line(gains_grad, gains_near, spread_far(gains_near)), axis=0)
    results = spread_line(result, result_near, result_far)
    return (
        results,
        input_grad.reshape(seqs, local_len, model),
        gains_grad,
        qkv_grad.transpose(1, 3, 0, 2).reshape(qkv_weight.shape),
        out_grad.reshape(out_weight.shape),
        hidden_grad[:, :2].transpose(1, 3, 0, 2).reshape(gateup_weight.shape),
        hidden_grad[:, 2].reshape(down_weight.shape),
    )


def solution(mesh):
    n_context, n_tensor = mesh.shape["context"], mesh.shape["tensor"]
    n_core, n_pair = math.gcd(n_context, 2), math.gcd(n_context, 4) // math.gcd(n_context, 2)
    context, tensor = ("chips", "pair", "core"), ("seq", "extra")

    def program(block_input, *others):
        seqs = block_input.shape[0]
        n_extra = n_tensor // seqs
        assert n_extra * seqs == n_tensor and seqs == 4
        parts = (n_context // (n_pair * n_core), n_pair, n_core, seqs, n_extra)
        split = Mesh(mesh.devices.reshape(parts), (*context, *tensor))
        in_specs = (
            P(None, context, None),
            P(),
            P(None, context),
            P(None, context, tensor),
            P(tensor, context),
            P(None, context, tensor),
            P(tensor, context),
            P(None, context, None),
        )
        out_specs = (
            P(None, context, None),
            P(None, context, None),
            P(None, context),
            P(None, context, tensor),
            P(tensor, context),
            P(None, context, tensor),
            P(tensor, context),
        )
        return jax.shard_map(
            functools.partial(shards, parts),
            mesh=split,
            in_specs=in_specs,
            out_specs=out_specs,
            check_vma=False,
        )(block_input, *others)

    return program
```

```python
import functools
import math

import jax
import jax.numpy as jnp
from jax import lax
from jax.experimental import pallas as pl
from jax.experimental.pallas import tpu as pltpu
from jax.sharding import Mesh
from jax.sharding import PartitionSpec as P

HEAD_DIM = 64
WINDOW = 2048
BLOCK = 512

epsilon = 1e-05
rope_base = 10000.0
masked_fill = -1e30
log2_e = math.log2(math.e)
query_scale = HEAD_DIM ** (-0.5) * log2_e

f32 = jnp.float32
bf16 = jnp.bfloat16
VMEM_BYTES = 56 * 1024 * 1024


def dot(a, b, ca, cb):
    return lax.dot_general(a, b, (((ca,), (cb,)), ((), ())), preferred_element_type=f32)


def visible_block(low_row, q0, k0, q_rows, k_rows):
    key = k0 + lax.broadcasted_iota(jnp.int32, (k_rows, q_rows), 0)
    query = q0 + lax.broadcasted_iota(jnp.int32, (k_rows, q_rows), 1)
    return (key >= low_row) & (key <= query)


def key_loops(lo_ref, full_ref, block, step, carry):
    qb = pl.program_id(0)
    lo = lo_ref[qb]
    full = jnp.minimum(jnp.maximum(full_ref[qb], lo), qb)

    def over(masked, kb, carry):
        return step(masked, pl.multiple_of(kb * block, block), block, 0, carry)

    carry = lax.fori_loop(lo, full, functools.partial(over, True), carry)
    return lax.fori_loop(full, qb, functools.partial(over, False), carry)


def project_kernel(x_ref, weight_ref, cos_ref, sin_ref, q_ref, k_ref, v_ref, kh_ref, vh_ref):
    width = q_ref.shape[0]
    half_dim = HEAD_DIM // 2
    cosine, sine = cos_ref[...], sin_ref[...]
    x = x_ref[...]

    def rotated(v):
        out = []
        for at in range(0, width, HEAD_DIM):
            a, b = v[at : at + half_dim], v[at + half_dim : at + HEAD_DIM]
            out += [a * cosine - b * sine, b * cosine + a * sine]
        return jnp.concatenate(out, axis=0)

    q_ref[...] = (rotated(dot(weight_ref[:width], x, 1, 1)) * query_scale).astype(bf16)
    keys = rotated(dot(weight_ref[width : 2 * width], x, 1, 1))
    values = dot(weight_ref[2 * width :], x, 1, 1)
    k_ref[...] = keys.astype(bf16)
    v_ref[...] = values.astype(bf16)
    keys, values = keys.T.astype(bf16), values.T.astype(bf16)
    for h in range(kh_ref.shape[0]):
        cols = slice(h * HEAD_DIM, (h + 1) * HEAD_DIM)
        kh_ref[h] = keys[:, cols]
        vh_ref[h] = values[:, cols]


def project(x, weight, cosine, sine):
    length, model = x.shape
    width = weight.shape[0] // 3
    heads = width // HEAD_DIM
    block = math.gcd(BLOCK, length)
    tile = pl.BlockSpec((width, block), lambda i: (0, i))
    by_head = pl.BlockSpec((heads, block, HEAD_DIM), lambda i: (0, i, 0))
    table = pl.BlockSpec((HEAD_DIM // 2, block), lambda i: (0, i))
    return pl.pallas_call(
        project_kernel,
        grid=(length // block,),
        out_shape=(
            *(jax.ShapeDtypeStruct((width, length), bf16) for _ in range(3)),
            *(jax.ShapeDtypeStruct((heads, length, HEAD_DIM), bf16) for _ in range(2)),
        ),
        in_specs=[
            pl.BlockSpec((block, model), lambda i: (i, 0)),
            pl.BlockSpec((3 * width, model), lambda i: (0, 0), pipeline_mode=pl.Buffered(1)),
            table,
            table,
        ],
        out_specs=[tile, tile, tile, by_head, by_head],
        compiler_params=pltpu.CompilerParams(vmem_limit_bytes=VMEM_BYTES),
        cost_estimate=pl.CostEstimate(
            flops=6 * length * width * model,
            transcendentals=0,
            bytes_accessed=2 * length * (model + 6 * width),
        ),
        name="project",
    )(x, weight, cosine, sine)


def attend_kernel(
    lo_ref,
    full_ref,
    low_ref,
    q_ref,
    k_ref,
    v_ref,
    out_ref,
    o_ref,
    lse_ref,
    part_ref,
    acc_ref,
):
    heads = range(k_ref.shape[0])
    block = q_ref.shape[1]
    q0 = pl.multiple_of(pl.program_id(0) * block, block)
    rows = [pl.ds(h * HEAD_DIM, HEAD_DIM) for h in heads]
    acc_ref[...] = jnp.zeros_like(acc_ref)

    def step(masked, k0, k_rows, q_from, carry):
        keys, mine = pl.ds(k0, k_rows), slice(q_from, block)
        scores = [dot(k_ref[h, keys, :], q_ref[rows[h], mine], 1, 0) for h in heads]
        if masked:
            visible = visible_block(low_ref[:, mine], q0 + q_from, k0, block - q_from, k_rows)
            scores = [jnp.where(visible, v, masked_fill) for v in scores]
        top = [jnp.maximum(carry[h][0], jnp.max(scores[h], axis=0, keepdims=True)) for h in heads]
        weights = [jnp.exp2(scores[h] - top[h]) for h in heads]
        added = [dot(v_ref[rows[h], keys], weights[h].astype(bf16), 1, 0) for h in heads]
        out = []
        for h in heads:
            fade = jnp.exp2(carry[h][0] - top[h])
            total = carry[h][1] * fade + jnp.sum(weights[h], axis=0, keepdims=True)
            acc_ref[rows[h], mine] = acc_ref[rows[h], mine] * fade + added[h]
            out.append((top[h], total))
        return tuple(out)

    start = tuple(
        (jnp.full((1, block), masked_fill, f32), jnp.zeros((1, block), f32)) for _ in heads
    )
    carry = key_loops(lo_ref, full_ref, block, step, start)
    half = block // 2
    carry = step(True, q0, half, 0, carry)
    later = tuple((top[:, half:], total[:, half:]) for top, total in carry)
    later = step(True, pl.multiple_of(q0 + half, half), half, half, later)
    for h in heads:
        top = jnp.concatenate([carry[h][0][:, :half], later[h][0]], axis=1)
        total = jnp.concatenate([carry[h][1][:, :half], later[h][1]], axis=1)
        o_ref[rows[h], :] = (acc_ref[rows[h], :] / total).astype(bf16)
        lse_ref[h : h + 1, :] = top + jnp.log(total) * log2_e
    attended = o_ref[...]
    for c in range(0, out_ref.shape[1], block):
        cols = pl.ds(c, block)
        part_ref[:, cols] = dot(attended, out_ref[:, cols], 0, 0).astype(bf16)


def attend_back_kernel(
    lo_ref,
    full_ref,
    low_ref,
    q_ref,
    hidden_ref,
    o_ref,
    lse_ref,
    k_ref,
    v_ref,
    kt_ref,
    out_ref,
    cos_ref,
    sin_ref,
    grad_ref,
    g_ref,
    dq_ref,
    dk_ref,
    dv_ref,
):
    heads = range(k_ref.shape[0])
    block = q_ref.shape[1]
    q0 = pl.multiple_of(pl.program_id(0) * block, block)
    width = q_ref.shape[0]
    half_dim = HEAD_DIM // 2
    rows = [pl.ds(h * HEAD_DIM, HEAD_DIM) for h in heads]

    def unrotated(ref, here, cols):
        cosine, sine = cos_ref[:, cols], sin_ref[:, cols]
        out = []
        for h in heads:
            at = h * HEAD_DIM
            a, b = ref[at : at + half_dim, here], ref[at + half_dim : at + HEAD_DIM, here]
            out += [a * cosine + b * sine, b * cosine - a * sine]
        return jnp.concatenate(out, axis=0).T

    @pl.when(pl.program_id(0) == 0)
    def _():
        dk_ref[...] = jnp.zeros_like(dk_ref)
        dv_ref[...] = jnp.zeros_like(dv_ref)

    g_ref[...] = dot(out_ref[...], hidden_ref[...], 1, 1).astype(bf16)
    dq_ref[...] = jnp.zeros_like(dq_ref)
    inner = [
        jnp.sum(g_ref[r, :].astype(f32) * o_ref[r, :].astype(f32), axis=0, keepdims=True)
        for r in rows
    ]

    def step(masked, k0, k_rows, q_from, carry):
        keys, mine = pl.ds(k0, k_rows), slice(q_from, block)
        if masked:
            visible = visible_block(low_ref[:, mine], q0 + q_from, k0, block - q_from, k_rows)
        for h in heads:
            r = rows[h]
            scores = dot(k_ref[h, keys, :], q_ref[r, mine], 1, 0)
            grad_probs = dot(v_ref[h, keys, :], g_ref[r, mine], 1, 0)
            if masked:
                scores = jnp.where(visible, scores, masked_fill)
            probs = jnp.exp2(scores - lse_ref[h : h + 1, mine])
            grad_scores = (probs * (grad_probs - inner[h][:, mine])).astype(bf16)
            dv = dot(g_ref[r, mine], probs.astype(bf16), 1, 1)
            dk = dot(q_ref[r, mine], grad_scores, 1, 1)
            dq = dot(kt_ref[r, keys], grad_scores, 1, 0)
            dv_ref[r, keys] += dv
            dk_ref[r, keys] += dk
            dq_ref[r, mine] += dq
        return carry

    key_loops(lo_ref, full_ref, block, step, 0)
    half = block // 2
    step(True, q0, half, 0, 0)
    step(True, pl.multiple_of(q0 + half, half), half, half, 0)
    here = pl.ds(q0, block)
    dq = unrotated(dq_ref, slice(None), here) * HEAD_DIM ** (-0.5)
    grad_ref[here, 0:width] = dq.astype(bf16)

    @pl.when(pl.program_id(0) == pl.num_programs(0) - 1)
    def _():
        for c in range(0, kt_ref.shape[1], block):
            cols = pl.ds(c, block)
            dk = unrotated(dk_ref, cols, cols) * (1 / log2_e)
            grad_ref[cols, width : 2 * width] = dk.astype(bf16)
            grad_ref[cols, 2 * width : 3 * width] = dv_ref[:, cols].T.astype(bf16)


def attention_specs(heads, length, q_block):
    width = heads * HEAD_DIM
    once = pl.Buffered(1)
    whole_t = pl.BlockSpec((width, length), lambda i, *_: (0, 0), pipeline_mode=once)
    whole_h = pl.BlockSpec((heads, length, HEAD_DIM), lambda i, *_: (0, 0, 0), pipeline_mode=once)
    tile = pl.BlockSpec((width, q_block), lambda i, *_: (0, i))
    low = pl.BlockSpec((1, q_block), lambda i, *_: (0, i))
    stat = pl.BlockSpec((heads, q_block), lambda i, *_: (0, i))
    return whole_t, whole_h, tile, low, stat


def attend(bounds, q_t, k_h, v_t, out_full):
    heads, length, _ = k_h.shape
    width, model = out_full.shape
    block = math.gcd(BLOCK, length)
    whole_t, whole_h, tile, low, stat = attention_specs(heads, length, block)
    pairs = length * WINDOW * heads
    return pl.pallas_call(
        attend_kernel,
        out_shape=(
            jax.ShapeDtypeStruct((width, length), bf16),
            jax.ShapeDtypeStruct((heads, length), f32),
            jax.ShapeDtypeStruct((length, model), bf16),
        ),
        grid_spec=pltpu.PrefetchScalarGridSpec(
            num_scalar_prefetch=2,
            grid=(length // block,),
            in_specs=[
                low,
                tile,
                whole_h,
                whole_t,
                pl.BlockSpec((width, model), lambda i, *_: (0, 0), pipeline_mode=pl.Buffered(1)),
            ],
            out_specs=[tile, stat, pl.BlockSpec((block, model), lambda i, *_: (i, 0))],
            scratch_shapes=[pltpu.VMEM((width, block), f32)],
        ),
        compiler_params=pltpu.CompilerParams(vmem_limit_bytes=VMEM_BYTES),
        cost_estimate=pl.CostEstimate(
            flops=pairs * 6 * 256, transcendentals=pairs, bytes_accessed=length * model * 2
        ),
        name="attend",
    )(*bounds, q_t, k_h, v_t, out_full)


def attend_back(bounds, q_t, grad_hidden, o_t, lse, k_h, v_h, k_t, out_full, cosine, sine):
    heads, length, _ = k_h.shape
    width, model = out_full.shape
    block = math.gcd(BLOCK, length)
    whole_t, whole_h, tile, low, stat = attention_specs(heads, length, block)
    once = pl.Buffered(1)
    table = pl.BlockSpec((HEAD_DIM // 2, length), lambda i, *_: (0, 0), pipeline_mode=once)
    pairs = length * WINDOW * heads
    return pl.pallas_call(
        attend_back_kernel,
        out_shape=jax.ShapeDtypeStruct((length, 3 * width), bf16),
        grid_spec=pltpu.PrefetchScalarGridSpec(
            num_scalar_prefetch=2,
            grid=(length // block,),
            in_specs=[
                low,
                tile,
                pl.BlockSpec((block, model), lambda i, *_: (i, 0)),
                tile,
                stat,
                whole_h,
                whole_h,
                whole_t,
                pl.BlockSpec((width, model), lambda i, *_: (0, 0), pipeline_mode=once),
                table,
                table,
            ],
            out_specs=pl.BlockSpec((length, 3 * width), lambda i, *_: (0, 0)),
            scratch_shapes=[
                pltpu.VMEM((width, block), bf16),
                pltpu.VMEM((width, block), f32),
                pltpu.VMEM((width, length), f32),
                pltpu.VMEM((width, length), f32),
            ],
        ),
        compiler_params=pltpu.CompilerParams(vmem_limit_bytes=VMEM_BYTES),
        cost_estimate=pl.CostEstimate(
            flops=pairs * 12 * 256, transcendentals=pairs, bytes_accessed=length * width * 24
        ),
        name="attend_back",
    )(*bounds, q_t, grad_hidden, o_t, lse, k_h, v_h, k_t, out_full, cosine, sine)


def feedforward_kernel(x_ref, ga_ref, gateup_ref, down_ref, act_ref, grad_ref, branch_ref):
    block, hidden = act_ref.shape
    step = math.gcd(hidden, 256)
    x = x_ref[...]
    for at in range(0, hidden, step):
        cols = slice(at, at + step)
        gate = dot(x, gateup_ref[at : at + step, :], 1, 1)
        raised = dot(x, gateup_ref[hidden + at : hidden + at + step, :], 1, 1)
        grad = ga_ref[:, cols]
        sigmoid = jax.nn.sigmoid(gate)
        silu = gate * sigmoid
        act_ref[:, cols] = (silu * raised).astype(bf16)
        grad_gate = grad * raised * sigmoid * (1.0 + gate * (1.0 - sigmoid))
        grad_ref[:, cols] = grad_gate.astype(bf16)
        grad_ref[:, hidden + at : hidden + at + step] = (grad * silu).astype(bf16)
    act = act_ref[...]
    for at in range(0, branch_ref.shape[1], block):
        cols = slice(at, at + block)
        branch_ref[:, cols] = dot(act, down_ref[:, cols], 1, 0).astype(bf16)


def feedforward(x, ga, gateup, down):
    length, model = x.shape
    hidden = down.shape[0]
    block = math.gcd(BLOCK, length)
    once = pl.Buffered(1)

    def rows_of(width):
        return pl.BlockSpec((block, width), lambda i: (i, 0))

    return pl.pallas_call(
        feedforward_kernel,
        grid=(length // block,),
        out_shape=tuple(
            jax.ShapeDtypeStruct((length, width), bf16) for width in (hidden, 2 * hidden, model)
        ),
        in_specs=[
            rows_of(model),
            rows_of(hidden),
            pl.BlockSpec((2 * hidden, model), lambda i: (0, 0), pipeline_mode=once),
            pl.BlockSpec((hidden, model), lambda i: (0, 0), pipeline_mode=once),
        ],
        out_specs=[rows_of(hidden), rows_of(2 * hidden), rows_of(model)],
        compiler_params=pltpu.CompilerParams(vmem_limit_bytes=VMEM_BYTES),
        cost_estimate=pl.CostEstimate(
            flops=6 * length * hidden * model,
            transcendentals=length * hidden,
            bytes_accessed=length * (4 * model + 10 * hidden),
        ),
        name="feedforward",
    )(x, ga, gateup, down)


def halves_kernel(order_ref, a_ref, b_ref, first_ref, second_ref):
    early = pl.program_id(0) < pl.num_programs(0) // 2

    @pl.when(early)
    def _():
        rows_kernel(a_ref, b_ref, first_ref)

    @pl.when(jnp.logical_not(early))
    def _():
        rows_kernel(a_ref, b_ref, second_ref)


def halves_product(order, a, b):
    length, inner = a.shape
    model = b.shape[1]
    count = order.shape[0]
    half, block = count // 2, length // count
    return pl.pallas_call(
        halves_kernel,
        out_shape=tuple(jax.ShapeDtypeStruct((length // 2, model), bf16) for _ in range(2)),
        grid_spec=pltpu.PrefetchScalarGridSpec(
            num_scalar_prefetch=1,
            grid=(count,),
            in_specs=[
                pl.BlockSpec((block, inner), lambda i, order: (order[i], 0)),
                pl.BlockSpec((inner, model), lambda i, _: (0, 0), pipeline_mode=pl.Buffered(1)),
            ],
            out_specs=[
                pl.BlockSpec((block, model), lambda i, _: (jnp.minimum(i, half - 1), 0)),
                pl.BlockSpec((block, model), lambda i, _: (jnp.maximum(i - half, 0), 0)),
            ],
        ),
        compiler_params=pltpu.CompilerParams(vmem_limit_bytes=VMEM_BYTES),
        cost_estimate=pl.CostEstimate(
            flops=2 * length * inner * model,
            transcendentals=0,
            bytes_accessed=2 * length * (inner + model),
        ),
        name="halves_product",
    )(order, a, b)


def rows_kernel(a_ref, b_ref, o_ref):
    a = a_ref[...]
    block = a_ref.shape[0]
    for at in range(0, o_ref.shape[1], block):
        cols = slice(at, at + block)
        o_ref[:, cols] = dot(a, b_ref[:, cols], 1, 0).astype(bf16)


def rows_product(a, b):
    length, inner = a.shape
    model = b.shape[1]
    block = math.gcd(BLOCK, length)
    return pl.pallas_call(
        rows_kernel,
        grid=(length // block,),
        out_shape=jax.ShapeDtypeStruct((length, model), bf16),
        in_specs=[
            pl.BlockSpec((block, inner), lambda i: (i, 0)),
            pl.BlockSpec((inner, model), lambda i: (0, 0), pipeline_mode=pl.Buffered(1)),
        ],
        out_specs=pl.BlockSpec((block, model), lambda i: (i, 0)),
        compiler_params=pltpu.CompilerParams(vmem_limit_bytes=VMEM_BYTES),
        cost_estimate=pl.CostEstimate(
            flops=2 * length * inner * model,
            transcendentals=0,
            bytes_accessed=2 * length * (inner + model),
        ),
        name="rows_product",
    )(a, b)


def attention_bounds(lengths, length):
    docs = lengths.shape[0]
    upto = jnp.arange(docs)[:, None] >= jnp.arange(docs)[None, :]
    ends = jnp.sum(jnp.where(upto, lengths[None, :], 0), axis=1)
    position = jnp.arange(length, dtype=jnp.int32)
    starts = jnp.max(jnp.where(ends[:, None] <= position[None, :], ends[:, None], 0), axis=0)
    low = jnp.maximum(starts, position - (WINDOW - 1)).astype(jnp.int32)
    block = math.gcd(BLOCK, length)
    by_block = low.reshape(length // block, block)
    first = by_block[:, 0] // block
    full = (by_block[:, -1] + block - 1) // block
    return first, full, low.reshape(1, length)


def rope_tables(length):
    half_dim = HEAD_DIM // 2
    counter = jnp.arange(half_dim, dtype=f32)
    frequency = jnp.exp(counter * (-2.0 * math.log(rope_base) / HEAD_DIM))
    angles = frequency[:, None] * jnp.arange(length, dtype=f32)[None, :]
    return jnp.cos(angles), jnp.sin(angles)


def norm_inverse(rows):
    return lax.rsqrt(jnp.mean(rows * rows, axis=-1, keepdims=True) + epsilon)


def norm_kernel(x_ref, branch_ref, gain_ref, hidden_ref, normed_ref):
    hidden = x_ref[...].astype(f32) + branch_ref[...].astype(f32)
    hidden_ref[...] = hidden
    normed_ref[...] = (hidden * norm_inverse(hidden) * gain_ref[...]).astype(bf16)


def norm_back_kernel(grad_ref, x_ref, base_ref, gain_ref, gain_grad_ref, *out_refs):
    @pl.when(pl.program_id(0) == 0)
    def _():
        gain_grad_ref[...] = jnp.zeros_like(gain_grad_ref)

    x, grad = x_ref[...].astype(f32), grad_ref[...].astype(f32)
    inverse = norm_inverse(x)
    normal = x * inverse
    grad_normal = grad * gain_ref[...]
    inner = jnp.mean(grad_normal * normal, axis=-1, keepdims=True)
    out = base_ref[...].astype(f32) + inverse * (grad_normal - normal * inner)
    for ref in out_refs:
        ref[...] = out.astype(ref.dtype)
    gain_grad_ref[...] += jnp.sum(grad * normal, axis=0, keepdims=True)


def cast_kernel(a_ref, o_ref):
    o_ref[...] = a_ref[...].astype(o_ref.dtype)


def by_rows(kernel, name, arrays, tables, outs, block):
    length, model = arrays[0].shape
    block = math.gcd(block, length)

    def spec(a):
        return pl.BlockSpec((min(block, a.shape[0]), model), lambda i: (i * (a.shape[0] > 1), 0))

    return pl.pallas_call(
        kernel,
        grid=(length // block,),
        out_shape=tuple(outs),
        in_specs=[spec(a) for a in (*arrays, *tables)],
        out_specs=tuple(spec(a) for a in outs),
        compiler_params=pltpu.CompilerParams(vmem_limit_bytes=VMEM_BYTES),
        cost_estimate=pl.CostEstimate(
            flops=8 * length * model, transcendentals=length, bytes_accessed=12 * length * model
        ),
        name=name,
    )(*arrays, *tables)


def add_and_norm(x, branch, gain):
    outs = [jax.ShapeDtypeStruct(x.shape, f32), jax.ShapeDtypeStruct(x.shape, bf16)]
    return by_rows(norm_kernel, "add_and_norm", (x, branch), (gain,), outs, 128)


def norm_backward(grad_normed, x, base, gain, dtypes):
    outs = [jax.ShapeDtypeStruct(gain.shape, f32)]
    outs += [jax.ShapeDtypeStruct(x.shape, dtype) for dtype in dtypes]
    return by_rows(norm_back_kernel, "norm_backward", (grad_normed, x, base), (gain,), outs, 128)


def widen(a):
    return by_rows(cast_kernel, "widen", (a,), (), [jax.ShapeDtypeStruct(a.shape, f32)], 512)[0]


def swap(a, axis):
    return lax.ppermute(a, axis, [(0, 1), (1, 0)])


def halve(terms, axis, dim):
    def part(index):
        return sum(lax.dynamic_index_in_dim(a, index, dim, False).astype(f32) for a in terms)

    index = lax.axis_index(axis)
    return part(index) + swap(part(1 - index).astype(bf16), axis).astype(f32)


def after(a, *others):
    return lax.optimization_barrier((a, *others))[0]


def shards(
    parts,
    block_input,
    doc_lengths,
    norm_gains,
    qkv_weight,
    out_weight,
    gateup_weight,
    down_weight,
    cotangent,
):
    n_chips, n_pair, n_core, seqs, n_extra = parts
    n_context = n_chips * n_pair * n_core
    context = ("chips", "pair", "core")
    plane = (*context, "extra")
    everyone = (*plane, "seq")
    cube = n_chips == n_pair == n_core == 2 and n_extra == 1
    model = block_input.shape[2]
    local_len = block_input.shape[1]
    length = local_len * n_context
    own_len = local_len // n_extra
    rows = model // n_context
    block_heads = qkv_weight.shape[2] // HEAD_DIM
    heads = seqs * block_heads // n_context
    split_heads = block_heads % n_context == 0
    block_hidden = gateup_weight.shape[2] // n_context
    hidden_width = seqs * block_hidden
    width = heads * HEAD_DIM
    seq = lax.axis_index("seq")
    first_row = lax.axis_index("extra") * own_len

    def exchange(a):
        return lax.all_to_all(a, context, split_axis=0, concat_axis=0, tiled=True)

    def send(a, *pairs):
        return lax.ppermute(a, "seq", pairs)

    def up(a, first=0):
        return send(a, *((i, i + 1) for i in range(first, seqs - 1)))

    def down(a, last=None):
        return send(a, *((i, i - 1) for i in range(1, seqs if last is None else last)))

    def spread_near(a):
        return [up(a), down(a)]

    def spread_far(near):
        across = jnp.where(seq == 1, near[0], near[1])
        return [up(near[0], 1), down(near[1], seqs - 1), send(across, (1, 3), (2, 0))]

    def spread_blocks(a, near, far):
        return [
            a,
            jnp.where(seq == 0, far[2], near[0]),
            jnp.where(seq >= 2, far[0], far[1]),
            jnp.where(seq == seqs - 1, far[2], near[1]),
        ]

    def spread_line(a, near, far):
        line = jnp.stack([far[2], far[0], near[0], a, near[1], far[1], far[2]])
        return lax.dynamic_slice_in_dim(line, seqs - 1 - seq, seqs, 0)

    def collect_far(blocks):
        across = jnp.where(seq == 0, blocks[1], blocks[3])
        return [
            send(blocks[2], *((i, i + 1) for i in range(seqs - 2))),
            send(blocks[2], *((i, i - 1) for i in range(2, seqs))),
            send(across, (0, 2), (3, 1)),
        ]

    def collect_near(blocks, far):
        above = blocks[3].astype(f32) + far[0].astype(f32) + jnp.where(seq == 2, far[2], 0)
        below = blocks[1].astype(f32) + far[1].astype(f32) + jnp.where(seq == 1, far[2], 0)
        return [blocks[0], up(above.astype(bf16)), down(below.astype(bf16))]

    def total(blocks):
        return sum((b.astype(f32) for b in blocks[1:]), blocks[0].astype(f32))

    def gather_plane(a):
        return lax.all_gather(a, plane, axis=0, tiled=True)

    def scatter_plane(a):
        return lax.psum_scatter(a.astype(bf16), plane, scatter_dimension=0, tiled=True)

    def scatter_middle(terms):
        half = own_len // 2
        one, two = [a[:, :, :half] for a in terms], [a[:, :, half:] for a in terms]
        return [halve(one, "pair", 1).astype(bf16), halve(two, "chips", 0).astype(bf16)]

    def scatter_end(halves):
        return jnp.concatenate(
            [halve(halves[:1], "chips", 0), halve(halves[1:], "pair", 0)], axis=0
        )

    def own(a):
        return lax.dynamic_slice(a, (seq, first_row, 0), (1, own_len, model))[0]

    def heads_out(a):
        if split_heads:
            return exchange(a.reshape(n_context, -1, rows))
        m = a.shape[1]
        a = lax.all_gather(a, "seq", axis=0, tiled=True)
        return exchange(a.reshape(n_context, heads * m, rows))

    def heads_whole(blocks, m):
        a = jnp.stack(blocks).reshape(len(blocks), n_context, heads // len(blocks), m, rows)
        return a.transpose(0, 2, 3, 1, 4).reshape(heads, m, model)

    def heads_split(a):
        a = a.astype(bf16).reshape(seqs, heads // seqs, a.shape[1], n_context, rows)
        return list(a.transpose(0, 3, 1, 2, 4).reshape(seqs, n_context, -1, rows))

    def heads_back(a):
        m = a.shape[1]
        a = a.astype(bf16).reshape(heads, m, n_context, rows).transpose(2, 0, 1, 3)
        a = exchange(a.reshape(n_context, -1, rows)).reshape(seqs * block_heads, m, rows)
        return lax.psum_scatter(a, "seq", scatter_dimension=0, tiled=True).astype(f32)

    rows_in = own(block_input)
    incoming = own(cotangent)
    wide = rows_in.astype(f32)
    normal_own = (wide * norm_inverse(wide)).astype(bf16)
    normal_all = gather_plane(normal_own)

    qkv_local, out_local, _ = lax.optimization_barrier((qkv_weight, out_weight, normal_own))
    heads_local = jnp.concatenate(
        [
            qkv_local.reshape(3, rows, block_heads, HEAD_DIM).transpose(2, 0, 3, 1),
            out_local.reshape(block_heads, 1, HEAD_DIM, rows),
        ],
        axis=1,
    )
    heads_block = heads_out(heads_local.reshape(block_heads, 4 * HEAD_DIM, rows))
    heads_block = heads_block.reshape(n_context, -1, 4, HEAD_DIM, rows)
    qkv_block = heads_block[:, :, :3].reshape(n_context, -1, rows)
    out_block = heads_block[:, :, 3].reshape(n_context, -1, rows)
    gains_local, gateup_local, down_local, qkv_block, out_block = lax.optimization_barrier(
        (norm_gains, gateup_weight, down_weight, qkv_block, out_block)
    )
    qkv_near = spread_near(qkv_block) if split_heads else []
    gateup_local = gateup_local.reshape(2, rows, n_context, block_hidden).transpose(2, 0, 3, 1)
    hidden_local = jnp.concatenate(
        [
            gateup_local.reshape(n_context, 2 * block_hidden, rows),
            down_local.reshape(n_context, block_hidden, rows),
        ],
        axis=1,
    )
    qkv_near, hidden_local, qkv_block, out_block = lax.optimization_barrier(
        (qkv_near, hidden_local, qkv_block, out_block)
    )
    if split_heads:
        qkv_blocks = spread_blocks(qkv_block, qkv_near, spread_far(qkv_near))
    else:
        qkv_blocks = [qkv_block]
    gains = lax.all_gather(gains_local, context, axis=1, tiled=True).astype(f32)
    out_near = spread_near(out_block) if split_heads else []
    qkv_blocks, out_near, gains = lax.optimization_barrier((qkv_blocks, out_near, gains))
    qkv_t = jnp.stack(qkv_blocks)
    qkv_t = qkv_t.reshape(len(qkv_blocks), n_context, -1, 3, HEAD_DIM, rows)
    qkv_t = qkv_t.transpose(3, 0, 2, 4, 1, 5).reshape(3 * width, model)
    qkv_gained = (qkv_t.astype(f32) * gains[0]).astype(bf16)
    cosine, sine = rope_tables(length)
    bounds = attention_bounds(lax.dynamic_slice_in_dim(doc_lengths, seq, 1, 0)[0], length)
    incoming_all = gather_plane(after(incoming, normal_all, *qkv_blocks))
    normal_all, qkv_t, qkv_gained, out_near, hidden_local, cosine, sine, bounds = (
        lax.optimization_barrier(
            (
                normal_all,
                qkv_t,
                qkv_gained,
                out_near,
                hidden_local,
                cosine,
                sine,
                bounds,
            )
        )
    )

    out_far = spread_far(out_near) if split_heads else []
    q_t, k_t, v_t, k_h, v_h = project(normal_all, qkv_gained, cosine, sine)
    q_t, out_far = lax.optimization_barrier((q_t, out_far))
    out_blocks = spread_blocks(out_block, out_near, out_far) if split_heads else [out_block]
    out_full = heads_whole(out_blocks, HEAD_DIM).reshape(width, model)
    hidden_block = exchange(hidden_local)
    o_t, lse, attention_part = attend(bounds, q_t, k_h, v_t, out_full)
    attention_part, incoming_all, hidden_block = lax.optimization_barrier(
        (attention_part, incoming_all, hidden_block)
    )
    hidden_near = spread_near(hidden_block)
    hidden_far = spread_far(hidden_near)
    attention_branch = scatter_plane(attention_part)
    attention_branch, hidden_far = lax.optimization_barrier((attention_branch, hidden_far))
    hidden, normed_own = add_and_norm(rows_in, attention_branch, gains[1:2])
    normed_two = gather_plane(normed_own)

    hidden_full = jnp.stack(spread_blocks(hidden_block, hidden_near, hidden_far))
    hidden_full = hidden_full.reshape(seqs, n_context, 3, block_hidden, rows)
    hidden_full = hidden_full.transpose(2, 0, 3, 1, 4).reshape(3 * hidden_width, model)
    gateup_t = hidden_full[: 2 * hidden_width]
    down_full = hidden_full[2 * hidden_width :]
    grad_activation = dot(incoming_all, down_full, 1, 1)
    normed_two, grad_activation = lax.optimization_barrier((normed_two, grad_activation))

    if cube:
        core = lax.axis_index("core")
        pairs = n_core * jnp.arange(n_chips * n_pair, dtype=jnp.int32)
        order = jnp.concatenate([pairs + 1 - core, pairs + core])
    else:
        order = jnp.arange(8, dtype=jnp.int32)
    activation, grad_gateup, feedforward_part = feedforward(
        normed_two, grad_activation, gateup_t, down_full
    )
    theirs, mine = halves_product(order, after(grad_gateup, feedforward_part), gateup_t)
    feedforward_branch = scatter_plane(feedforward_part)
    if cube:
        second_sums = (mine.astype(f32) + swap(theirs, "core").astype(f32)).astype(bf16)
        second_sums = [second_sums.reshape(n_chips, n_pair, own_len, model)]
    else:
        second_sums = [jnp.concatenate([theirs, mine], axis=0)]
    down_grad = dot(activation, incoming_all, 0, 0).astype(bf16)
    gateup_grad = dot(grad_gateup, normed_two, 0, 0).astype(bf16)
    hidden_grads = jnp.concatenate(
        [
            gateup_grad.reshape(2, seqs, block_hidden, n_context, rows),
            down_grad.reshape(1, seqs, block_hidden, n_context, rows),
        ],
        axis=0,
    )
    hidden_grads = list(hidden_grads.transpose(1, 3, 0, 2, 4).reshape(seqs, n_context, -1, rows))
    second_sums, hidden_grads = lax.optimization_barrier((second_sums, hidden_grads))
    hidden_grads_far = collect_far(hidden_grads)
    second_halves, hidden_grads_far = lax.optimization_barrier(
        (scatter_middle(second_sums) if cube else scatter_plane(*second_sums), hidden_grads_far)
    )
    grad_normed_two = scatter_end(second_halves) if cube else second_halves
    grad_normed_two, feedforward_branch = lax.optimization_barrier(
        (grad_normed_two, feedforward_branch)
    )

    result = (hidden + feedforward_branch.astype(f32)).astype(bf16)
    if n_extra > 1:
        result = lax.all_gather(result, "extra", axis=0, tiled=True)
    result_near = spread_near(result)
    gain_two, grad_hidden, grad_hidden_low = norm_backward(
        grad_normed_two, hidden, incoming, gains[1:2], (f32, bf16)
    )
    grad_hidden_all = gather_plane(grad_hidden_low)
    hidden_grads = collect_near(hidden_grads, hidden_grads_far)
    grad_hidden_all, hidden_grads, result_near = lax.optimization_barrier(
        (grad_hidden_all, hidden_grads, result_near)
    )

    result_far = spread_far(result_near)
    grad_projected = attend_back(
        bounds, q_t, grad_hidden_all, o_t, lse, k_h, v_h, k_t, out_full, cosine, sine
    )
    grad_projected, result_far = lax.optimization_barrier((grad_projected, result_far))

    first_part = rows_product(grad_projected, qkv_t)
    first_part, grad_projected = lax.optimization_barrier((first_part, grad_projected))
    grad_normed_one = scatter_plane(first_part)
    qkv_grad = dot(grad_projected, normal_all, 0, 0) * gains[0]
    qkv_grad = qkv_grad.reshape(3, heads, HEAD_DIM, model).transpose(1, 0, 2, 3)
    qkv_grad = qkv_grad.reshape(heads, 3 * HEAD_DIM, model)
    out_grad = dot(o_t, grad_hidden_all, 1, 0).reshape(heads, HEAD_DIM, model)
    heads_grad = jnp.concatenate([qkv_grad, out_grad], axis=1)
    heads_grads = heads_split(heads_grad) if split_heads else []
    if split_heads:
        heads_grads = collect_near(heads_grads, collect_far(heads_grads))
    grad_normed_one, heads_grads = lax.optimization_barrier((grad_normed_one, heads_grads))

    gain_one, grad_input = norm_backward(
        grad_normed_one, rows_in, grad_hidden, gains[0:1], (bf16,)
    )
    input_grad = widen(lax.all_gather(grad_input, ("seq", "extra"), axis=0, tiled=True))
    if split_heads:
        heads_grad = exchange(total(heads_grads).astype(bf16)).astype(f32)
        heads_grad = heads_grad.reshape(block_heads, 4 * HEAD_DIM, rows)
    else:
        heads_grad = heads_back(heads_grad)
    qkv_grad = heads_grad[:, : 3 * HEAD_DIM].reshape(block_heads, 3, HEAD_DIM, rows)
    out_grad = heads_grad[:, 3 * HEAD_DIM :]
    hidden_grad = exchange(total(hidden_grads).astype(bf16)).astype(f32)
    hidden_grad = hidden_grad.reshape(n_context, 3, block_hidden, rows)

    gains_grad = jnp.stack([gain_one, gain_two]).reshape(2, n_context, rows).transpose(1, 0, 2)
    gains_grad = jnp.sum(exchange(gains_grad), axis=0)
    if n_extra > 1:
        gains_grad = lax.psum(gains_grad, "extra")
    gains_near = spread_near(gains_grad)
    gains_grad = jnp.sum(spread_line(gains_grad, gains_near, spread_far(gains_near)), axis=0)
    results = spread_line(result, result_near, result_far)
    return (
        results,
        input_grad.reshape(seqs, local_len, model),
        gains_grad,
        qkv_grad.transpose(1, 3, 0, 2).reshape(qkv_weight.shape),
        out_grad.reshape(out_weight.shape),
        hidden_grad[:, :2].transpose(1, 3, 0, 2).reshape(gateup_weight.shape),
        hidden_grad[:, 2].reshape(down_weight.shape),
    )


def solution(mesh):
    n_context, n_tensor = mesh.shape["context"], mesh.shape["tensor"]
    n_core, n_pair = math.gcd(n_context, 2), math.gcd(n_context, 4) // math.gcd(n_context, 2)
    context, tensor = ("chips", "pair", "core"), ("seq", "extra")

    def program(block_input, *others):
        seqs = block_input.shape[0]
        n_extra = n_tensor // seqs
        assert n_extra * seqs == n_tensor and seqs == 4
        parts = (n_context // (n_pair * n_core), n_pair, n_core, seqs, n_extra)
        split = Mesh(mesh.devices.reshape(parts), (*context, *tensor))
        in_specs = (
            P(None, context, None),
            P(),
            P(None, context),
            P(None, context, tensor),
            P(tensor, context),
            P(None, context, tensor),
            P(tensor, context),
            P(None, context, None),
        )
        out_specs = (
            P(None, context, None),
            P(None, context, None),
            P(None, context),
            P(None, context, tensor),
            P(tensor, context),
            P(None, context, tensor),
            P(tensor, context),
        )
        return jax.shard_map(
            functools.partial(shards, parts),
            mesh=split,
            in_specs=in_specs,
            out_specs=out_specs,
            check_vma=False,
        )(block_input, *others)

    return program
```

```python
import functools
import math

import jax
import jax.numpy as jnp
from jax import lax
from jax.experimental import pallas as pl
from jax.experimental.pallas import tpu as pltpu
from jax.sharding import Mesh
from jax.sharding import PartitionSpec as P

HEAD_DIM = 64
WINDOW = 2048
BLOCK = 512

epsilon = 1e-05
rope_base = 10000.0
masked_fill = -1e30
log2_e = math.log2(math.e)
query_scale = HEAD_DIM ** (-0.5) * log2_e

f32 = jnp.float32
bf16 = jnp.bfloat16
VMEM_BYTES = 56 * 1024 * 1024


def dot(a, b, ca, cb):
    return lax.dot_general(a, b, (((ca,), (cb,)), ((), ())), preferred_element_type=f32)


def visible_block(low_row, q0, k0, q_rows, k_rows):
    key = k0 + lax.broadcasted_iota(jnp.int32, (k_rows, q_rows), 0)
    query = q0 + lax.broadcasted_iota(jnp.int32, (k_rows, q_rows), 1)
    return (key >= low_row) & (key <= query)


def key_loops(lo_ref, full_ref, block, step, carry):
    qb = pl.program_id(0)
    lo = lo_ref[qb]
    full = jnp.minimum(jnp.maximum(full_ref[qb], lo), qb)

    def over(masked, kb, carry):
        return step(masked, pl.multiple_of(kb * block, block), block, 0, carry)

    carry = lax.fori_loop(lo, full, functools.partial(over, True), carry)
    return lax.fori_loop(full, qb, functools.partial(over, False), carry)


def project_kernel(x_ref, weight_ref, cos_ref, sin_ref, q_ref, k_ref, v_ref, kh_ref, vh_ref):
    width = q_ref.shape[0]
    half_dim = HEAD_DIM // 2
    cosine, sine = cos_ref[...], sin_ref[...]
    x = x_ref[...]

    def rotated(v):
        out = []
        for at in range(0, width, HEAD_DIM):
            a, b = v[at : at + half_dim], v[at + half_dim : at + HEAD_DIM]
            out += [a * cosine - b * sine, b * cosine + a * sine]
        return jnp.concatenate(out, axis=0)

    q_ref[...] = (rotated(dot(weight_ref[:width], x, 1, 1)) * query_scale).astype(bf16)
    keys = rotated(dot(weight_ref[width : 2 * width], x, 1, 1))
    values = dot(weight_ref[2 * width :], x, 1, 1)
    k_ref[...] = keys.astype(bf16)
    v_ref[...] = values.astype(bf16)
    keys, values = keys.T.astype(bf16), values.T.astype(bf16)
    for h in range(kh_ref.shape[0]):
        cols = slice(h * HEAD_DIM, (h + 1) * HEAD_DIM)
        kh_ref[h] = keys[:, cols]
        vh_ref[h] = values[:, cols]


def project(x, weight, cosine, sine):
    length, model = x.shape
    width = weight.shape[0] // 3
    heads = width // HEAD_DIM
    block = math.gcd(BLOCK, length)
    tile = pl.BlockSpec((width, block), lambda i: (0, i))
    by_head = pl.BlockSpec((heads, block, HEAD_DIM), lambda i: (0, i, 0))
    table = pl.BlockSpec((HEAD_DIM // 2, block), lambda i: (0, i))
    return pl.pallas_call(
        project_kernel,
        grid=(length // block,),
        out_shape=(
            *(jax.ShapeDtypeStruct((width, length), bf16) for _ in range(3)),
            *(jax.ShapeDtypeStruct((heads, length, HEAD_DIM), bf16) for _ in range(2)),
        ),
        in_specs=[
            pl.BlockSpec((block, model), lambda i: (i, 0)),
            pl.BlockSpec((3 * width, model), lambda i: (0, 0), pipeline_mode=pl.Buffered(1)),
            table,
            table,
        ],
        out_specs=[tile, tile, tile, by_head, by_head],
        compiler_params=pltpu.CompilerParams(vmem_limit_bytes=VMEM_BYTES),
        cost_estimate=pl.CostEstimate(
            flops=6 * length * width * model,
            transcendentals=0,
            bytes_accessed=2 * length * (model + 6 * width),
        ),
        name="project",
    )(x, weight, cosine, sine)


def attend_kernel(
    lo_ref,
    full_ref,
    low_ref,
    q_ref,
    k_ref,
    v_ref,
    out_ref,
    o_ref,
    lse_ref,
    part_ref,
    acc_ref,
):
    heads = range(k_ref.shape[0])
    block = q_ref.shape[1]
    q0 = pl.multiple_of(pl.program_id(0) * block, block)
    rows = [pl.ds(h * HEAD_DIM, HEAD_DIM) for h in heads]
    acc_ref[...] = jnp.zeros_like(acc_ref)

    def step(masked, k0, k_rows, q_from, carry):
        keys, mine = pl.ds(k0, k_rows), slice(q_from, block)
        scores = [dot(k_ref[h, keys, :], q_ref[rows[h], mine], 1, 0) for h in heads]
        if masked:
            visible = visible_block(low_ref[:, mine], q0 + q_from, k0, block - q_from, k_rows)
            scores = [jnp.where(visible, v, masked_fill) for v in scores]
        top = [jnp.maximum(carry[h][0], jnp.max(scores[h], axis=0, keepdims=True)) for h in heads]
        weights = [jnp.exp2(scores[h] - top[h]) for h in heads]
        added = [dot(v_ref[rows[h], keys], weights[h].astype(bf16), 1, 0) for h in heads]
        out = []
        for h in heads:
            fade = jnp.exp2(carry[h][0] - top[h])
            total = carry[h][1] * fade + jnp.sum(weights[h], axis=0, keepdims=True)
            acc_ref[rows[h], mine] = acc_ref[rows[h], mine] * fade + added[h]
            out.append((top[h], total))
        return tuple(out)

    start = tuple(
        (jnp.full((1, block), masked_fill, f32), jnp.zeros((1, block), f32)) for _ in heads
    )
    carry = key_loops(lo_ref, full_ref, block, step, start)
    half = block // 2
    carry = step(True, q0, half, 0, carry)
    later = tuple((top[:, half:], total[:, half:]) for top, total in carry)
    later = step(True, pl.multiple_of(q0 + half, half), half, half, later)
    for h in heads:
        top = jnp.concatenate([carry[h][0][:, :half], later[h][0]], axis=1)
        total = jnp.concatenate([carry[h][1][:, :half], later[h][1]], axis=1)
        o_ref[rows[h], :] = (acc_ref[rows[h], :] / total).astype(bf16)
        lse_ref[h : h + 1, :] = top + jnp.log(total) * log2_e
    attended = o_ref[...]
    for c in range(0, out_ref.shape[1], block):
        cols = pl.ds(c, block)
        part_ref[:, cols] = dot(attended, out_ref[:, cols], 0, 0).astype(bf16)


def attend_back_kernel(
    lo_ref,
    full_ref,
    low_ref,
    q_ref,
    hidden_ref,
    o_ref,
    lse_ref,
    k_ref,
    v_ref,
    kt_ref,
    out_ref,
    cos_ref,
    sin_ref,
    grad_ref,
    g_ref,
    dq_ref,
    dk_ref,
    dv_ref,
):
    heads = range(k_ref.shape[0])
    block = q_ref.shape[1]
    q0 = pl.multiple_of(pl.program_id(0) * block, block)
    width = q_ref.shape[0]
    half_dim = HEAD_DIM // 2
    rows = [pl.ds(h * HEAD_DIM, HEAD_DIM) for h in heads]

    def unrotated(ref, here, cols):
        cosine, sine = cos_ref[:, cols], sin_ref[:, cols]
        out = []
        for h in heads:
            at = h * HEAD_DIM
            a, b = ref[at : at + half_dim, here], ref[at + half_dim : at + HEAD_DIM, here]
            out += [a * cosine + b * sine, b * cosine - a * sine]
        return jnp.concatenate(out, axis=0).T

    @pl.when(pl.program_id(0) == 0)
    def _():
        dk_ref[...] = jnp.zeros_like(dk_ref)
        dv_ref[...] = jnp.zeros_like(dv_ref)

    g_ref[...] = dot(out_ref[...], hidden_ref[...], 1, 1).astype(bf16)
    dq_ref[...] = jnp.zeros_like(dq_ref)
    inner = [
        jnp.sum(g_ref[r, :].astype(f32) * o_ref[r, :].astype(f32), axis=0, keepdims=True)
        for r in rows
    ]

    def step(masked, k0, k_rows, q_from, carry):
        keys, mine = pl.ds(k0, k_rows), slice(q_from, block)
        if masked:
            visible = visible_block(low_ref[:, mine], q0 + q_from, k0, block - q_from, k_rows)
        for h in heads:
            r = rows[h]
            scores = dot(k_ref[h, keys, :], q_ref[r, mine], 1, 0)
            grad_probs = dot(v_ref[h, keys, :], g_ref[r, mine], 1, 0)
            if masked:
                scores = jnp.where(visible, scores, masked_fill)
            probs = jnp.exp2(scores - lse_ref[h : h + 1, mine])
            grad_scores = (probs * (grad_probs - inner[h][:, mine])).astype(bf16)
            dv = dot(g_ref[r, mine], probs.astype(bf16), 1, 1)
            dk = dot(q_ref[r, mine], grad_scores, 1, 1)
            dq = dot(kt_ref[r, keys], grad_scores, 1, 0)
            dv_ref[r, keys] += dv
            dk_ref[r, keys] += dk
            dq_ref[r, mine] += dq
        return carry

    key_loops(lo_ref, full_ref, block, step, 0)
    half = block // 2
    step(True, q0, half, 0, 0)
    step(True, pl.multiple_of(q0 + half, half), half, half, 0)
    here = pl.ds(q0, block)
    dq = unrotated(dq_ref, slice(None), here) * HEAD_DIM ** (-0.5)
    grad_ref[here, 0:width] = dq.astype(bf16)

    @pl.when(pl.program_id(0) == pl.num_programs(0) - 1)
    def _():
        for c in range(0, kt_ref.shape[1], block):
            cols = pl.ds(c, block)
            dk = unrotated(dk_ref, cols, cols) * (1 / log2_e)
            grad_ref[cols, width : 2 * width] = dk.astype(bf16)
            grad_ref[cols, 2 * width : 3 * width] = dv_ref[:, cols].T.astype(bf16)


def attention_specs(heads, length, q_block):
    width = heads * HEAD_DIM
    once = pl.Buffered(1)
    whole_t = pl.BlockSpec((width, length), lambda i, *_: (0, 0), pipeline_mode=once)
    whole_h = pl.BlockSpec((heads, length, HEAD_DIM), lambda i, *_: (0, 0, 0), pipeline_mode=once)
    tile = pl.BlockSpec((width, q_block), lambda i, *_: (0, i))
    low = pl.BlockSpec((1, q_block), lambda i, *_: (0, i))
    stat = pl.BlockSpec((heads, q_block), lambda i, *_: (0, i))
    return whole_t, whole_h, tile, low, stat


def attend(bounds, q_t, k_h, v_t, out_full):
    heads, length, _ = k_h.shape
    width, model = out_full.shape
    block = math.gcd(BLOCK, length)
    whole_t, whole_h, tile, low, stat = attention_specs(heads, length, block)
    pairs = length * WINDOW * heads
    return pl.pallas_call(
        attend_kernel,
        out_shape=(
            jax.ShapeDtypeStruct((width, length), bf16),
            jax.ShapeDtypeStruct((heads, length), f32),
            jax.ShapeDtypeStruct((length, model), bf16),
        ),
        grid_spec=pltpu.PrefetchScalarGridSpec(
            num_scalar_prefetch=2,
            grid=(length // block,),
            in_specs=[
                low,
                tile,
                whole_h,
                whole_t,
                pl.BlockSpec((width, model), lambda i, *_: (0, 0), pipeline_mode=pl.Buffered(1)),
            ],
            out_specs=[tile, stat, pl.BlockSpec((block, model), lambda i, *_: (i, 0))],
            scratch_shapes=[pltpu.VMEM((width, block), f32)],
        ),
        compiler_params=pltpu.CompilerParams(vmem_limit_bytes=VMEM_BYTES),
        cost_estimate=pl.CostEstimate(
            flops=pairs * 6 * 256, transcendentals=pairs, bytes_accessed=length * model * 2
        ),
        name="attend",
    )(*bounds, q_t, k_h, v_t, out_full)


def attend_back(bounds, q_t, grad_hidden, o_t, lse, k_h, v_h, k_t, out_full, cosine, sine):
    heads, length, _ = k_h.shape
    width, model = out_full.shape
    block = math.gcd(BLOCK, length)
    whole_t, whole_h, tile, low, stat = attention_specs(heads, length, block)
    once = pl.Buffered(1)
    table = pl.BlockSpec((HEAD_DIM // 2, length), lambda i, *_: (0, 0), pipeline_mode=once)
    pairs = length * WINDOW * heads
    return pl.pallas_call(
        attend_back_kernel,
        out_shape=jax.ShapeDtypeStruct((length, 3 * width), bf16),
        grid_spec=pltpu.PrefetchScalarGridSpec(
            num_scalar_prefetch=2,
            grid=(length // block,),
            in_specs=[
                low,
                tile,
                pl.BlockSpec((block, model), lambda i, *_: (i, 0)),
                tile,
                stat,
                whole_h,
                whole_h,
                whole_t,
                pl.BlockSpec((width, model), lambda i, *_: (0, 0), pipeline_mode=once),
                table,
                table,
            ],
            out_specs=pl.BlockSpec((length, 3 * width), lambda i, *_: (0, 0)),
            scratch_shapes=[
                pltpu.VMEM((width, block), bf16),
                pltpu.VMEM((width, block), f32),
                pltpu.VMEM((width, length), f32),
                pltpu.VMEM((width, length), f32),
            ],
        ),
        compiler_params=pltpu.CompilerParams(vmem_limit_bytes=VMEM_BYTES),
        cost_estimate=pl.CostEstimate(
            flops=pairs * 12 * 256, transcendentals=pairs, bytes_accessed=length * width * 24
        ),
        name="attend_back",
    )(*bounds, q_t, grad_hidden, o_t, lse, k_h, v_h, k_t, out_full, cosine, sine)


def feedforward_kernel(x_ref, ga_ref, gateup_ref, down_ref, act_ref, grad_ref, branch_ref):
    block, hidden = act_ref.shape
    step = math.gcd(hidden, 256)
    x = x_ref[...]
    for at in range(0, hidden, step):
        cols = slice(at, at + step)
        gate = dot(x, gateup_ref[at : at + step, :], 1, 1)
        raised = dot(x, gateup_ref[hidden + at : hidden + at + step, :], 1, 1)
        grad = ga_ref[:, cols]
        sigmoid = jax.nn.sigmoid(gate)
        silu = gate * sigmoid
        act_ref[:, cols] = (silu * raised).astype(bf16)
        grad_gate = grad * raised * sigmoid * (1.0 + gate * (1.0 - sigmoid))
        grad_ref[:, cols] = grad_gate.astype(bf16)
        grad_ref[:, hidden + at : hidden + at + step] = (grad * silu).astype(bf16)
    act = act_ref[...]
    for at in range(0, branch_ref.shape[1], block):
        cols = slice(at, at + block)
        branch_ref[:, cols] = dot(act, down_ref[:, cols], 1, 0).astype(bf16)


def feedforward(x, ga, gateup, down):
    length, model = x.shape
    hidden = down.shape[0]
    block = math.gcd(BLOCK, length)
    once = pl.Buffered(1)

    def rows_of(width):
        return pl.BlockSpec((block, width), lambda i: (i, 0))

    return pl.pallas_call(
        feedforward_kernel,
        grid=(length // block,),
        out_shape=tuple(
            jax.ShapeDtypeStruct((length, width), bf16) for width in (hidden, 2 * hidden, model)
        ),
        in_specs=[
            rows_of(model),
            rows_of(hidden),
            pl.BlockSpec((2 * hidden, model), lambda i: (0, 0), pipeline_mode=once),
            pl.BlockSpec((hidden, model), lambda i: (0, 0), pipeline_mode=once),
        ],
        out_specs=[rows_of(hidden), rows_of(2 * hidden), rows_of(model)],
        compiler_params=pltpu.CompilerParams(vmem_limit_bytes=VMEM_BYTES),
        cost_estimate=pl.CostEstimate(
            flops=6 * length * hidden * model,
            transcendentals=length * hidden,
            bytes_accessed=length * (4 * model + 10 * hidden),
        ),
        name="feedforward",
    )(x, ga, gateup, down)


def halves_kernel(order_ref, a_ref, b_ref, first_ref, second_ref):
    early = pl.program_id(0) < pl.num_programs(0) // 2

    @pl.when(early)
    def _():
        rows_kernel(a_ref, b_ref, first_ref)

    @pl.when(jnp.logical_not(early))
    def _():
        rows_kernel(a_ref, b_ref, second_ref)


def halves_product(order, a, b):
    length, inner = a.shape
    model = b.shape[1]
    count = order.shape[0]
    half, block = count // 2, length // count
    return pl.pallas_call(
        halves_kernel,
        out_shape=tuple(jax.ShapeDtypeStruct((length // 2, model), bf16) for _ in range(2)),
        grid_spec=pltpu.PrefetchScalarGridSpec(
            num_scalar_prefetch=1,
            grid=(count,),
            in_specs=[
                pl.BlockSpec((block, inner), lambda i, order: (order[i], 0)),
                pl.BlockSpec((inner, model), lambda i, _: (0, 0), pipeline_mode=pl.Buffered(1)),
            ],
            out_specs=[
                pl.BlockSpec((block, model), lambda i, _: (jnp.minimum(i, half - 1), 0)),
                pl.BlockSpec((block, model), lambda i, _: (jnp.maximum(i - half, 0), 0)),
            ],
        ),
        compiler_params=pltpu.CompilerParams(vmem_limit_bytes=VMEM_BYTES),
        cost_estimate=pl.CostEstimate(
            flops=2 * length * inner * model,
            transcendentals=0,
            bytes_accessed=2 * length * (inner + model),
        ),
        name="halves_product",
    )(order, a, b)


def rows_kernel(a_ref, b_ref, o_ref):
    a = a_ref[...]
    block = a_ref.shape[0]
    for at in range(0, o_ref.shape[1], block):
        cols = slice(at, at + block)
        o_ref[:, cols] = dot(a, b_ref[:, cols], 1, 0).astype(bf16)


def rows_product(a, b):
    length, inner = a.shape
    model = b.shape[1]
    block = math.gcd(BLOCK, length)
    return pl.pallas_call(
        rows_kernel,
        grid=(length // block,),
        out_shape=jax.ShapeDtypeStruct((length, model), bf16),
        in_specs=[
            pl.BlockSpec((block, inner), lambda i: (i, 0)),
            pl.BlockSpec((inner, model), lambda i: (0, 0), pipeline_mode=pl.Buffered(1)),
        ],
        out_specs=pl.BlockSpec((block, model), lambda i: (i, 0)),
        compiler_params=pltpu.CompilerParams(vmem_limit_bytes=VMEM_BYTES),
        cost_estimate=pl.CostEstimate(
            flops=2 * length * inner * model,
            transcendentals=0,
            bytes_accessed=2 * length * (inner + model),
        ),
        name="rows_product",
    )(a, b)


def attention_bounds(lengths, length):
    docs = lengths.shape[0]
    upto = jnp.arange(docs)[:, None] >= jnp.arange(docs)[None, :]
    ends = jnp.sum(jnp.where(upto, lengths[None, :], 0), axis=1)
    position = jnp.arange(length, dtype=jnp.int32)
    starts = jnp.max(jnp.where(ends[:, None] <= position[None, :], ends[:, None], 0), axis=0)
    low = jnp.maximum(starts, position - (WINDOW - 1)).astype(jnp.int32)
    block = math.gcd(BLOCK, length)
    by_block = low.reshape(length // block, block)
    first = by_block[:, 0] // block
    full = (by_block[:, -1] + block - 1) // block
    return first, full, low.reshape(1, length)


def rope_tables(length):
    half_dim = HEAD_DIM // 2
    counter = jnp.arange(half_dim, dtype=f32)
    frequency = jnp.exp(counter * (-2.0 * math.log(rope_base) / HEAD_DIM))
    angles = frequency[:, None] * jnp.arange(length, dtype=f32)[None, :]
    return jnp.cos(angles), jnp.sin(angles)


def norm_inverse(rows):
    return lax.rsqrt(jnp.mean(rows * rows, axis=-1, keepdims=True) + epsilon)


def norm_kernel(x_ref, branch_ref, gain_ref, hidden_ref, normed_ref):
    hidden = x_ref[...].astype(f32) + branch_ref[...].astype(f32)
    hidden_ref[...] = hidden
    normed_ref[...] = (hidden * norm_inverse(hidden) * gain_ref[...]).astype(bf16)


def norm_back_kernel(grad_ref, x_ref, base_ref, gain_ref, gain_grad_ref, *out_refs):
    @pl.when(pl.program_id(0) == 0)
    def _():
        gain_grad_ref[...] = jnp.zeros_like(gain_grad_ref)

    x, grad = x_ref[...].astype(f32), grad_ref[...].astype(f32)
    inverse = norm_inverse(x)
    normal = x * inverse
    grad_normal = grad * gain_ref[...]
    inner = jnp.mean(grad_normal * normal, axis=-1, keepdims=True)
    out = base_ref[...].astype(f32) + inverse * (grad_normal - normal * inner)
    for ref in out_refs:
        ref[...] = out.astype(ref.dtype)
    gain_grad_ref[...] += jnp.sum(grad * normal, axis=0, keepdims=True)


def cast_kernel(a_ref, o_ref):
    o_ref[...] = a_ref[...].astype(o_ref.dtype)


def by_rows(kernel, name, arrays, tables, outs, block):
    length, model = arrays[0].shape
    block = math.gcd(block, length)

    def spec(a):
        return pl.BlockSpec((min(block, a.shape[0]), model), lambda i: (i * (a.shape[0] > 1), 0))

    return pl.pallas_call(
        kernel,
        grid=(length // block,),
        out_shape=tuple(outs),
        in_specs=[spec(a) for a in (*arrays, *tables)],
        out_specs=tuple(spec(a) for a in outs),
        compiler_params=pltpu.CompilerParams(vmem_limit_bytes=VMEM_BYTES),
        cost_estimate=pl.CostEstimate(
            flops=8 * length * model, transcendentals=length, bytes_accessed=12 * length * model
        ),
        name=name,
    )(*arrays, *tables)


def add_and_norm(x, branch, gain):
    outs = [jax.ShapeDtypeStruct(x.shape, f32), jax.ShapeDtypeStruct(x.shape, bf16)]
    return by_rows(norm_kernel, "add_and_norm", (x, branch), (gain,), outs, 128)


def norm_backward(grad_normed, x, base, gain, dtypes):
    outs = [jax.ShapeDtypeStruct(gain.shape, f32)]
    outs += [jax.ShapeDtypeStruct(x.shape, dtype) for dtype in dtypes]
    return by_rows(norm_back_kernel, "norm_backward", (grad_normed, x, base), (gain,), outs, 128)


def widen(a):
    return by_rows(cast_kernel, "widen", (a,), (), [jax.ShapeDtypeStruct(a.shape, f32)], 512)[0]


def swap(a, axis):
    return lax.ppermute(a, axis, [(0, 1), (1, 0)])


def halve(terms, axis, dim):
    def part(index):
        return sum(lax.dynamic_index_in_dim(a, index, dim, False).astype(f32) for a in terms)

    index = lax.axis_index(axis)
    return part(index) + swap(part(1 - index).astype(bf16), axis).astype(f32)


def after(a, *others):
    return lax.optimization_barrier((a, *others))[0]


def shards(
    parts,
    block_input,
    doc_lengths,
    norm_gains,
    qkv_weight,
    out_weight,
    gateup_weight,
    down_weight,
    cotangent,
):
    n_chips, n_pair, n_core, seqs, n_extra = parts
    n_context = n_chips * n_pair * n_core
    context = ("chips", "pair", "core")
    plane = (*context, "extra")
    everyone = (*plane, "seq")
    cube = n_chips == n_pair == n_core == 2 and n_extra == 1
    model = block_input.shape[2]
    local_len = block_input.shape[1]
    length = local_len * n_context
    own_len = local_len // n_extra
    rows = model // n_context
    block_heads = qkv_weight.shape[2] // HEAD_DIM
    heads = seqs * block_heads // n_context
    split_heads = block_heads % n_context == 0
    block_hidden = gateup_weight.shape[2] // n_context
    hidden_width = seqs * block_hidden
    width = heads * HEAD_DIM
    seq = lax.axis_index("seq")
    first_row = lax.axis_index("extra") * own_len

    def exchange(a):
        return lax.all_to_all(a, context, split_axis=0, concat_axis=0, tiled=True)

    def send(a, *pairs):
        return lax.ppermute(a, "seq", pairs)

    def up(a, first=0):
        return send(a, *((i, i + 1) for i in range(first, seqs - 1)))

    def down(a, last=None):
        return send(a, *((i, i - 1) for i in range(1, seqs if last is None else last)))

    def spread_near(a):
        return [up(a), down(a)]

    def spread_far(near):
        across = jnp.where(seq == 1, near[0], near[1])
        return [up(near[0], 1), down(near[1], seqs - 1), send(across, (1, 3), (2, 0))]

    def spread_blocks(a, near, far):
        return [
            a,
            jnp.where(seq == 0, far[2], near[0]),
            jnp.where(seq >= 2, far[0], far[1]),
            jnp.where(seq == seqs - 1, far[2], near[1]),
        ]

    def spread_line(a, near, far):
        line = jnp.stack([far[2], far[0], near[0], a, near[1], far[1], far[2]])
        return lax.dynamic_slice_in_dim(line, seqs - 1 - seq, seqs, 0)

    def collect_far(blocks):
        across = jnp.where(seq == 0, blocks[1], blocks[3])
        return [
            send(blocks[2], *((i, i + 1) for i in range(seqs - 2))),
            send(blocks[2], *((i, i - 1) for i in range(2, seqs))),
            send(across, (0, 2), (3, 1)),
        ]

    def collect_near(blocks, far):
        above = blocks[3].astype(f32) + far[0].astype(f32) + jnp.where(seq == 2, far[2], 0)
        below = blocks[1].astype(f32) + far[1].astype(f32) + jnp.where(seq == 1, far[2], 0)
        return [blocks[0], up(above.astype(bf16)), down(below.astype(bf16))]

    def total(blocks):
        return sum((b.astype(f32) for b in blocks[1:]), blocks[0].astype(f32))

    def gather_plane(a):
        return lax.all_gather(a, plane, axis=0, tiled=True)

    def scatter_plane(a):
        return lax.psum_scatter(a.astype(bf16), plane, scatter_dimension=0, tiled=True)

    def scatter_middle(terms):
        half = own_len // 2
        one, two = [a[:, :, :half] for a in terms], [a[:, :, half:] for a in terms]
        return [halve(one, "pair", 1).astype(bf16), halve(two, "chips", 0).astype(bf16)]

    def scatter_end(halves):
        return jnp.concatenate(
            [halve(halves[:1], "chips", 0), halve(halves[1:], "pair", 0)], axis=0
        )

    def own(a):
        return lax.dynamic_slice(a, (seq, first_row, 0), (1, own_len, model))[0]

    def heads_out(a):
        if split_heads:
            return exchange(a.reshape(n_context, -1, rows))
        m = a.shape[1]
        a = lax.all_gather(a, "seq", axis=0, tiled=True)
        return exchange(a.reshape(n_context, heads * m, rows))

    def heads_whole(blocks, m):
        a = jnp.stack(blocks).reshape(len(blocks), n_context, heads // len(blocks), m, rows)
        return a.transpose(0, 2, 3, 1, 4).reshape(heads, m, model)

    def heads_split(a):
        a = a.astype(bf16).reshape(seqs, heads // seqs, a.shape[1], n_context, rows)
        return list(a.transpose(0, 3, 1, 2, 4).reshape(seqs, n_context, -1, rows))

    def heads_back(a):
        m = a.shape[1]
        a = a.astype(bf16).reshape(heads, m, n_context, rows).transpose(2, 0, 1, 3)
        a = exchange(a.reshape(n_context, -1, rows)).reshape(seqs * block_heads, m, rows)
        return lax.psum_scatter(a, "seq", scatter_dimension=0, tiled=True).astype(f32)

    rows_in = own(block_input)
    incoming = own(cotangent)
    wide = rows_in.astype(f32)
    normal_own = (wide * norm_inverse(wide)).astype(bf16)
    normal_all = gather_plane(normal_own)

    qkv_local, out_local, _ = lax.optimization_barrier((qkv_weight, out_weight, normal_own))
    heads_local = jnp.concatenate(
        [
            qkv_local.reshape(3, rows, block_heads, HEAD_DIM).transpose(2, 0, 3, 1),
            out_local.reshape(block_heads, 1, HEAD_DIM, rows),
        ],
        axis=1,
    )
    heads_block = heads_out(heads_local.reshape(block_heads, 4 * HEAD_DIM, rows))
    heads_block = heads_block.reshape(n_context, -1, 4, HEAD_DIM, rows)
    qkv_block = heads_block[:, :, :3].reshape(n_context, -1, rows)
    out_block = heads_block[:, :, 3].reshape(n_context, -1, rows)
    gains_local, gateup_local, down_local, qkv_block, out_block = lax.optimization_barrier(
        (norm_gains, gateup_weight, down_weight, qkv_block, out_block)
    )
    qkv_near = spread_near(qkv_block) if split_heads else []
    gateup_local = gateup_local.reshape(2, rows, n_context, block_hidden).transpose(2, 0, 3, 1)
    hidden_local = jnp.concatenate(
        [
            gateup_local.reshape(n_context, 2 * block_hidden, rows),
            down_local.reshape(n_context, block_hidden, rows),
        ],
        axis=1,
    )
    qkv_near, hidden_local, qkv_block, out_block = lax.optimization_barrier(
        (qkv_near, hidden_local, qkv_block, out_block)
    )
    if split_heads:
        qkv_blocks = spread_blocks(qkv_block, qkv_near, spread_far(qkv_near))
    else:
        qkv_blocks = [qkv_block]
    gains = lax.all_gather(gains_local, context, axis=1, tiled=True).astype(f32)
    out_near = spread_near(out_block) if split_heads else []
    qkv_blocks, out_near, gains = lax.optimization_barrier((qkv_blocks, out_near, gains))
    qkv_t = jnp.stack(qkv_blocks)
    qkv_t = qkv_t.reshape(len(qkv_blocks), n_context, -1, 3, HEAD_DIM, rows)
    qkv_t = qkv_t.transpose(3, 0, 2, 4, 1, 5).reshape(3 * width, model)
    qkv_gained = (qkv_t.astype(f32) * gains[0]).astype(bf16)
    cosine, sine = rope_tables(length)
    bounds = attention_bounds(lax.dynamic_slice_in_dim(doc_lengths, seq, 1, 0)[0], length)
    incoming_all = gather_plane(after(incoming, normal_all, *qkv_blocks))
    normal_all, qkv_t, qkv_gained, out_near, hidden_local, cosine, sine, bounds = (
        lax.optimization_barrier(
            (
                normal_all,
                qkv_t,
                qkv_gained,
                out_near,
                hidden_local,
                cosine,
                sine,
                bounds,
            )
        )
    )

    out_far = spread_far(out_near) if split_heads else []
    q_t, k_t, v_t, k_h, v_h = project(normal_all, qkv_gained, cosine, sine)
    q_t, out_far = lax.optimization_barrier((q_t, out_far))
    out_blocks = spread_blocks(out_block, out_near, out_far) if split_heads else [out_block]
    out_full = heads_whole(out_blocks, HEAD_DIM).reshape(width, model)
    hidden_block = exchange(hidden_local)
    o_t, lse, attention_part = attend(bounds, q_t, k_h, v_t, out_full)
    attention_part, incoming_all, hidden_block = lax.optimization_barrier(
        (attention_part, incoming_all, hidden_block)
    )
    hidden_near = spread_near(hidden_block)
    hidden_far = spread_far(hidden_near)
    attention_branch = scatter_plane(attention_part)
    attention_branch, hidden_far = lax.optimization_barrier((attention_branch, hidden_far))
    hidden, normed_own = add_and_norm(rows_in, attention_branch, gains[1:2])
    normed_two = gather_plane(normed_own)

    hidden_full = jnp.stack(spread_blocks(hidden_block, hidden_near, hidden_far))
    hidden_full = hidden_full.reshape(seqs, n_context, 3, block_hidden, rows)
    hidden_full = hidden_full.transpose(2, 0, 3, 1, 4).reshape(3 * hidden_width, model)
    gateup_t = hidden_full[: 2 * hidden_width]
    down_full = hidden_full[2 * hidden_width :]
    grad_activation = dot(incoming_all, down_full, 1, 1)
    normed_two, grad_activation = lax.optimization_barrier((normed_two, grad_activation))

    if cube:
        core = lax.axis_index("core")
        pairs = n_core * jnp.arange(n_chips * n_pair, dtype=jnp.int32)
        order = jnp.concatenate([pairs + 1 - core, pairs + core])
    else:
        order = jnp.arange(8, dtype=jnp.int32)
    activation, grad_gateup, feedforward_part = feedforward(
        normed_two, grad_activation, gateup_t, down_full
    )
    theirs, mine = halves_product(order, after(grad_gateup, feedforward_part), gateup_t)
    feedforward_branch = scatter_plane(feedforward_part)
    if cube:
        second_sums = (mine.astype(f32) + swap(theirs, "core").astype(f32)).astype(bf16)
        second_sums = [second_sums.reshape(n_chips, n_pair, own_len, model)]
    else:
        second_sums = [jnp.concatenate([theirs, mine], axis=0)]
    down_grad = dot(activation, incoming_all, 0, 0).astype(bf16)
    gateup_grad = dot(grad_gateup, normed_two, 0, 0).astype(bf16)
    hidden_grads = jnp.concatenate(
        [
            gateup_grad.reshape(2, seqs, block_hidden, n_context, rows),
            down_grad.reshape(1, seqs, block_hidden, n_context, rows),
        ],
        axis=0,
    )
    hidden_grads = list(hidden_grads.transpose(1, 3, 0, 2, 4).reshape(seqs, n_context, -1, rows))
    second_sums, hidden_grads = lax.optimization_barrier((second_sums, hidden_grads))
    hidden_grads_far = collect_far(hidden_grads)
    second_halves, hidden_grads_far = lax.optimization_barrier(
        (scatter_middle(second_sums) if cube else scatter_plane(*second_sums), hidden_grads_far)
    )
    grad_normed_two = scatter_end(second_halves) if cube else second_halves
    grad_normed_two, feedforward_branch = lax.optimization_barrier(
        (grad_normed_two, feedforward_branch)
    )

    result = (hidden + feedforward_branch.astype(f32)).astype(bf16)
    if n_extra > 1:
        result = lax.all_gather(result, "extra", axis=0, tiled=True)
    result_near = spread_near(result)
    gain_two, grad_hidden, grad_hidden_low = norm_backward(
        grad_normed_two, hidden, incoming, gains[1:2], (f32, bf16)
    )
    grad_hidden_all = gather_plane(grad_hidden_low)
    hidden_grads = collect_near(hidden_grads, hidden_grads_far)
    grad_hidden_all, hidden_grads, result_near = lax.optimization_barrier(
        (grad_hidden_all, hidden_grads, result_near)
    )

    result_far = spread_far(result_near)
    grad_projected = attend_back(
        bounds, q_t, grad_hidden_all, o_t, lse, k_h, v_h, k_t, out_full, cosine, sine
    )
    grad_projected, result_far = lax.optimization_barrier((grad_projected, result_far))

    owners = 2 * jnp.arange(n_context * n_extra, dtype=jnp.int32)
    first_half, second_half = halves_product(
        jnp.concatenate([owners, owners + 1]), grad_projected, qkv_t
    )
    first_half, second_half, grad_projected = lax.optimization_barrier(
        (first_half, second_half, grad_projected)
    )
    grad_one = scatter_plane(first_half)
    grad_two = scatter_plane(after(second_half, grad_one))
    qkv_grad = dot(grad_projected, normal_all, 0, 0) * gains[0]
    qkv_grad = qkv_grad.reshape(3, heads, HEAD_DIM, model).transpose(1, 0, 2, 3)
    qkv_grad = qkv_grad.reshape(heads, 3 * HEAD_DIM, model)
    out_grad = dot(o_t, grad_hidden_all, 1, 0).reshape(heads, HEAD_DIM, model)
    heads_grad = jnp.concatenate([qkv_grad, out_grad], axis=1)
    heads_grads = heads_split(heads_grad) if split_heads else []
    if split_heads:
        heads_grads = collect_near(heads_grads, collect_far(heads_grads))
    grad_two, heads_grads = lax.optimization_barrier((grad_two, heads_grads))

    half = own_len // 2
    gain_one = 0
    gathered = None
    input_grad = jnp.zeros((seqs * n_extra, own_len, model), f32)
    for at, grad_normed in ((0, grad_one), (half, grad_two)):
        part = slice(at, at + half)
        gain_part, grad_input = norm_backward(
            grad_normed, rows_in[part], grad_hidden[part], gains[0:1], (bf16,)
        )
        gain_one = gain_one + gain_part
        if at:
            grad_input = after(grad_input, gathered)
        gathered = lax.all_gather(grad_input, ("seq", "extra"), axis=0, tiled=False)
        input_grad = lax.dynamic_update_slice_in_dim(input_grad, gathered.astype(f32), at, 1)
    if split_heads:
        heads_grad = exchange(total(heads_grads).astype(bf16)).astype(f32)
        heads_grad = heads_grad.reshape(block_heads, 4 * HEAD_DIM, rows)
    else:
        heads_grad = heads_back(heads_grad)
    qkv_grad = heads_grad[:, : 3 * HEAD_DIM].reshape(block_heads, 3, HEAD_DIM, rows)
    out_grad = heads_grad[:, 3 * HEAD_DIM :]
    hidden_grad = exchange(total(hidden_grads).astype(bf16)).astype(f32)
    hidden_grad = hidden_grad.reshape(n_context, 3, block_hidden, rows)

    gains_grad = jnp.stack([gain_one, gain_two]).reshape(2, n_context, rows).transpose(1, 0, 2)
    gains_grad = jnp.sum(exchange(gains_grad), axis=0)
    if n_extra > 1:
        gains_grad = lax.psum(gains_grad, "extra")
    gains_near = spread_near(gains_grad)
    gains_grad = jnp.sum(spread_line(gains_grad, gains_near, spread_far(gains_near)), axis=0)
    results = spread_line(result, result_near, result_far)
    return (
        results,
        input_grad.reshape(seqs, local_len, model),
        gains_grad,
        qkv_grad.transpose(1, 3, 0, 2).reshape(qkv_weight.shape),
        out_grad.reshape(out_weight.shape),
        hidden_grad[:, :2].transpose(1, 3, 0, 2).reshape(gateup_weight.shape),
        hidden_grad[:, 2].reshape(down_weight.shape),
    )


def solution(mesh):
    n_context, n_tensor = mesh.shape["context"], mesh.shape["tensor"]
    n_core, n_pair = math.gcd(n_context, 2), math.gcd(n_context, 4) // math.gcd(n_context, 2)
    context, tensor = ("chips", "pair", "core"), ("seq", "extra")

    def program(block_input, *others):
        seqs = block_input.shape[0]
        n_extra = n_tensor // seqs
        assert n_extra * seqs == n_tensor and seqs == 4
        parts = (n_context // (n_pair * n_core), n_pair, n_core, seqs, n_extra)
        split = Mesh(mesh.devices.reshape(parts), (*context, *tensor))
        in_specs = (
            P(None, context, None),
            P(),
            P(None, context),
            P(None, context, tensor),
            P(tensor, context),
            P(None, context, tensor),
            P(tensor, context),
            P(None, context, None),
        )
        out_specs = (
            P(None, context, None),
            P(None, context, None),
            P(None, context),
            P(None, context, tensor),
            P(tensor, context),
            P(None, context, tensor),
            P(tensor, context),
        )
        return jax.shard_map(
            functools.partial(shards, parts),
            mesh=split,
            in_specs=in_specs,
            out_specs=out_specs,
            check_vma=False,
        )(block_input, *others)

    return program
```
